32 devices in a mesh: grp: 16 (over z, y, core), mdl: 2 (over x).
Axes of the slice: x: 2, y: 2, z: 4, core: 2. Of those that a mesh axis runs over, the one named last changes fastest.
Arguments:
- model: float32 [4096, 2, 128], P(None, 'mdl'), may hold values from -1 to 1.5
- source: float32 [64, 3, 8, 4096], P(('grp', 'mdl')), may hold values from -6 to 6
- observed: float32 [64, 3, 8, 4096], P(('grp', 'mdl')), may hold values from -6 to 6
- owner_ids: int32 [64, 8, 1], P(('grp', 'mdl')), may hold values from 0 to 1; in each aligned block of 16 rows (0 to 15, 16 to 31, ..., all dimensions but the last counted through in order) at most 16 rows name the same one
- offsets: int32 [64, 8], P(('grp', 'mdl')), may hold values from 0 to 4064
- lengths: int32 [64, 8], P(('grp', 'mdl')), may hold values from 1 to 32, 192 in all within a row
Outputs:
- gradient: float32 [4096, 2, 128], P('grp', 'mdl')
The draws below stay inside these ranges and needn't reach their ends.
Inputs may be any that keep to these rules, and one draw needn't show every extreme that they name: `owner_ids`: among the layers of the soundings of one device (aligned blocks of 16 layers), no owner is named by more than 16 layers; in some blocks one owner is named by exactly 16. A layer covers rows offsets to offsets + lengths - 1 of its owner's block. The first lengths rows of a layer lie in the earth, the others in the air; a sounding's 8 lengths sum to 192.
All inputs are finite; a program needn't handle non-finite values.
Results may differ from the reference program's by a relative error of at most 0.0003.
Values sent between devices are 32-bit elements; how exact they have to be, the bound alone decides.
No kernel may reach another device: no remote copies, remote signals or barrier semaphores. Data moves between devices by JAX's collectives and lax.ppermute only.
A program may use at most 64 MiB of HBM per device.

```python
import math
import jax
import jax.numpy as jnp
import numpy as np
from jax import lax

LY = 64
LZ = 8
S_DEV = 2
STEPS_FWD = 4
STEPS_ADJ = 4
BLK_ROWS = 4096
LAYER = 4096
TILE = 32
OWNERS = 2
SOUNDINGS = 64
CAP_T = 16


def place_ends(array, own_key, smallest, top_value):
    dims = array.shape
    spot = [jax.random.randint(jax.random.fold_in(own_key, axis), (), 0, dims[axis]) for axis in range(len(dims))]
    array = array.at[tuple(spot)].set(smallest)
    longest = dims.index(max(dims))
    spot[longest] = (spot[longest] + 1) % dims[longest]
    return array.at[tuple(spot)].set(top_value)


def shard_levels(stream_key, shape, cuts, least, high):
    level = 1.0
    for dim, shards_of in cuts:
        draws = jax.random.uniform(jax.random.fold_in(jax.random.fold_in(stream_key, 6), dim), (shards_of,), jnp.float32, least / len(cuts), high / len(cuts))
        level = level * jnp.repeat(jnp.exp(draws), shape[dim] // shards_of).reshape((-1,) + (1,) * (len(shape) - 1 - dim))
    return level


def profile(count, total, bound, skew):
    loads = [(1 << 20) // math.isqrt(standing ** skew) + 1 for standing in range(2, count + 1)]
    spare, holding = total - bound - (count - 1), [1] * (count - 1)
    while spare > 0:
        free = [i for i in range(count - 1) if holding[i] < bound]
        pool, budget = sum([loads[i] for i in free]), spare
        for i in free:
            addition = min(bound - holding[i], max(1, budget * loads[i] // pool), spare)
            holding[i] = holding[i] + addition
            spare = spare - addition
    return np.array([bound] + holding)


def ragged(own_key, number_of, total, reach, skew):
    if number_of == 2:
        one = jax.random.randint(own_key, (), max(1, total - reach), min(reach, total - 1) + 1)
        return jnp.stack([one, total - one])
    tallies = jnp.asarray(profile(number_of, total, reach, skew), jnp.int32)
    couples = (number_of - 1) // 2
    donor, receiver = tallies[1:1 + 2 * couples:2], tallies[2:2 + 2 * couples:2]
    margin = jnp.minimum(donor - 1, reach - receiver)
    moved = jax.random.randint(jax.random.fold_in(own_key, 1), (couples,), 0, 1 << 20) % (margin + 1)
    tallies = tallies.at[1:1 + 2 * couples:2].set(donor - moved).at[2:2 + 2 * couples:2].set(receiver + moved)
    return tallies[jax.random.permutation(jax.random.fold_in(own_key, 2), number_of)]


def shared_out(stream_key, own, number, rows, count, top, limit, skew):
    order = jax.random.permutation(stream_key, count)
    crowded, usual = shares(count, rows * top, limit, skew, True), shares(count, rows * top, limit, skew, False)
    places = jnp.arange(count)

    def named(sizes, offset_by):
        used = int((sizes > 0).sum())
        fixed = max(1, used // 4)
        shifted = fixed + (places - fixed + offset_by * (used - fixed)) % max(1, count - fixed)
        return jnp.zeros((count,), jnp.int32).at[order[jnp.where(places < fixed, places, shifted)]].set(jnp.asarray(sizes, jnp.int32))

    sizes = jnp.where(number % 4 == 0, named(crowded, number // 4), named(usual, number - number // 4 - 1))
    mixed = jax.random.permutation(jax.random.fold_in(own, 3), count)
    source_of, sink = mixed[0:count // 2 * 2:2], mixed[1:count // 2 * 2:2]
    slack = jnp.minimum(sizes[source_of] - 1, limit - sizes[sink]) // 2
    slack = jnp.where((source_of == order[0]) | (sink == order[0]) | (sizes[sink] == 0), 0, jnp.maximum(slack, 0))
    shifted = jax.random.randint(jax.random.fold_in(own, 4), (count // 2,), 0, 1 << 20) % (slack + 1)
    sizes = sizes.at[source_of].add(-shifted).at[sink].add(shifted)
    labels = jnp.searchsorted(jnp.cumsum(sizes), jnp.arange(rows * top), side="right").astype(jnp.int32)
    listing = labels.reshape(top, rows).T
    listing = listing[jax.random.permutation(jax.random.fold_in(own, 1), rows)]
    offset_by = jax.random.randint(jax.random.fold_in(own, 2), (rows, 1), 0, top)
    return jnp.take_along_axis(listing, (jnp.arange(top)[None, :] + offset_by) % top, axis=1)


def shares(amount, total, limit, lean, full):
    portions = [(1 << 20) // math.isqrt(rank ** lean) + 1 for rank in range(1, amount + 1)]
    largest = limit if full else min(limit, max(-(-total // amount), total * portions[0] // sum(portions)))
    least = 1 if total - largest >= amount - 1 else 0
    holding, rest = [largest] + [least] * (amount - 1), total - largest - least * (amount - 1)
    while rest > 0:
        candidates = [i for i in range(1, amount) if holding[i] < largest] or [i for i in range(1, amount) if holding[i] < limit]
        pool, budget = sum([portions[i] for i in candidates]), rest
        for i in candidates:
            extra = min(limit - holding[i], max(1, budget * portions[i] // pool), rest)
            holding[i] = holding[i] + extra
            rest = rest - extra
    return np.array(holding)


def gaussian(rng, shape, scale, limit, cuts=(), held_as=jnp.bfloat16):
    drawn = scale * jax.random.normal(rng, shape, jnp.float32)
    if cuts:
        drawn = drawn * shard_levels(rng, shape, cuts, -0.22, 0.18)
    return jnp.clip(drawn, -limit, limit).astype(held_as)


def setup_inputs(seed: int = 0) -> dict:
    key_of = jax.random.split(jax.random.key(seed), 7)
    model = jnp.clip(-1.0 + 2.5 * jax.random.uniform(key_of[0], (BLK_ROWS, OWNERS, 128), jnp.float32) ** shard_levels(key_of[0], (BLK_ROWS, OWNERS, 128), ((1, 2),), -0.2, 0.2), -1.0, 1.5)
    source = gaussian(key_of[1], (SOUNDINGS, 3, LZ, LAYER), 1.0, 6.0, ((0, 32),), jnp.float32)
    observed = gaussian(key_of[2], (SOUNDINGS, 3, LZ, LAYER), 1.0, 6.0, ((0, 32),), jnp.float32)
    owner_ids_keys = jax.random.split(jax.random.fold_in(key_of[3], 1), SOUNDINGS * LZ // (S_DEV * LZ))
    owner_ids_turns = jax.random.permutation(jax.random.fold_in(key_of[3], 3), SOUNDINGS * LZ // (S_DEV * LZ))
    owner_ids = jax.vmap(lambda own, number: shared_out(jax.random.fold_in(key_of[3], 2), own, number, S_DEV * LZ, OWNERS, 1, CAP_T, 2))(owner_ids_keys, owner_ids_turns).reshape((SOUNDINGS, LZ, 1))
    offsets = place_ends(jax.random.randint(key_of[4], (SOUNDINGS, LZ), 0, BLK_ROWS - TILE + 1), jax.random.fold_in(key_of[4], 1), 0, BLK_ROWS - TILE).astype(jnp.int32)
    lengths = jax.vmap(lambda own: ragged(own, LZ, LZ * TILE * 3 // 4, TILE, 2))(jax.random.split(key_of[5], SOUNDINGS)).reshape((SOUNDINGS, LZ)).astype(jnp.int32)
    return {"model": model, "source": source, "observed": observed, "owner_ids": owner_ids, "offsets": offsets, "lengths": lengths}


AIR = 0.05
OMEGA = 0.5
BETA = 0.5


def shift_next(field, count):
    filler = jnp.zeros(field.shape[:-1] + (count,), field.dtype)
    return jnp.concatenate([field[..., count:], filler], axis=-1)


def shift_prev(field, count):
    filler = jnp.zeros(field.shape[:-1] + (count,), field.dtype)
    return jnp.concatenate([filler, field[..., :-count]], axis=-1)


def layer_masks(width):
    column = jnp.arange(LAYER, dtype=jnp.int32) % width
    return (column != width - 1).astype(jnp.float32), (column != 0).astype(jnp.float32)


def forward_diff(field, which, masks):
    if which == 0:
        return shift_next(field, LY) - field
    if which == 1:
        return shift_next(field, 1) * masks[0] - field
    deeper = jnp.concatenate([field[:, 1:], jnp.zeros_like(field[:, :1])], axis=1)
    return deeper - field


def adjoint_diff(field, which, masks):
    if which == 0:
        return shift_prev(field, LY) - field
    if which == 1:
        return shift_prev(field, 1) * masks[1] - field
    upper = jnp.concatenate([jnp.zeros_like(field[:, :1]), field[:, :-1]], axis=1)
    return upper - field


def apply_operator(field, conduct, masks):
    east, north, vertical = field[:, 0], field[:, 1], field[:, 2]
    curl_x = forward_diff(vertical, 1, masks) - forward_diff(north, 2, masks)
    curl_y = forward_diff(east, 2, masks) - forward_diff(vertical, 0, masks)
    curl_z = forward_diff(north, 0, masks) - forward_diff(east, 1, masks)
    back_x = adjoint_diff(curl_y, 2, masks) - adjoint_diff(curl_z, 1, masks)
    back_y = adjoint_diff(curl_z, 0, masks) - adjoint_diff(curl_x, 2, masks)
    back_z = adjoint_diff(curl_x, 1, masks) - adjoint_diff(curl_y, 0, masks)
    return jnp.stack([back_x, back_y, back_z], axis=1) + conduct[:, None] * field


def relax(right_side, conduct, count, masks):
    state = jnp.zeros_like(right_side)
    scale = OMEGA / (4.0 + conduct[:, None])
    for sweep in range(count):
        state = state + scale * (right_side - apply_operator(state, conduct, masks))
    return state


def sounding_partial(source, observed, conduct, earth, masks):
    efield = relax(source, conduct, STEPS_FWD, masks)
    adjoint_field = relax(efield - observed, conduct, STEPS_ADJ, masks)
    return -conduct * jnp.sum(efield * adjoint_field, axis=1) * earth


def smoothing(values):
    left = jnp.concatenate([values[..., :1], values[..., :-1]], axis=-1)
    right = jnp.concatenate([values[..., 1:], values[..., -1:]], axis=-1)
    return BETA * (2.0 * values - left - right)


def reference(model, source, observed, owner_ids, offsets, lengths):
    masks = layer_masks(LY)
    flat_model = model.reshape(BLK_ROWS * OWNERS, 128)
    batches = SOUNDINGS // S_DEV
    within = jnp.arange(TILE, dtype=jnp.int32)

    def one_batch(total, pieces):
        batch_source, batch_observed, batch_owner, batch_start, batch_length = pieces
        rows = (batch_start[..., None] + within) * OWNERS + batch_owner[..., None]
        rows = rows.astype(jnp.int32)
        earth = (within < batch_length[..., None]).astype(jnp.float32)
        earth = jnp.broadcast_to(earth[..., None], (S_DEV, LZ, TILE, 128)).reshape(S_DEV, LZ, LAYER)
        values = jnp.exp(flat_model[rows]).reshape(S_DEV, LZ, LAYER)
        conduct = jnp.where(earth > 0.5, values, AIR)
        partial_value = sounding_partial(batch_source, batch_observed, conduct, earth, masks)
        total = total.at[rows.reshape(-1)].add(partial_value.reshape(-1, 128))
        return total, None

    initial = jnp.zeros((BLK_ROWS * OWNERS, 128), jnp.float32)
    pieces = (
        source.reshape(batches, S_DEV, 3, LZ, LAYER),
        observed.reshape(batches, S_DEV, 3, LZ, LAYER),
        owner_ids.reshape(batches, S_DEV, LZ),
        offsets.reshape(batches, S_DEV, LZ),
        lengths.reshape(batches, S_DEV, LZ),
    )
    total, unused = lax.scan(one_batch, initial, pieces)
    return total.reshape(BLK_ROWS, OWNERS, 128) + smoothing(model)
```

```python
import jax
import jax.numpy as jnp
from jax import lax
from jax.sharding import PartitionSpec as P

LY = 64
LZ = 8
STEPS_FWD = 4
STEPS_ADJ = 4
LAYER = 4096
TILE = 32


AIR = 0.05
OMEGA = 0.5
BETA = 0.5


def shift_next(field, count):
    filler = jnp.zeros(field.shape[:-1] + (count,), field.dtype)
    return jnp.concatenate([field[..., count:], filler], axis=-1)


def shift_prev(field, count):
    filler = jnp.zeros(field.shape[:-1] + (count,), field.dtype)
    return jnp.concatenate([filler, field[..., :-count]], axis=-1)


def layer_masks(width):
    column = jnp.arange(LAYER, dtype=jnp.int32) % width
    return ((column != width - 1).astype(jnp.float32), (column != 0).astype(jnp.float32))


def forward_diff(field, which, masks):
    if which == 0:
        return shift_next(field, LY) - field
    if which == 1:
        return shift_next(field, 1) * masks[0] - field
    deeper = jnp.concatenate([field[:, 1:], jnp.zeros_like(field[:, :1])], axis=1)
    return deeper - field


def adjoint_diff(field, which, masks):
    if which == 0:
        return shift_prev(field, LY) - field
    if which == 1:
        return shift_prev(field, 1) * masks[1] - field
    upper = jnp.concatenate([jnp.zeros_like(field[:, :1]), field[:, :-1]], axis=1)
    return upper - field


def apply_operator(field, conduct, masks):
    east, north, vertical = (field[:, 0], field[:, 1], field[:, 2])
    curl_x = forward_diff(vertical, 1, masks) - forward_diff(north, 2, masks)
    curl_y = forward_diff(east, 2, masks) - forward_diff(vertical, 0, masks)
    curl_z = forward_diff(north, 0, masks) - forward_diff(east, 1, masks)
    back_x = adjoint_diff(curl_y, 2, masks) - adjoint_diff(curl_z, 1, masks)
    back_y = adjoint_diff(curl_z, 0, masks) - adjoint_diff(curl_x, 2, masks)
    back_z = adjoint_diff(curl_x, 1, masks) - adjoint_diff(curl_y, 0, masks)
    return jnp.stack([back_x, back_y, back_z], axis=1) + conduct[:, None] * field


def relax(right_side, conduct, count, masks):
    state = jnp.zeros_like(right_side)
    scale = OMEGA / (4.0 + conduct[:, None])
    for sweep in range(count):
        state = state + scale * (right_side - apply_operator(state, conduct, masks))
    return state


def sounding_partial(source, observed, conduct, earth, masks):
    efield = relax(source, conduct, STEPS_FWD, masks)
    adjoint_field = relax(efield - observed, conduct, STEPS_ADJ, masks)
    return -conduct * jnp.sum(efield * adjoint_field, axis=1) * earth


def smoothing(values):
    left = jnp.concatenate([values[..., :1], values[..., :-1]], axis=-1)
    right = jnp.concatenate([values[..., 1:], values[..., -1:]], axis=-1)
    return BETA * (2.0 * values - left - right)


def place_slots(owner_flat, owners_count, capacity):
    chosen = (owner_flat[:, None] == jnp.arange(owners_count, dtype=jnp.int32)[None, :]).astype(
        jnp.int32
    )
    before = jnp.cumsum(chosen, axis=0) - chosen
    return owner_flat * capacity + jnp.sum(before * chosen, axis=1)


def settle(block, source, observed, owner_ids, offsets, lengths, owners_count, capacity, masks):
    count = source.shape[0]
    tiles = count * LZ
    within = jnp.arange(TILE, dtype=jnp.int32)
    places = place_slots(owner_ids.reshape(tiles), owners_count, capacity)
    request = (
        jnp.zeros((owners_count * capacity,), jnp.int32).at[places].set(offsets.reshape(tiles))
    )
    request = request.reshape(owners_count, capacity)
    values = jnp.exp(
        block[
            lax.all_to_all(request, "mdl", split_axis=0, concat_axis=0, tiled=True)[..., None]
            + within
        ]
    )
    answer = lax.all_to_all(values, "mdl", split_axis=0, concat_axis=0, tiled=True)
    fetched = answer.reshape(owners_count * capacity, TILE, 128)[places].reshape(count, LZ, LAYER)
    earth = (within[None, :] < lengths.reshape(tiles)[:, None]).astype(jnp.float32)
    earth = jnp.broadcast_to(earth[..., None], (tiles, TILE, 128)).reshape(count, LZ, LAYER)
    conduct = jnp.where(earth > 0.5, fetched, AIR)
    partial_value = sounding_partial(source, observed, conduct, earth, masks)
    outgoing = jnp.zeros((owners_count * capacity, TILE, 128), jnp.float32)
    outgoing = outgoing.at[places].set(partial_value.reshape(tiles, TILE, 128))
    outgoing = outgoing.reshape(owners_count, capacity, TILE, 128)
    arrived, arrived_starts = (
        lax.all_to_all(outgoing, "mdl", split_axis=0, concat_axis=0, tiled=True),
        lax.all_to_all(request, "mdl", split_axis=0, concat_axis=0, tiled=True),
    )
    target_rows = (arrived_starts[..., None] + within).reshape(-1)
    return (
        jnp.zeros((block.shape[0], 128), jnp.float32).at[target_rows].add(arrived.reshape(-1, 128))
    )


def halve(blocks, bit):
    held, data = blocks
    where = held.index(bit)
    mine = (lax.axis_index("grp") >> bit) & 1
    keep = lax.dynamic_index_in_dim(data, mine, where, keepdims=False)
    give = lax.dynamic_index_in_dim(data, 1 - mine, where, keepdims=False)
    ring = [(i, i ^ (1 << bit)) for i in range(lax.axis_size("grp"))]
    got = lax.ppermute(give, "grp", ring)
    return held[:where] + held[where + 1 :], keep + got


def scatter_sums(total):
    groups = lax.axis_size("grp")
    bits = groups.bit_length() - 1
    share = total.shape[0] // groups
    held = tuple(range(bits - 1, -1, -1))
    blocks = halve((held, total.reshape((2,) * bits + (share, 128))), 0)
    rest = tuple(range(1, bits))
    swapped = rest[1:2] + rest[0:1] + rest[2:]
    half = share // 2
    low = (blocks[0], blocks[1][..., :half, :])
    high = (blocks[0], blocks[1][..., half:, :])
    for first, second in zip(rest, swapped):
        low, high = halve(low, first), halve(high, second)
    return jnp.concatenate([low[1], high[1]], axis=0)


def per_device(model, source, observed, owner_ids, offsets, lengths):
    block = model[:, 0, :]
    masks = layer_masks(LY)
    owners_count = lax.axis_size("mdl")
    capacity = max(4, 2 * source.shape[0] * LZ // owners_count)
    block_partial = settle(
        block, source, observed, owner_ids, offsets, lengths, owners_count, capacity, masks
    )
    share = block.shape[0] // lax.axis_size("grp")
    mine = scatter_sums(block_partial)
    local_model = lax.dynamic_slice_in_dim(block, lax.axis_index("grp") * share, share, 0)
    return (mine + smoothing(local_model))[:, None, :]


def solution(mesh):
    placed = (
        P(None, "mdl", None),
        P(("grp", "mdl"), None, None, None),
        P(("grp", "mdl"), None, None, None),
        P(("grp", "mdl"), None, None),
        P(("grp", "mdl"), None),
        P(("grp", "mdl"), None),
    )
    return jax.shard_map(
        per_device, mesh=mesh, in_specs=placed, out_specs=P("grp", "mdl", None), check_vma=False
    )
```

```python
import functools

import jax
import jax.numpy as jnp
from jax import lax
from jax.experimental import pallas as pl
from jax.experimental.pallas import tpu as pltpu
from jax.sharding import PartitionSpec as P

LY = 64
LZ = 8
STEPS_FWD = 4
STEPS_ADJ = 4
TILE = 32
LANES = 128
SUB = 8
PARTS = TILE // SUB

AIR = 0.05
OMEGA = 0.5
BETA = 0.5

VMEM = pl.BlockSpec(memory_space=pltpu.VMEM)
SMEM = pl.BlockSpec(memory_space=pltpu.SMEM)


def place_slots(owner_flat, owners_count, capacity):
    chosen = (owner_flat[:, None] == jnp.arange(owners_count, dtype=jnp.int32)[None, :]).astype(
        jnp.int32
    )
    before = jnp.cumsum(chosen, axis=0) - chosen
    return owner_flat * capacity + jnp.sum(before * chosen, axis=1)


def swap_over(axis, mask):
    ring = [(i, i ^ mask) for i in range(lax.axis_size(axis))]
    return lambda value: lax.ppermute(value, axis, ring)


def gather_body(index_ref, block_ref, out_ref):
    for tile in range(out_ref.shape[0]):
        start = index_ref[0, tile]
        out_ref[tile] = block_ref[pl.ds(start, TILE), :]


def gather_rows(index, block):
    tiles = index.shape[1]
    return pl.pallas_call(
        gather_body,
        out_shape=jax.ShapeDtypeStruct((tiles, TILE, LANES), jnp.float32),
        in_specs=[SMEM, VMEM],
        out_specs=VMEM,
        cost_estimate=pl.CostEstimate(
            flops=0, bytes_accessed=2 * tiles * TILE * LANES * 4, transcendentals=0
        ),
        name="gather_rows",
    )(index, block)


def stencil_body(
    index_ref, lengths_ref, table_ref, answer_ref, source_ref, observed_ref, out_ref,
    field, adjoint, right, scale, decay,
):
    me = lax.axis_index("mdl")
    lane = lax.broadcasted_iota(jnp.int32, (PARTS, SUB, LANES), 2)
    sub = lax.broadcasted_iota(jnp.int32, (1, SUB, LANES), 1)
    row = (
        PARTS * lax.broadcasted_iota(jnp.int32, (PARTS, SUB, LANES), 1)
        + lax.broadcasted_iota(jnp.int32, (PARTS, SUB, LANES), 0)
    )
    low = lane < LY
    not_last = lane % LY != LY - 1
    not_first = lane % LY != 0

    def turn(value, count):
        return pltpu.roll(value, count % LANES, 2)

    def y_next(value):
        return jnp.where(not_last, turn(value, -1), 0.0)

    def y_prev(value):
        return jnp.where(not_first, turn(value, 1), 0.0)

    def x_next(value):
        wrapped = jnp.where(sub != SUB - 1, pltpu.roll(value[:1], SUB - 1, 1), 0.0)
        below = jnp.concatenate([value[1:], wrapped], axis=0)
        return turn(jnp.where(low, below, value), LY)

    def x_prev(value):
        wrapped = jnp.where(sub != 0, pltpu.roll(value[PARTS - 1 :], 1, 1), 0.0)
        above = jnp.concatenate([wrapped, value[: PARTS - 1]], axis=0)
        return turn(jnp.where(low, value, above), LY)

    def rows_of(ref, base, step):
        return jnp.stack(
            [ref[pl.ds(base + step * j, SUB, stride=step * PARTS), :] for j in range(PARTS)]
        )

    def sweep(state):
        east, north, vert = state[0, 0], state[1, 0], state[2, 0]
        zero = jnp.zeros_like(east)
        up_x, up_y = zero, zero
        for z in range(LZ):
            if z + 1 < LZ:
                east_d, north_d, vert_d = state[0, z + 1], state[1, z + 1], state[2, z + 1]
            else:
                east_d, north_d, vert_d = zero, zero, zero
            curl_x = (y_next(vert) - vert) - (north_d - north)
            curl_y = (east_d - east) - (x_next(vert) - vert)
            curl_z = (x_next(north) - north) - (y_next(east) - east)
            back_x = (up_y - curl_y) - (y_prev(curl_z) - curl_z)
            back_y = (x_prev(curl_z) - curl_z) - (up_x - curl_x)
            back_z = (y_prev(curl_x) - curl_x) - (x_prev(curl_y) - curl_y)
            s, d = scale[z], decay[z]
            state[0, z] = d * east + (right[0, z] - s * back_x)
            state[1, z] = d * north + (right[1, z] - s * back_y)
            state[2, z] = d * vert + (right[2, z] - s * back_z)
            up_x, up_y = curl_x, curl_y
            east, north, vert = east_d, north_d, vert_d

    for sounding in range(source_ref.shape[0] // (3 * LZ * TILE)):
        first = sounding * LZ

        def conduct_of(z):
            tile = first + z
            length = lengths_ref[tile]
            raw = rows_of(table_ref, index_ref[0, tile], 1)
            sent = rows_of(answer_ref, tile * TILE, 1)
            mine = jnp.full((PARTS, SUB, LANES), index_ref[1, tile] == me)
            value = jnp.exp(jnp.where(mine, raw, sent))
            earth = row < length
            return jnp.where(earth, value, AIR), earth

        def cells(ref, part, z):
            return rows_of(ref, (sounding * 3 + part) * LZ * TILE + z, LZ)

        for z in range(LZ):
            conduct, _ = conduct_of(z)
            s = OMEGA / (4.0 + conduct)
            scale[z] = s
            decay[z] = 1.0 - s * conduct
            for part in range(3):
                value = s * cells(source_ref, part, z)
                right[part, z] = value
                field[part, z] = value

        @pl.loop(0, STEPS_FWD - 1)
        def _(step):
            sweep(field)

        for z in range(LZ):
            for part in range(3):
                value = scale[z] * (field[part, z] - cells(observed_ref, part, z))
                right[part, z] = value
                adjoint[part, z] = value

        @pl.loop(0, STEPS_ADJ - 1)
        def _(step):
            sweep(adjoint)

        for z in range(LZ):
            conduct, earth = conduct_of(z)
            total = field[0, z] * adjoint[0, z]
            total += field[1, z] * adjoint[1, z]
            total += field[2, z] * adjoint[2, z]
            partial = jnp.where(earth, -conduct * total, 0.0)
            for j in range(PARTS):
                out_ref[pl.ds((first + z) * TILE + j, SUB, stride=PARTS), :] = partial[j]


def by_rows(values):
    count = values.shape[0]
    parts = values.reshape(count, 3, LZ, TILE, LANES)
    return parts.transpose(0, 1, 3, 2, 4).reshape(count * 3 * TILE * LZ, LANES)


def soundings_partial(index, lengths, table, answer, source, observed):
    tiles = index.shape[1]
    count = tiles // LZ
    planes = pltpu.VMEM((3, LZ, PARTS, SUB, LANES), jnp.float32)
    single = pltpu.VMEM((LZ, PARTS, SUB, LANES), jnp.float32)
    out = pl.pallas_call(
        stencil_body,
        out_shape=jax.ShapeDtypeStruct((tiles * TILE, LANES), jnp.float32),
        in_specs=[SMEM, SMEM, VMEM, VMEM, VMEM, VMEM],
        out_specs=VMEM,
        scratch_shapes=[planes, planes, planes, single, single],
        cost_estimate=pl.CostEstimate(
            flops=count * 8 * 60 * LZ * TILE * LANES,
            bytes_accessed=4 * (2 * source.size + 3 * tiles * TILE * LANES),
            transcendentals=2 * tiles * TILE * LANES,
        ),
        name="soundings_partial",
    )(
        index, lengths, table, answer.reshape(tiles * TILE, LANES), by_rows(source),
        by_rows(observed),
    )
    return out.reshape(tiles, TILE, LANES)


def arranged(order):
    if not order:
        return [0]
    rest = arranged(order[1:])
    return [slot | (1 << order[0]) for slot in rest] + rest


def accumulate_body(orders, groups, terms_count, *refs):
    indexes, terms = refs[:terms_count], refs[terms_count : 2 * terms_count]
    model_ref = refs[2 * terms_count]
    outs, total = refs[2 * terms_count + 1 : -1], refs[-1]
    owner, me = lax.axis_index("mdl"), lax.axis_index("grp")
    share = model_ref.shape[0] // groups
    span = share + 2 * TILE
    slots = groups // 2
    half = share // 2
    total[...] = jnp.zeros_like(total)
    local = model_ref[pl.ds(pl.multiple_of(me * share, share), share), :]
    lane = lax.broadcasted_iota(jnp.int32, local.shape, 1)
    left = jnp.where(lane == 0, local, pltpu.roll(local, 1, 1))
    right = jnp.where(lane == LANES - 1, local, pltpu.roll(local, LANES - 1, 1))
    total[TILE : TILE + share, :] = BETA * (2.0 * local - left - right)

    for index_ref, terms_ref in zip(indexes, terms):

        @pl.loop(0, terms_ref.shape[0])
        def _(tile):
            start = index_ref[0, tile]
            first = lax.div(start, share)
            target = first + ((first ^ me) & 1)
            where = start - target * share

            @pl.when((index_ref[1, tile] == owner) & (where > -TILE))
            def _():
                base = ((target >> 1) ^ (me >> 1)) * span + TILE + where
                total[pl.ds(base, TILE), :] += terms_ref[tile]

    for which, order in enumerate(orders):
        for place, slot in enumerate(arranged(order)):
            out = outs[2 * which + (place * 2 >= slots)]
            begin = slot * span + TILE + which * half
            out[place % (slots // 2)] = total[begin : begin + half, :]


def accumulate(indexes, terms, block, orders):
    groups = lax.axis_size("grp")
    share, slots = block.shape[0] // groups, groups // 2
    out = jax.ShapeDtypeStruct((slots // 2, share // 2, LANES), jnp.float32)
    count = len(terms)
    return pl.pallas_call(
        functools.partial(accumulate_body, orders, groups, count),
        out_shape=(out,) * 4,
        in_specs=[SMEM] * count + [VMEM] * (count + 1),
        out_specs=(VMEM,) * 4,
        scratch_shapes=[pltpu.VMEM((slots * (share + 2 * TILE), LANES), jnp.float32)],
        cost_estimate=pl.CostEstimate(
            flops=sum(t.size for t in terms),
            bytes_accessed=4 * sum(t.size for t in terms),
            transcendentals=0,
        ),
        name="accumulate",
    )(*indexes, *terms, block)


def per_device(model, source, observed, owner_ids, offsets, lengths):
    rows, owners, groups = model.shape[0], lax.axis_size("mdl"), lax.axis_size("grp")
    block = model.reshape(rows, LANES)
    tiles = source.shape[0] * LZ
    across, beside = swap_over("mdl", 1), swap_over("grp", 1)
    flat_owner, flat_start = owner_ids.reshape(tiles), offsets.reshape(tiles)
    flat_length = lengths.reshape(tiles)
    index = jnp.stack([flat_start, flat_owner])
    if owners == 2:
        asked = across(index)
        answer = across(gather_rows(asked, block))
        terms = soundings_partial(index, flat_length, block, answer, source, observed)
        others = across(terms)
        index_pair = beside(jnp.stack([index, asked]))
        indexes = [index, asked, index_pair[0], index_pair[1]]
        terms_list = [terms, others, beside(terms), beside(others)]
    else:
        capacity = max(4, 2 * tiles // owners)
        places = place_slots(flat_owner, owners, capacity)
        swap = functools.partial(
            lax.all_to_all, axis_name="mdl", split_axis=0, concat_axis=0, tiled=True
        )
        request = jnp.zeros((owners * capacity,), jnp.int32).at[places].set(flat_start)
        asked = swap(request.reshape(owners, capacity)).reshape(1, owners * capacity)
        mine = jnp.full_like(asked, lax.axis_index("mdl"))
        asked = jnp.concatenate([asked, mine])
        given = gather_rows(asked, block).reshape(owners, capacity, TILE, LANES)
        fetched = swap(given).reshape(owners * capacity * TILE, LANES)
        local = jnp.stack([places * TILE, jnp.full_like(places, lax.axis_index("mdl"))])
        dummy = jnp.zeros((tiles, TILE, LANES), jnp.float32)
        terms = soundings_partial(local, flat_length, fetched, dummy, source, observed)
        outgoing = jnp.zeros((owners * capacity, TILE, LANES), jnp.float32)
        outgoing = outgoing.at[places].set(terms).reshape(owners, capacity, TILE, LANES)
        arrived = swap(outgoing).reshape(owners * capacity, TILE, LANES)
        indexes = [asked, beside(asked)]
        terms_list = [arrived, beside(arrived)]

    bits = tuple(range(groups.bit_length() - 2))
    orders = (bits, bits[1:2] + bits[0:1] + bits[2:])
    low_give, low, high_give, high = accumulate(indexes, terms_list, block, orders)
    for step, (low_bit, high_bit) in enumerate(zip(*orders)):
        got_low = swap_over("grp", 2 << low_bit)(low_give)
        got_high = swap_over("grp", 2 << high_bit)(high_give)
        cut = low.shape[0] // 2
        if cut:
            low_give, low = got_low[:cut] + low[:cut], got_low[cut:] + low[cut:]
            high_give, high = got_high[:cut] + high[:cut], got_high[cut:] + high[cut:]
        else:
            low, high = got_low + low, got_high + high
    return jnp.concatenate([low[0], high[0]], axis=0)[:, None, :]


def solution(mesh):
    placed = (
        P(None, "mdl", None),
        P(("grp", "mdl"), None, None, None),
        P(("grp", "mdl"), None, None, None),
        P(("grp", "mdl"), None, None),
        P(("grp", "mdl"), None),
        P(("grp", "mdl"), None),
    )
    return jax.shard_map(
        per_device, mesh=mesh, in_specs=placed, out_specs=P("grp", "mdl", None), check_vma=False
    )
```

```python
import functools

import jax
import jax.numpy as jnp
from jax import lax
from jax.experimental import pallas as pl
from jax.experimental.pallas import tpu as pltpu
from jax.sharding import PartitionSpec as P

LY = 64
LZ = 8
STEPS_FWD = 4
STEPS_ADJ = 4
TILE = 32
LANES = 128
SUB = 8
PARTS = TILE // SUB

AIR = 0.05
OMEGA = 0.5
BETA = 0.5

HALVES = LANES // LY
PACKED = TILE // SUB * HALVES

VMEM = pl.BlockSpec(memory_space=pltpu.VMEM)
SMEM = pl.BlockSpec(memory_space=pltpu.SMEM)
LIMIT = 16 << 20


def call(body, name, out, in_specs, work, moved, **kwargs):
    return pl.pallas_call(
        body,
        out_shape=out,
        in_specs=in_specs,
        out_specs=jax.tree.map(lambda _: VMEM, out),
        compiler_params=pltpu.CompilerParams(vmem_limit_bytes=LIMIT),
        cost_estimate=pl.CostEstimate(flops=work, bytes_accessed=moved, transcendentals=0),
        name=name,
        **kwargs,
    )


def floats(*shape):
    return jax.ShapeDtypeStruct(shape, jnp.float32)


def place_slots(owner_flat, owners_count, capacity):
    chosen = (owner_flat[:, None] == jnp.arange(owners_count, dtype=jnp.int32)[None, :]).astype(
        jnp.int32
    )
    before = jnp.cumsum(chosen, axis=0) - chosen
    return owner_flat * capacity + jnp.sum(before * chosen, axis=1)


def swap_over(axis, mask):
    ring = [(i, i ^ mask) for i in range(lax.axis_size(axis))]
    return lambda value: lax.ppermute(value, axis, ring)


def gather_body(starts_ref, block_ref, out_ref):
    wide = starts_ref.shape[1]
    for tile in range(out_ref.shape[0]):
        start = starts_ref[tile // wide, tile % wide]
        out_ref[tile] = block_ref[pl.ds(start, TILE), :]


def gather_rows(starts, block):
    out = floats(starts.size, TILE, LANES)
    return call(gather_body, "gather_rows", out, [SMEM, VMEM], 0, 8 * out.size)(starts, block)


def low_half():
    return lax.broadcasted_iota(jnp.int32, (SUB, LANES), 1) < LY


def pack(first, second, low):
    even = jnp.where(low, first, pltpu.roll(second, LY, 1))
    odd = jnp.where(low, pltpu.roll(first, LY, 1), second)
    return even, odd


def rows_of(ref, base, step):
    return ref[pl.ds(base, SUB, stride=step * PARTS), :]


def prepare_body(source_ref, observed_ref, source_out, observed_out):
    low = low_half()
    for ref, out in ((source_ref, source_out), (observed_ref, observed_out)):
        for part in range(3):
            for z in range(LZ):
                for j in range(PARTS):
                    base = part * LZ * TILE + z + LZ * j
                    first = rows_of(ref, base, LZ)
                    second = rows_of(ref, base + 3 * LZ * TILE, LZ)
                    out[part, z, 2 * j], out[part, z, 2 * j + 1] = pack(first, second, low)


def by_rows(values):
    count = values.shape[0]
    parts = values.reshape(count, 3, LZ, TILE, LANES)
    return parts.transpose(0, 1, 3, 2, 4).reshape(count * 3 * TILE * LZ, LANES)


def prepare(source, observed):
    out = floats(3, LZ, PACKED, SUB, LANES)
    return call(
        prepare_body, "prepare", (out, out), [VMEM, VMEM], 8 * source.size, 16 * source.size
    )(by_rows(source), by_rows(observed))


def fields_body(
    starts_ref, owners_ref, lengths_ref, table_ref, answer_ref, source_ref, observed_ref, out_ref,
    field, adjoint, right, curl, scale, decay, weight,
):
    me = lax.axis_index("mdl")
    lane = lax.broadcasted_iota(jnp.int32, (SUB, LANES), 1)
    sub = lax.broadcasted_iota(jnp.int32, (SUB, LANES), 0)
    low = low_half()
    not_last = lane % LY != LY - 1
    not_first = lane % LY != 0
    top, bottom = sub != 0, sub != SUB - 1
    zero = jnp.zeros((SUB, LANES), jnp.float32)

    def y_next(value):
        return jnp.where(not_last, pltpu.roll(value, LANES - 1, 1), 0.0)

    def y_prev(value):
        return jnp.where(not_first, pltpu.roll(value, 1, 1), 0.0)

    def x_next(ref, part, z, k):
        if k + 1 < PACKED:
            return ref[part, z, k + 1]
        return jnp.where(bottom, pltpu.roll(ref[part, z, 0], SUB - 1, 0), 0.0)

    def x_prev(ref, part, z, k):
        if k > 0:
            return ref[part, z, k - 1]
        return jnp.where(top, pltpu.roll(ref[part, z, PACKED - 1], 1, 0), 0.0)

    def sweep(state):
        for z in range(LZ):
            for k in range(PACKED):
                east, north, vert = state[0, z, k], state[1, z, k], state[2, z, k]
                east_d = state[0, z + 1, k] if z + 1 < LZ else zero
                north_d = state[1, z + 1, k] if z + 1 < LZ else zero
                curl[0, z, k] = (y_next(vert) - vert) - (north_d - north)
                curl[1, z, k] = (east_d - east) - (x_next(state, 2, z, k) - vert)
                curl[2, z, k] = (x_next(state, 1, z, k) - north) - (y_next(east) - east)
            for k in range(PACKED):
                curl_x, curl_y, curl_z = curl[0, z, k], curl[1, z, k], curl[2, z, k]
                up_x = curl[0, z - 1, k] if z else zero
                up_y = curl[1, z - 1, k] if z else zero
                back_x = (up_y - curl_y) - (y_prev(curl_z) - curl_z)
                back_y = (x_prev(curl, 2, z, k) - curl_z) - (up_x - curl_x)
                back_z = (y_prev(curl_x) - curl_x) - (x_prev(curl, 1, z, k) - curl_y)
                s, d = scale[z, k], decay[z, k]
                state[0, z, k] = d * state[0, z, k] + (right[0, z, k] - s * back_x)
                state[1, z, k] = d * state[1, z, k] + (right[1, z, k] - s * back_y)
                state[2, z, k] = d * state[2, z, k] + (right[2, z, k] - s * back_z)

    for z in range(LZ):

        def layer(sounding, j):
            raw = rows_of(table_ref, starts_ref[sounding, z] + j, 1)
            sent = rows_of(answer_ref, (sounding * LZ + z) * TILE + j, 1)
            mine = jnp.full((SUB, LANES), owners_ref[sounding, z] == me)
            return jnp.where(mine, raw, sent)

        length = jnp.where(low, lengths_ref[0, z], lengths_ref[1, z])
        for j in range(PARTS):
            earth = PARTS * sub + j < length
            for odd, logs in enumerate(pack(layer(0, j), layer(1, j), low)):
                k = 2 * j + odd
                conduct = jnp.where(earth, jnp.exp(logs), AIR)
                s = OMEGA / (4.0 + conduct)
                scale[z, k] = s
                decay[z, k] = 1.0 - s * conduct
                weight[z, k] = jnp.where(earth, -conduct, 0.0)
                for part in range(3):
                    value = s * source_ref[part, z, k]
                    right[part, z, k] = value
                    field[part, z, k] = value

    @pl.loop(0, STEPS_FWD - 1)
    def _(step):
        sweep(field)

    for z in range(LZ):
        for k in range(PACKED):
            for part in range(3):
                value = scale[z, k] * (field[part, z, k] - observed_ref[part, z, k])
                right[part, z, k] = value
                adjoint[part, z, k] = value

    @pl.loop(0, STEPS_ADJ - 1)
    def _(step):
        sweep(adjoint)

    for z in range(LZ):

        def partial(k):
            total = field[0, z, k] * adjoint[0, z, k]
            total += field[1, z, k] * adjoint[1, z, k]
            total += field[2, z, k] * adjoint[2, z, k]
            return weight[z, k] * total

        for j in range(PARTS):
            first, second = pack(partial(2 * j), partial(2 * j + 1), low)
            out_ref[pl.ds(z * TILE + j, SUB, stride=PARTS), :] = first
            out_ref[pl.ds((LZ + z) * TILE + j, SUB, stride=PARTS), :] = second


def soundings_partial(starts, owners, lengths, table, answer, source, observed):
    tiles = starts.size
    planes = pltpu.VMEM((3, LZ, PACKED, SUB, LANES), jnp.float32)
    single = pltpu.VMEM((LZ, PACKED, SUB, LANES), jnp.float32)
    cells = tiles * TILE * LANES
    out = call(
        fields_body, "soundings_partial", floats(tiles * TILE, LANES),
        [SMEM] * 3 + [VMEM] * 4, 500 * cells, 40 * cells,
        scratch_shapes=[planes] * 4 + [single] * 3,
    )(starts, owners, lengths, table, answer.reshape(tiles * TILE, LANES), source, observed)
    return out.reshape(tiles, TILE, LANES)


def arranged(order):
    if not order:
        return [0]
    rest = arranged(order[1:])
    return [slot | (1 << order[0]) for slot in rest] + rest


def add_terms(starts_ref, owners_ref, terms_ref, total, share, slots):
    owner, me = lax.axis_index("mdl"), lax.axis_index("grp")
    span, wide = share + 2 * TILE, starts_ref.shape[1]
    for tile in range(terms_ref.shape[0]):
        start = starts_ref[tile // wide, tile % wide]
        first = lax.div(start, share)
        target = first + ((first ^ me) & 1)
        where = start - target * share
        wanted = (owners_ref[tile // wide, tile % wide] == owner) & (where > -TILE)
        base = ((target >> 1) ^ (me >> 1)) * span + TILE + where
        base = jnp.where(wanted, base, slots * span)
        total[pl.ds(base, TILE), :] += terms_ref[tile]


def first_body(groups, count, *refs):
    model_ref, total = refs[3 * count], refs[-1]
    me = lax.axis_index("grp")
    share = model_ref.shape[0] // groups
    total[...] = jnp.zeros_like(total)
    local = model_ref[pl.ds(pl.multiple_of(me * share, share), share), :]
    lane = lax.broadcasted_iota(jnp.int32, local.shape, 1)
    left = jnp.where(lane == 0, local, pltpu.roll(local, 1, 1))
    right = jnp.where(lane == LANES - 1, local, pltpu.roll(local, LANES - 1, 1))
    total[TILE : TILE + share, :] = BETA * (2.0 * local - left - right)
    for i in range(count):
        add_terms(*refs[3 * i : 3 * i + 3], total, share, groups // 2)


def first_sums(groups_of, block):
    groups = lax.axis_size("grp")
    share = block.shape[0] // groups
    out = floats(groups // 2 * (share + 2 * TILE) + TILE, LANES)
    flat = [a for triple in groups_of for a in triple]
    return call(
        functools.partial(first_body, groups, len(groups_of)), "first_sums", out,
        [SMEM, SMEM, VMEM] * len(groups_of) + [VMEM], out.size, 8 * out.size,
    )(*flat, block)


def last_body(orders, groups, share, count, *refs):
    total, outs = refs[3 * count + 1], refs[3 * count + 2 :]
    span, slots, half = share + 2 * TILE, groups // 2, share // 2
    for i in range(count):
        add_terms(*refs[3 * i : 3 * i + 3], total, share, slots)
    for which, order in enumerate(orders):
        for place, slot in enumerate(arranged(order)):
            out = outs[2 * which + (place * 2 >= slots)]
            begin = slot * span + TILE + which * half
            out[place % (slots // 2)] = total[begin : begin + half, :]


def last_sums(groups_of, total, rows, orders):
    groups = lax.axis_size("grp")
    share, slots = rows // groups, groups // 2
    out = floats(slots // 2, share // 2, LANES)
    flat = [a for triple in groups_of for a in triple]
    count = len(groups_of)
    return call(
        functools.partial(last_body, orders, groups, share, count), "last_sums",
        (floats(*total.shape),) + (out,) * 4, [SMEM, SMEM, VMEM] * count + [VMEM],
        total.size, 8 * total.size, input_output_aliases={3 * count: 0},
    )(*flat, total)[1:]


def finish_body(got_low, low, got_high, high, out_ref):
    half = out_ref.shape[0] // 2
    out_ref[:half] = got_low[0] + low[0]
    out_ref[half:] = got_high[0] + high[0]


def per_device(model, source, observed, owner_ids, offsets, lengths):
    rows, owners_count, groups = model.shape[0], lax.axis_size("mdl"), lax.axis_size("grp")
    block = model.reshape(rows, LANES)
    tiles = source.shape[0] * LZ
    across, beside = swap_over("mdl", 1), swap_over("grp", 1)
    if owners_count == 2:
        asked, asked_ids = lax.optimization_barrier((across(offsets), across(owner_ids)))
        owners, asked_owners = (ids.reshape(offsets.shape) for ids in (owner_ids, asked_ids))
        source, observed = prepare(source, observed)
        answer = across(gather_rows(asked, block))
        told = beside(jnp.concatenate([offsets, owners, asked, asked_owners]))
        answer, told = lax.optimization_barrier((answer, told))
        told = told.reshape(4, *offsets.shape)
        terms = soundings_partial(offsets, owners, lengths, block, answer, source, observed)
        others = across(terms)
        total = first_sums([(offsets, owners, terms), (told[0], told[1], beside(terms))], block)
        final = [(asked, asked_owners, others), (told[2], told[3], beside(others))]
    else:
        capacity = max(4, 2 * tiles // owners_count)
        places = place_slots(owner_ids.reshape(tiles), owners_count, capacity)
        swap = functools.partial(
            lax.all_to_all, axis_name="mdl", split_axis=0, concat_axis=0, tiled=True
        )
        request = jnp.zeros((owners_count * capacity,), jnp.int32).at[places].set(
            offsets.reshape(tiles)
        )
        asked = swap(request.reshape(owners_count, capacity))
        source, observed = prepare(source, observed)
        given = gather_rows(asked, block).reshape(owners_count, capacity, TILE, LANES)
        fetched = swap(given).reshape(owners_count * capacity * TILE, LANES)
        mine = jnp.full_like(asked, lax.axis_index("mdl"))
        terms = soundings_partial(
            (places * TILE).reshape(offsets.shape), jnp.full_like(offsets, lax.axis_index("mdl")),
            lengths, fetched, jnp.zeros((tiles, TILE, LANES), jnp.float32), source, observed,
        )
        outgoing = jnp.zeros((owners_count * capacity, TILE, LANES), jnp.float32)
        outgoing = outgoing.at[places].set(terms).reshape(owners_count, capacity, TILE, LANES)
        arrived = swap(outgoing).reshape(owners_count * capacity, TILE, LANES)
        total = first_sums([(asked, mine, arrived)], block)
        final = [(beside(asked), mine, beside(arrived))]

    bits = tuple(range(groups.bit_length() - 2))
    orders = (bits, bits[1:2] + bits[0:1] + bits[2:])
    low_give, low, high_give, high = last_sums(final, total, rows, orders)
    for low_bit, high_bit in zip(*orders):
        got_low = swap_over("grp", 2 << low_bit)(low_give)
        got_high = swap_over("grp", 2 << high_bit)(high_give)
        cut = low.shape[0] // 2
        if cut:
            low_give, low = got_low[:cut] + low[:cut], got_low[cut:] + low[cut:]
            high_give, high = got_high[:cut] + high[:cut], got_high[cut:] + high[cut:]
    out = call(
        finish_body, "finish", floats(rows // groups, LANES), [VMEM] * 4, low.size, 24 * low.size
    )(got_low, low, got_high, high)
    return out[:, None, :]


def solution(mesh):
    placed = (
        P(None, "mdl", None),
        P(("grp", "mdl"), None, None, None),
        P(("grp", "mdl"), None, None, None),
        P(("grp", "mdl"), None, None),
        P(("grp", "mdl"), None),
        P(("grp", "mdl"), None),
    )
    return jax.shard_map(
        per_device, mesh=mesh, in_specs=placed, out_specs=P("grp", "mdl", None), check_vma=False
    )
```

```python
import functools

import jax
import jax.numpy as jnp
from jax import lax
from jax.experimental import pallas as pl
from jax.experimental.pallas import tpu as pltpu
from jax.sharding import PartitionSpec as P


LY = 64
LZ = 8
STEPS_FWD = 4
STEPS_ADJ = 4
TILE = 32
LANES = 128
SUB = 8
PARTS = TILE // SUB

AIR = 0.05
OMEGA = 0.5
BETA = 0.5

HALVES = LANES // LY
PACKED = TILE // SUB * HALVES

VMEM = pl.BlockSpec(memory_space=pltpu.VMEM)
SMEM = pl.BlockSpec(memory_space=pltpu.SMEM)
LIMIT = 16 << 20


def call(body, out, in_specs, work, moved, **kwargs):
    return pl.pallas_call(
        body,
        out_shape=out,
        in_specs=in_specs,
        out_specs=jax.tree.map(lambda _: VMEM, out),
        compiler_params=pltpu.CompilerParams(vmem_limit_bytes=LIMIT),
        cost_estimate=pl.CostEstimate(flops=work, bytes_accessed=moved, transcendentals=0),
        **kwargs,
    )


def floats(*shape):
    return jax.ShapeDtypeStruct(shape, jnp.float32)


def place_slots(owner_flat, owners_count, capacity):
    chosen = (owner_flat[:, None] == jnp.arange(owners_count, dtype=jnp.int32)[None, :]).astype(
        jnp.int32
    )
    before = jnp.cumsum(chosen, axis=0) - chosen
    return owner_flat * capacity + jnp.sum(before * chosen, axis=1)


def swap_over(axis, mask):
    ring = [(i, i ^ mask) for i in range(lax.axis_size(axis))]
    return lambda value: lax.ppermute(value, axis, ring)


def gather_body(starts_ref, block_ref, out_ref):
    wide = starts_ref.shape[1]
    for tile in range(out_ref.shape[0]):
        start = starts_ref[tile // wide, tile % wide]
        out_ref[tile] = block_ref[pl.ds(start, TILE), :]


def gather_rows(starts, block):
    out = floats(starts.size, TILE, LANES)
    return call(gather_body, out, [SMEM, VMEM], 0, 8 * out.size)(starts, block)


def low_half():
    return lax.broadcasted_iota(jnp.int32, (SUB, LANES), 1) < LY


def pack(first, second, low):
    even = jnp.where(low, first, pltpu.roll(second, LY, 1))
    odd = jnp.where(low, pltpu.roll(first, LY, 1), second)
    return even, odd


def rows_of(ref, base, step):
    return ref[pl.ds(base, SUB, stride=step * PARTS), :]


def prepare_body(source_ref, observed_ref, source_out, observed_out):
    low = low_half()
    for ref, out in ((source_ref, source_out), (observed_ref, observed_out)):
        for part in range(3):
            for z in range(LZ):
                for j in range(PARTS):
                    base = part * LZ * TILE + z + LZ * j
                    first = rows_of(ref, base, LZ)
                    second = rows_of(ref, base + 3 * LZ * TILE, LZ)
                    out[part, z, 2 * j], out[part, z, 2 * j + 1] = pack(first, second, low)


def by_rows(values):
    count = values.shape[0]
    parts = values.reshape(count, 3, LZ, TILE, LANES)
    return parts.transpose(0, 1, 3, 2, 4).reshape(count * 3 * TILE * LZ, LANES)


def prepare(source, observed):
    out = floats(3, LZ, PACKED, SUB, LANES)
    return call(
        prepare_body, (out, out), [VMEM, VMEM], 8 * source.size, 16 * source.size
    )(by_rows(source), by_rows(observed))


def fields_body(
    starts_ref, owners_ref, lengths_ref, table_ref, answer_ref, source_ref, observed_ref, kept_ref,
    given_ref, field, adjoint, right, curl, scale, decay, weight,
):
    me = lax.axis_index("mdl")
    lane = lax.broadcasted_iota(jnp.int32, (SUB, LANES), 1)
    sub = lax.broadcasted_iota(jnp.int32, (SUB, LANES), 0)
    low = low_half()
    not_last = lane % LY != LY - 1
    not_first = lane % LY != 0
    top, bottom = sub != 0, sub != SUB - 1
    zero = jnp.zeros((SUB, LANES), jnp.float32)

    def y_next(value):
        return jnp.where(not_last, pltpu.roll(value, LANES - 1, 1), 0.0)

    def y_prev(value):
        return jnp.where(not_first, pltpu.roll(value, 1, 1), 0.0)

    def x_next(ref, part, z, k):
        if k + 1 < PACKED:
            return ref[part, z, k + 1]
        return jnp.where(bottom, pltpu.roll(ref[part, z, 0], SUB - 1, 0), 0.0)

    def x_prev(ref, part, z, k):
        if k > 0:
            return ref[part, z, k - 1]
        return jnp.where(top, pltpu.roll(ref[part, z, PACKED - 1], 1, 0), 0.0)

    def sweep(state):
        for z in range(LZ):
            for k in range(PACKED):
                east, north, vert = state[0, z, k], state[1, z, k], state[2, z, k]
                east_d = state[0, z + 1, k] if z + 1 < LZ else zero
                north_d = state[1, z + 1, k] if z + 1 < LZ else zero
                curl[0, z, k] = (y_next(vert) - vert) - (north_d - north)
                curl[1, z, k] = (east_d - east) - (x_next(state, 2, z, k) - vert)
                curl[2, z, k] = (x_next(state, 1, z, k) - north) - (y_next(east) - east)
            for k in range(PACKED):
                curl_x, curl_y, curl_z = curl[0, z, k], curl[1, z, k], curl[2, z, k]
                up_x = curl[0, z - 1, k] if z else zero
                up_y = curl[1, z - 1, k] if z else zero
                back_x = (up_y - curl_y) - (y_prev(curl_z) - curl_z)
                back_y = (x_prev(curl, 2, z, k) - curl_z) - (up_x - curl_x)
                back_z = (y_prev(curl_x) - curl_x) - (x_prev(curl, 1, z, k) - curl_y)
                s, d = scale[z, k], decay[z, k]
                state[0, z, k] = d * state[0, z, k] + (right[0, z, k] - s * back_x)
                state[1, z, k] = d * state[1, z, k] + (right[1, z, k] - s * back_y)
                state[2, z, k] = d * state[2, z, k] + (right[2, z, k] - s * back_z)

    for z in range(LZ):

        def layer(sounding, j):
            raw = rows_of(table_ref, starts_ref[sounding, z] + j, 1)
            sent = rows_of(answer_ref, (sounding * LZ + z) * TILE + j, 1)
            mine = jnp.full((SUB, LANES), owners_ref[sounding, z] == me)
            return jnp.where(mine, raw, sent)

        length = jnp.where(low, lengths_ref[0, z], lengths_ref[1, z])
        for j in range(PARTS):
            earth = PARTS * sub + j < length
            for odd, logs in enumerate(pack(layer(0, j), layer(1, j), low)):
                k = 2 * j + odd
                conduct = jnp.where(earth, jnp.exp(logs), AIR)
                s = OMEGA / (4.0 + conduct)
                scale[z, k] = s
                decay[z, k] = 1.0 - s * conduct
                weight[z, k] = jnp.where(earth, -conduct, 0.0)
                for part in range(3):
                    value = s * source_ref[part, z, k]
                    right[part, z, k] = value
                    field[part, z, k] = value

    @pl.loop(0, STEPS_FWD - 1)
    def _(step):
        sweep(field)

    for z in range(LZ):
        for k in range(PACKED):
            for part in range(3):
                value = scale[z, k] * (field[part, z, k] - observed_ref[part, z, k])
                right[part, z, k] = value
                adjoint[part, z, k] = value

    @pl.loop(0, STEPS_ADJ - 1)
    def _(step):
        sweep(adjoint)

    for z in range(LZ):

        def partial(k):
            total = field[0, z, k] * adjoint[0, z, k]
            total += field[1, z, k] * adjoint[1, z, k]
            total += field[2, z, k] * adjoint[2, z, k]
            return weight[z, k] * total

        for j in range(PARTS):
            first, second = pack(partial(2 * j), partial(2 * j + 1), low)
            for sounding, value in enumerate((first, second)):
                mine = jnp.full((SUB, LANES), owners_ref[sounding, z] == me)
                place = pl.ds((sounding * LZ + z) * TILE + j, SUB, stride=PARTS)
                kept_ref[place, :] = jnp.where(mine, value, 0.0)
                given_ref[place, :] = jnp.where(mine, 0.0, value)


def soundings_partial(starts, owners, lengths, table, answer, source, observed):
    tiles = starts.size
    planes = pltpu.VMEM((3, LZ, PACKED, SUB, LANES), jnp.float32)
    single = pltpu.VMEM((LZ, PACKED, SUB, LANES), jnp.float32)
    cells = tiles * TILE * LANES
    out = floats(tiles * TILE, LANES)
    kept, given = call(
        fields_body, (out, out),
        [SMEM] * 3 + [VMEM] * 4, 500 * cells, 40 * cells,
        scratch_shapes=[planes] * 4 + [single] * 3,
    )(starts, owners, lengths, table, answer.reshape(tiles * TILE, LANES), source, observed)
    return kept.reshape(tiles, TILE, LANES), given.reshape(tiles, TILE, LANES)


def arranged(order):
    if not order:
        return [0]
    rest = arranged(order[1:])
    return [slot | (1 << order[0]) for slot in rest] + rest


def add_terms(starts_ref, terms_ref, total, share, slots):
    me = lax.axis_index("grp")
    span, wide = share + 2 * TILE, starts_ref.shape[1]
    for tile in range(terms_ref.shape[0]):
        start = starts_ref[tile // wide, tile % wide]
        first = lax.div(start, share)
        target = first + ((first ^ me) & 1)
        where = start - target * share
        base = ((target >> 1) ^ (me >> 1)) * span + TILE + where
        base = jnp.where(where > -TILE, base, slots * span)
        total[pl.ds(base, TILE), :] += terms_ref[tile]


def first_body(groups, count, *refs):
    model_ref, total = refs[2 * count], refs[-1]
    me = lax.axis_index("grp")
    share = model_ref.shape[0] // groups
    total[...] = jnp.zeros_like(total)
    local = model_ref[pl.ds(pl.multiple_of(me * share, share), share), :]
    lane = lax.broadcasted_iota(jnp.int32, local.shape, 1)
    left = jnp.where(lane == 0, local, pltpu.roll(local, 1, 1))
    right = jnp.where(lane == LANES - 1, local, pltpu.roll(local, LANES - 1, 1))
    total[TILE : TILE + share, :] = BETA * (2.0 * local - left - right)
    for i in range(count):
        add_terms(*refs[2 * i : 2 * i + 2], total, share, groups // 2)


def first_sums(groups_of, block):
    groups = lax.axis_size("grp")
    share = block.shape[0] // groups
    out = floats(groups // 2 * (share + 2 * TILE) + TILE, LANES)
    flat = [a for pair in groups_of for a in pair]
    return call(
        functools.partial(first_body, groups, len(groups_of)), out,
        [SMEM, VMEM] * len(groups_of) + [VMEM], out.size, 8 * out.size,
    )(*flat, block)


def last_body(orders, groups, share, count, *refs):
    total, outs = refs[2 * count + 1], refs[2 * count + 2 :]
    span, slots, half = share + 2 * TILE, groups // 2, share // 2
    for i in range(count):
        add_terms(*refs[2 * i : 2 * i + 2], total, share, slots)
    for which, order in enumerate(orders):
        for place, slot in enumerate(arranged(order)):
            out = outs[2 * which + (place * 2 >= slots)]
            begin = slot * span + TILE + which * half
            out[place % (slots // 2)] = total[begin : begin + half, :]


def last_sums(groups_of, total, rows, orders):
    groups = lax.axis_size("grp")
    share, slots = rows // groups, groups // 2
    out = floats(slots // 2, share // 2, LANES)
    flat = [a for pair in groups_of for a in pair]
    count = len(groups_of)
    return call(
        functools.partial(last_body, orders, groups, share, count),
        (floats(*total.shape),) + (out,) * 4, [SMEM, VMEM] * count + [VMEM],
        total.size, 8 * total.size, input_output_aliases={2 * count: 0},
    )(*flat, total)[1:]


def join_body(got_low, low, got_high, high, give_ref, keep_ref):
    cut = low.shape[0] // 2
    for half, (got, held) in enumerate(((got_low, low), (got_high, high))):
        give_ref[half] = got[:cut] + held[:cut]
        keep_ref[half] = got[cut:] + held[cut:]


def finish_body(got, held, out_ref):
    out_ref[...] = got[...] + held[...]


def halve(low_give, low, high_give, high, orders):
    bit_pairs = list(zip(*orders))
    for step, (low_bit, high_bit) in enumerate(bit_pairs[:2]):
        got_low = swap_over("grp", 2 << low_bit)(low_give)
        got_high = swap_over("grp", 2 << high_bit)(high_give)
        cut = low.shape[0] // 2
        if step == 0:
            low_give, low = got_low[:cut] + low[:cut], got_low[cut:] + low[cut:]
            high_give, high = got_high[:cut] + high[:cut], got_high[cut:] + high[cut:]
    out = floats(2, cut, *low.shape[1:])
    give, keep = call(
        join_body, (out, out), [VMEM] * 4, low.size, 24 * low.size
    )(got_low, low, got_high, high)
    for bit, _ in bit_pairs[2:]:
        got = swap_over("grp", 2 << bit)(give)
        cut = keep.shape[1] // 2
        if cut:
            give, keep = got[:, :cut] + keep[:, :cut], got[:, cut:] + keep[:, cut:]
    return call(finish_body, floats(*keep.shape), [VMEM] * 2, keep.size, 12 * keep.size)(got, keep)


def hold_body(block_ref, out_ref, sem):
    copy = pltpu.make_async_copy(block_ref, out_ref, sem)
    copy.start()
    copy.wait()


def hold(block):
    return call(
        hold_body, floats(*block.shape), [pl.BlockSpec(memory_space=pltpu.HBM)], 0,
        8 * block.size, scratch_shapes=[pltpu.SemaphoreType.DMA],
    )(block)


def per_device(model, source, observed, owner_ids, offsets, lengths):
    rows, owners_count, groups = model.shape[0], lax.axis_size("mdl"), lax.axis_size("grp")
    tiles = source.shape[0] * LZ
    across, beside = swap_over("mdl", 1), swap_over("grp", 1)
    block = hold(model.reshape(rows, LANES))
    source, observed = prepare(source, observed)
    if owners_count == 2:
        asked = across(offsets)
        asked, block = lax.optimization_barrier((asked, block))
        given = gather_rows(asked, block)
        answer = across(given)
        told = beside(jnp.concatenate([offsets, asked]))
        answer, told = lax.optimization_barrier((answer, told))
        told = told.reshape(2, *offsets.shape)
        kept, given = soundings_partial(
            offsets, owner_ids.reshape(offsets.shape), lengths, block, answer, source, observed
        )
        others = across(given)
        kept_beside = beside(kept)
        total = first_sums([(offsets, kept), (told[0], kept_beside)], block)
        final = [(asked, others), (told[1], beside(others))]
    else:
        capacity = max(4, 2 * tiles // owners_count)
        places = place_slots(owner_ids.reshape(tiles), owners_count, capacity)
        swap = functools.partial(
            lax.all_to_all, axis_name="mdl", split_axis=0, concat_axis=0, tiled=True
        )
        request = jnp.zeros((owners_count * capacity,), jnp.int32).at[places].set(
            offsets.reshape(tiles)
        )
        asked = swap(request.reshape(owners_count, capacity))
        given = gather_rows(asked, block).reshape(owners_count, capacity, TILE, LANES)
        fetched = swap(given).reshape(owners_count * capacity * TILE, LANES)
        terms, _ = soundings_partial(
            (places * TILE).reshape(offsets.shape), jnp.full_like(offsets, lax.axis_index("mdl")),
            lengths, fetched, jnp.zeros((tiles, TILE, LANES), jnp.float32), source, observed,
        )
        outgoing = jnp.zeros((owners_count * capacity, TILE, LANES), jnp.float32)
        outgoing = outgoing.at[places].set(terms).reshape(owners_count, capacity, TILE, LANES)
        arrived = swap(outgoing).reshape(owners_count * capacity, TILE, LANES)
        total = first_sums([(asked, arrived)], block)
        final = [(beside(asked), beside(arrived))]

    bits = tuple(range(groups.bit_length() - 2))
    orders = (bits, bits[1:2] + bits[0:1] + bits[2:])
    sums = halve(*last_sums(final, total, rows, orders), orders)
    return sums.reshape(rows // groups, 1, LANES)


def solution(mesh):
    placed = (
        P(None, "mdl", None),
        P(("grp", "mdl"), None, None, None),
        P(("grp", "mdl"), None, None, None),
        P(("grp", "mdl"), None, None),
        P(("grp", "mdl"), None),
        P(("grp", "mdl"), None),
    )

    return jax.shard_map(
        per_device, mesh=mesh, in_specs=placed, out_specs=P("grp", "mdl", None), check_vma=False
    )
```

```python
import functools

import jax
import jax.numpy as jnp
from jax import lax
from jax.experimental import pallas as pl
from jax.experimental.pallas import tpu as pltpu
from jax.sharding import PartitionSpec as P


LY = 64
LZ = 8
STEPS_FWD = 4
STEPS_ADJ = 4
TILE = 32
LANES = 128
SUB = 8
PARTS = TILE // SUB

AIR = 0.05
OMEGA = 0.5
BETA = 0.5

HALVES = LANES // LY
PACKED = TILE // SUB * HALVES

VMEM = pl.BlockSpec(memory_space=pltpu.VMEM)
SMEM = pl.BlockSpec(memory_space=pltpu.SMEM)
LIMIT = 16 << 20


def call(body, out, in_specs, work, moved, **kwargs):
    return pl.pallas_call(
        body,
        out_shape=out,
        in_specs=in_specs,
        out_specs=jax.tree.map(lambda _: VMEM, out),
        compiler_params=pltpu.CompilerParams(vmem_limit_bytes=LIMIT),
        cost_estimate=pl.CostEstimate(flops=work, bytes_accessed=moved, transcendentals=0),
        **kwargs,
    )


def floats(*shape):
    return jax.ShapeDtypeStruct(shape, jnp.float32)


def place_slots(owner_flat, owners_count, capacity):
    chosen = (owner_flat[:, None] == jnp.arange(owners_count, dtype=jnp.int32)[None, :]).astype(
        jnp.int32
    )
    before = jnp.cumsum(chosen, axis=0) - chosen
    return owner_flat * capacity + jnp.sum(before * chosen, axis=1)


def swap_over(axis, mask):
    ring = [(i, i ^ mask) for i in range(lax.axis_size(axis))]
    return lambda value: lax.ppermute(value, axis, ring)


def gather_body(starts_ref, block_ref, out_ref):
    wide = starts_ref.shape[1]
    for tile in range(out_ref.shape[0]):
        start = starts_ref[tile // wide, tile % wide]
        out_ref[tile] = block_ref[pl.ds(start, TILE), :]


def gather_rows(starts, block):
    out = floats(starts.size, TILE, LANES)
    return call(gather_body, out, [SMEM, VMEM], 0, 8 * out.size)(starts, block)


def low_half():
    return lax.broadcasted_iota(jnp.int32, (SUB, LANES), 1) < LY


def pack(first, second, low):
    even = jnp.where(low, first, pltpu.roll(second, LY, 1))
    odd = jnp.where(low, pltpu.roll(first, LY, 1), second)
    return even, odd


def rows_of(ref, base, step):
    return ref[pl.ds(base, SUB, stride=step * PARTS), :]


def prepare_body(source_ref, observed_ref, source_out, observed_out):
    low = low_half()
    for ref, out in ((source_ref, source_out), (observed_ref, observed_out)):
        for part in range(3):
            for z in range(LZ):
                for j in range(PARTS):
                    base = part * LZ * TILE + z + LZ * j
                    first = rows_of(ref, base, LZ)
                    second = rows_of(ref, base + 3 * LZ * TILE, LZ)
                    out[part, z, 2 * j], out[part, z, 2 * j + 1] = pack(first, second, low)


def by_rows(values):
    count = values.shape[0]
    parts = values.reshape(count, 3, LZ, TILE, LANES)
    return parts.transpose(0, 1, 3, 2, 4).reshape(count * 3 * TILE * LZ, LANES)


def prepare(source, observed):
    out = floats(3, LZ, PACKED, SUB, LANES)
    return call(
        prepare_body, (out, out), [VMEM, VMEM], 8 * source.size, 16 * source.size
    )(by_rows(source), by_rows(observed))


def fields_body(
    starts_ref, owners_ref, lengths_ref, table_ref, answer_ref, source_ref, observed_ref, kept_ref,
    given_ref, field, adjoint, right, curl, scale, decay, weight,
):
    me = lax.axis_index("mdl")
    lane = lax.broadcasted_iota(jnp.int32, (SUB, LANES), 1)
    sub = lax.broadcasted_iota(jnp.int32, (SUB, LANES), 0)
    low = low_half()
    not_last = lane % LY != LY - 1
    not_first = lane % LY != 0
    top, bottom = sub != 0, sub != SUB - 1
    zero = jnp.zeros((SUB, LANES), jnp.float32)

    def y_next(value):
        return jnp.where(not_last, pltpu.roll(value, LANES - 1, 1), 0.0)

    def y_prev(value):
        return jnp.where(not_first, pltpu.roll(value, 1, 1), 0.0)

    def x_next(ref, part, z, k):
        if k + 1 < PACKED:
            return ref[part, z, k + 1]
        return jnp.where(bottom, pltpu.roll(ref[part, z, 0], SUB - 1, 0), 0.0)

    def x_prev(ref, part, z, k):
        if k > 0:
            return ref[part, z, k - 1]
        return jnp.where(top, pltpu.roll(ref[part, z, PACKED - 1], 1, 0), 0.0)

    def sweep(state):
        for z in range(LZ):
            for k in range(PACKED):
                east, north, vert = state[0, z, k], state[1, z, k], state[2, z, k]
                east_d = state[0, z + 1, k] if z + 1 < LZ else zero
                north_d = state[1, z + 1, k] if z + 1 < LZ else zero
                curl[0, z, k] = (y_next(vert) - vert) - (north_d - north)
                curl[1, z, k] = (east_d - east) - (x_next(state, 2, z, k) - vert)
                curl[2, z, k] = (x_next(state, 1, z, k) - north) - (y_next(east) - east)
            for k in range(PACKED):
                curl_x, curl_y, curl_z = curl[0, z, k], curl[1, z, k], curl[2, z, k]
                up_x = curl[0, z - 1, k] if z else zero
                up_y = curl[1, z - 1, k] if z else zero
                back_x = (up_y - curl_y) - (y_prev(curl_z) - curl_z)
                back_y = (x_prev(curl, 2, z, k) - curl_z) - (up_x - curl_x)
                back_z = (y_prev(curl_x) - curl_x) - (x_prev(curl, 1, z, k) - curl_y)
                s, d = scale[z, k], decay[z, k]
                state[0, z, k] = d * state[0, z, k] + (right[0, z, k] - s * back_x)
                state[1, z, k] = d * state[1, z, k] + (right[1, z, k] - s * back_y)
                state[2, z, k] = d * state[2, z, k] + (right[2, z, k] - s * back_z)

    for z in range(LZ):

        def layer(sounding, j):
            raw = rows_of(table_ref, starts_ref[sounding, z] + j, 1)
            sent = rows_of(answer_ref, (sounding * LZ + z) * TILE + j, 1)
            mine = jnp.full((SUB, LANES), owners_ref[sounding, z] == me)
            return jnp.where(mine, raw, sent)

        length = jnp.where(low, lengths_ref[0, z], lengths_ref[1, z])
        for j in range(PARTS):
            earth = PARTS * sub + j < length
            for odd, logs in enumerate(pack(layer(0, j), layer(1, j), low)):
                k = 2 * j + odd
                conduct = jnp.where(earth, jnp.exp(logs), AIR)
                s = OMEGA / (4.0 + conduct)
                scale[z, k] = s
                decay[z, k] = 1.0 - s * conduct
                weight[z, k] = jnp.where(earth, -conduct, 0.0)
                for part in range(3):
                    value = s * source_ref[part, z, k]
                    right[part, z, k] = value
                    field[part, z, k] = value

    @pl.loop(0, STEPS_FWD - 1)
    def _(step):
        sweep(field)

    for z in range(LZ):
        for k in range(PACKED):
            for part in range(3):
                value = scale[z, k] * (field[part, z, k] - observed_ref[part, z, k])
                right[part, z, k] = value
                adjoint[part, z, k] = value

    @pl.loop(0, STEPS_ADJ - 1)
    def _(step):
        sweep(adjoint)

    for z in range(LZ):

        def partial(k):
            total = field[0, z, k] * adjoint[0, z, k]
            total += field[1, z, k] * adjoint[1, z, k]
            total += field[2, z, k] * adjoint[2, z, k]
            return weight[z, k] * total

        for j in range(PARTS):
            first, second = pack(partial(2 * j), partial(2 * j + 1), low)
            for sounding, value in enumerate((first, second)):
                mine = jnp.full((SUB, LANES), owners_ref[sounding, z] == me)
                place = pl.ds((sounding * LZ + z) * TILE + j, SUB, stride=PARTS)
                kept_ref[place, :] = jnp.where(mine, value, 0.0)
                given_ref[place, :] = jnp.where(mine, 0.0, value)


def soundings_partial(starts, owners, lengths, table, answer, source, observed):
    tiles = starts.size
    planes = pltpu.VMEM((3, LZ, PACKED, SUB, LANES), jnp.float32)
    single = pltpu.VMEM((LZ, PACKED, SUB, LANES), jnp.float32)
    cells = tiles * TILE * LANES
    out = floats(tiles * TILE, LANES)
    kept, given = call(
        fields_body, (out, out),
        [SMEM] * 3 + [VMEM] * 4, 500 * cells, 40 * cells,
        scratch_shapes=[planes] * 4 + [single] * 3,
    )(starts, owners, lengths, table, answer.reshape(tiles * TILE, LANES), source, observed)
    return kept.reshape(tiles, TILE, LANES), given.reshape(tiles, TILE, LANES)


def arranged(order):
    if not order:
        return [0]
    rest = arranged(order[1:])
    return [slot | (1 << order[0]) for slot in rest] + rest


def slot_of(target, me):
    far = (target >> 1) ^ (me >> 1)
    flip = (far ^ (far >> 1)) & (me & 1)
    return far ^ (flip | (flip << 1))


def add_terms(starts_ref, terms_ref, total, share, slots):
    me = lax.axis_index("grp")
    span, wide = share + 2 * TILE, starts_ref.shape[1]
    for tile in range(terms_ref.shape[0]):
        start = starts_ref[tile // wide, tile % wide]
        first = lax.div(start, share)
        target = first + ((first ^ me) & 1)
        where = start - target * share
        base = slot_of(target, me) * span + TILE + where
        base = jnp.where(where > -TILE, base, slots * span)
        total[pl.ds(base, TILE), :] += terms_ref[tile]


def first_body(groups, count, *refs):
    model_ref, total = refs[2 * count], refs[-1]
    me = lax.axis_index("grp")
    share = model_ref.shape[0] // groups
    total[...] = jnp.zeros_like(total)
    local = model_ref[pl.ds(pl.multiple_of(me * share, share), share), :]
    lane = lax.broadcasted_iota(jnp.int32, local.shape, 1)
    left = jnp.where(lane == 0, local, pltpu.roll(local, 1, 1))
    right = jnp.where(lane == LANES - 1, local, pltpu.roll(local, LANES - 1, 1))
    total[TILE : TILE + share, :] = BETA * (2.0 * local - left - right)
    for i in range(count):
        add_terms(*refs[2 * i : 2 * i + 2], total, share, groups // 2)


def first_sums(groups_of, block):
    groups = lax.axis_size("grp")
    share = block.shape[0] // groups
    out = floats(groups // 2 * (share + 2 * TILE) + TILE, LANES)
    flat = [a for pair in groups_of for a in pair]
    return call(
        functools.partial(first_body, groups, len(groups_of)), out,
        [SMEM, VMEM] * len(groups_of) + [VMEM], out.size, 8 * out.size,
    )(*flat, block)


def last_body(groups, share, count, *refs):
    total, give, keep = refs[2 * count + 1 :]
    span, slots = share + 2 * TILE, groups // 2
    for i in range(count):
        add_terms(*refs[2 * i : 2 * i + 2], total, share, slots)
    for place, slot in enumerate(arranged(tuple(range(slots.bit_length() - 1)))):
        begin = slot * span + TILE
        out = keep if place * 2 >= slots else give
        out[place % (slots // 2)] = total[begin : begin + share, :]


def last_sums(groups_of, total, rows):
    groups = lax.axis_size("grp")
    share, slots = rows // groups, groups // 2
    out = floats(slots // 2, share, LANES)
    flat = [a for pair in groups_of for a in pair]
    count = len(groups_of)
    return call(
        functools.partial(last_body, groups, share, count),
        (floats(*total.shape), out, out), [SMEM, VMEM] * count + [VMEM],
        total.size, 8 * total.size, input_output_aliases={2 * count: 0},
    )(*flat, total)[1:]


def finish_body(got, held, out_ref):
    out_ref[...] = got[0] + held[0]


def halve(give, keep):
    groups = lax.axis_size("grp")
    bits = groups.bit_length() - 2
    for step in range(bits):
        other = 1 - step if step < 2 else step
        ring = [(i, i ^ (2 << (other if i & 1 else step))) for i in range(groups)]
        got = lax.ppermute(give, "grp", ring)
        cut = keep.shape[0] // 2
        if cut:
            give, keep = got[:cut] + keep[:cut], got[cut:] + keep[cut:]
    return call(
        finish_body, floats(*keep.shape[1:]), [VMEM] * 2, keep.size, 12 * keep.size
    )(got, keep)


def hold_body(block_ref, out_ref, sem):
    copy = pltpu.make_async_copy(block_ref, out_ref, sem)
    copy.start()
    copy.wait()


def hold(block):
    return call(
        hold_body, floats(*block.shape), [pl.BlockSpec(memory_space=pltpu.HBM)], 0,
        8 * block.size, scratch_shapes=[pltpu.SemaphoreType.DMA],
    )(block)


def per_device(model, source, observed, owner_ids, offsets, lengths):
    rows, owners_count = model.shape[0], lax.axis_size("mdl")
    tiles = source.shape[0] * LZ
    across, beside = swap_over("mdl", 1), swap_over("grp", 1)
    block = hold(model.reshape(rows, LANES))
    source, observed = prepare(source, observed)
    if owners_count == 2:
        asked = across(offsets)
        asked, block = lax.optimization_barrier((asked, block))
        given = gather_rows(asked, block)
        answer = across(given)
        told = beside(jnp.concatenate([offsets, asked]))
        answer, told = lax.optimization_barrier((answer, told))
        told = told.reshape(2, *offsets.shape)
        kept, given = soundings_partial(
            offsets, owner_ids.reshape(offsets.shape), lengths, block, answer, source, observed
        )
        others = across(given)
        kept_beside = beside(kept)
        total = first_sums([(offsets, kept), (told[0], kept_beside)], block)
        final = [(asked, others), (told[1], beside(others))]
    else:
        capacity = max(4, 2 * tiles // owners_count)
        places = place_slots(owner_ids.reshape(tiles), owners_count, capacity)
        swap = functools.partial(
            lax.all_to_all, axis_name="mdl", split_axis=0, concat_axis=0, tiled=True
        )
        request = jnp.zeros((owners_count * capacity,), jnp.int32).at[places].set(
            offsets.reshape(tiles)
        )
        asked = swap(request.reshape(owners_count, capacity))
        given = gather_rows(asked, block).reshape(owners_count, capacity, TILE, LANES)
        fetched = swap(given).reshape(owners_count * capacity * TILE, LANES)
        terms, _ = soundings_partial(
            (places * TILE).reshape(offsets.shape), jnp.full_like(offsets, lax.axis_index("mdl")),
            lengths, fetched, jnp.zeros((tiles, TILE, LANES), jnp.float32), source, observed,
        )
        outgoing = jnp.zeros((owners_count * capacity, TILE, LANES), jnp.float32)
        outgoing = outgoing.at[places].set(terms).reshape(owners_count, capacity, TILE, LANES)
        arrived = swap(outgoing).reshape(owners_count * capacity, TILE, LANES)
        total = first_sums([(asked, arrived)], block)
        final = [(beside(asked), beside(arrived))]

    return halve(*last_sums(final, total, rows))[:, None, :]


def solution(mesh):
    placed = (
        P(None, "mdl", None),
        P(("grp", "mdl"), None, None, None),
        P(("grp", "mdl"), None, None, None),
        P(("grp", "mdl"), None, None),
        P(("grp", "mdl"), None),
        P(("grp", "mdl"), None),
    )

    return jax.shard_map(
        per_device, mesh=mesh, in_specs=placed, out_specs=P("grp", "mdl", None), check_vma=False
    )
```

```python
import functools

import jax
import jax.numpy as jnp
from jax import lax
from jax.experimental import pallas as pl
from jax.experimental.pallas import tpu as pltpu
from jax.sharding import PartitionSpec as P


LY = 64
LZ = 8
STEPS_FWD = 4
STEPS_ADJ = 4
TILE = 32
LANES = 128
SUB = 8
PARTS = TILE // SUB

AIR = 0.05
OMEGA = 0.5
BETA = 0.5

HALVES = LANES // LY
PACKED = TILE // SUB * HALVES

VMEM = pl.BlockSpec(memory_space=pltpu.VMEM)
SMEM = pl.BlockSpec(memory_space=pltpu.SMEM)
LIMIT = 16 << 20

EARTH = LZ * TILE * 3 // 4
PADDED = EARTH + TILE


def call(body, out, in_specs, work, moved, **kwargs):
    return pl.pallas_call(
        body,
        out_shape=out,
        in_specs=in_specs,
        out_specs=jax.tree.map(lambda _: VMEM, out),
        compiler_params=pltpu.CompilerParams(vmem_limit_bytes=LIMIT),
        cost_estimate=pl.CostEstimate(flops=work, bytes_accessed=moved, transcendentals=0),
        **kwargs,
    )


def floats(*shape):
    return jax.ShapeDtypeStruct(shape, jnp.float32)


def place_slots(owner_flat, owners_count, capacity):
    chosen = (owner_flat[:, None] == jnp.arange(owners_count, dtype=jnp.int32)[None, :]).astype(
        jnp.int32
    )
    before = jnp.cumsum(chosen, axis=0) - chosen
    return owner_flat * capacity + jnp.sum(before * chosen, axis=1)


def swap_over(axis, mask):
    ring = [(i, i ^ mask) for i in range(lax.axis_size(axis))]
    return lambda value: lax.ppermute(value, axis, ring)


def gather_body(starts_ref, block_ref, out_ref):
    wide = starts_ref.shape[1]
    for tile in range(out_ref.shape[0]):
        start = starts_ref[tile // wide, tile % wide]
        out_ref[tile] = block_ref[pl.ds(start, TILE), :]


def gather_rows(starts, block):
    out = floats(starts.size, TILE, LANES)
    return call(gather_body, out, [SMEM, VMEM], 0, 8 * out.size)(starts, block)


def earth_gather_body(index_ref, block_ref, out_ref, padded):
    count = index_ref.shape[0] // 2
    for sounding in range(count):
        place = sounding * PADDED
        for z in range(LZ):
            rows = block_ref[pl.ds(index_ref[sounding, z], TILE), :]
            padded[pl.ds(place, TILE), :] = rows
            place += index_ref[count + sounding, z]
    unpad(padded, out_ref, count)


def unpad(padded, out_ref, count):
    for sounding in range(count):
        begin, first = sounding * EARTH, sounding * PADDED
        out_ref[begin : begin + EARTH, :] = padded[first : first + EARTH, :]


def pad_end(rows_ref, padded):
    count = rows_ref.shape[0]
    padded[:count, :] = rows_ref[...]
    padded[count:, :] = jnp.zeros((TILE, LANES), jnp.float32)


def padded_rows(count):
    return pltpu.VMEM((count, LANES), jnp.float32)


def gather_earth(index, block):
    count = index.shape[0] // 2
    out = floats(count * EARTH, LANES)
    return call(
        earth_gather_body, out, [SMEM, VMEM], 0, 8 * out.size,
        scratch_shapes=[padded_rows(count * PADDED)],
    )(index, block)


def low_half():
    return lax.broadcasted_iota(jnp.int32, (SUB, LANES), 1) < LY


def pack(first, second, low):
    even = jnp.where(low, first, pltpu.roll(second, LY, 1))
    odd = jnp.where(low, pltpu.roll(first, LY, 1), second)
    return even, odd


def rows_of(ref, base, step):
    return ref[pl.ds(base, SUB, stride=step * PARTS), :]


def prepare_body(source_ref, observed_ref, source_out, observed_out):
    low = low_half()
    for ref, out in ((source_ref, source_out), (observed_ref, observed_out)):
        for part in range(3):
            for z in range(LZ):
                for j in range(PARTS):
                    base = part * LZ * TILE + z + LZ * j
                    first = rows_of(ref, base, LZ)
                    second = rows_of(ref, base + 3 * LZ * TILE, LZ)
                    out[part, z, 2 * j], out[part, z, 2 * j + 1] = pack(first, second, low)


def by_rows(values):
    count = values.shape[0]
    parts = values.reshape(count, 3, LZ, TILE, LANES)
    return parts.transpose(0, 1, 3, 2, 4).reshape(count * 3 * TILE * LZ, LANES)


def prepare(source, observed):
    out = floats(3, LZ, PACKED, SUB, LANES)
    return call(
        prepare_body, (out, out), [VMEM, VMEM], 8 * source.size, 16 * source.size
    )(by_rows(source), by_rows(observed))


def fields_body(
    packed, starts_ref, owners_ref, lengths_ref, table_ref, answer_ref, source_ref, observed_ref, kept_ref,
    given_ref, field, adjoint, right, curl, scale, decay, weight, sent_rows, given_rows,
):
    me = lax.axis_index("mdl")
    lane = lax.broadcasted_iota(jnp.int32, (SUB, LANES), 1)
    sub = lax.broadcasted_iota(jnp.int32, (SUB, LANES), 0)
    low = low_half()
    not_last = lane % LY != LY - 1
    not_first = lane % LY != 0
    top, bottom = sub != 0, sub != SUB - 1
    zero = jnp.zeros((SUB, LANES), jnp.float32)

    def y_next(value):
        return jnp.where(not_last, pltpu.roll(value, LANES - 1, 1), 0.0)

    def y_prev(value):
        return jnp.where(not_first, pltpu.roll(value, 1, 1), 0.0)

    def x_next(ref, part, z, k):
        if k + 1 < PACKED:
            return ref[part, z, k + 1]
        return jnp.where(bottom, pltpu.roll(ref[part, z, 0], SUB - 1, 0), 0.0)

    def x_prev(ref, part, z, k):
        if k > 0:
            return ref[part, z, k - 1]
        return jnp.where(top, pltpu.roll(ref[part, z, PACKED - 1], 1, 0), 0.0)

    def sweep(state):
        for z in range(LZ):
            for k in range(PACKED):
                east, north, vert = state[0, z, k], state[1, z, k], state[2, z, k]
                east_d = state[0, z + 1, k] if z + 1 < LZ else zero
                north_d = state[1, z + 1, k] if z + 1 < LZ else zero
                curl[0, z, k] = (y_next(vert) - vert) - (north_d - north)
                curl[1, z, k] = (east_d - east) - (x_next(state, 2, z, k) - vert)
                curl[2, z, k] = (x_next(state, 1, z, k) - north) - (y_next(east) - east)
            for k in range(PACKED):
                curl_x, curl_y, curl_z = curl[0, z, k], curl[1, z, k], curl[2, z, k]
                up_x = curl[0, z - 1, k] if z else zero
                up_y = curl[1, z - 1, k] if z else zero
                back_x = (up_y - curl_y) - (y_prev(curl_z) - curl_z)
                back_y = (x_prev(curl, 2, z, k) - curl_z) - (up_x - curl_x)
                back_z = (y_prev(curl_x) - curl_x) - (x_prev(curl, 1, z, k) - curl_y)
                s, d = scale[z, k], decay[z, k]
                state[0, z, k] = d * state[0, z, k] + (right[0, z, k] - s * back_x)
                state[1, z, k] = d * state[1, z, k] + (right[1, z, k] - s * back_y)
                state[2, z, k] = d * state[2, z, k] + (right[2, z, k] - s * back_z)

    count = starts_ref.shape[0]
    sent_at, given_at = [], []
    for sounding in range(count):
        place = 0
        for z in range(LZ):
            tile = sounding * LZ + z
            sent_at.append(sounding * EARTH + place if packed else tile * TILE)
            given_at.append(sounding * PADDED + place if packed else tile * TILE)
            place += lengths_ref[sounding, z]
    if packed:
        pad_end(answer_ref, sent_rows)
    sent_from = sent_rows if packed else answer_ref
    given_to = given_rows if packed else given_ref

    for z in range(LZ):

        def layer(sounding, j):
            raw = rows_of(table_ref, starts_ref[sounding, z] + j, 1)
            sent = rows_of(sent_from, sent_at[sounding * LZ + z] + j, 1)
            mine = jnp.full((SUB, LANES), owners_ref[sounding, z] == me)
            return jnp.where(mine, raw, sent)

        length = jnp.where(low, lengths_ref[0, z], lengths_ref[1, z])
        for j in range(PARTS):
            earth = PARTS * sub + j < length
            for odd, logs in enumerate(pack(layer(0, j), layer(1, j), low)):
                k = 2 * j + odd
                conduct = jnp.where(earth, jnp.exp(logs), AIR)
                s = OMEGA / (4.0 + conduct)
                scale[z, k] = s
                decay[z, k] = 1.0 - s * conduct
                weight[z, k] = jnp.where(earth, -conduct, 0.0)
                for part in range(3):
                    value = s * source_ref[part, z, k]
                    right[part, z, k] = value
                    field[part, z, k] = value

    @pl.loop(0, STEPS_FWD - 1)
    def _(step):
        sweep(field)

    for z in range(LZ):
        for k in range(PACKED):
            for part in range(3):
                value = scale[z, k] * (field[part, z, k] - observed_ref[part, z, k])
                right[part, z, k] = value
                adjoint[part, z, k] = value

    @pl.loop(0, STEPS_ADJ - 1)
    def _(step):
        sweep(adjoint)

    for z in range(LZ):

        def partial(k):
            total = field[0, z, k] * adjoint[0, z, k]
            total += field[1, z, k] * adjoint[1, z, k]
            total += field[2, z, k] * adjoint[2, z, k]
            return weight[z, k] * total

        for j in range(PARTS):
            first, second = pack(partial(2 * j), partial(2 * j + 1), low)
            for sounding, value in enumerate((first, second)):
                mine = jnp.full((SUB, LANES), owners_ref[sounding, z] == me)
                tile = sounding * LZ + z
                kept_ref[pl.ds(tile * TILE + j, SUB, stride=PARTS), :] = jnp.where(mine, value, 0.0)
                place = pl.ds(given_at[tile] + j, SUB, stride=PARTS)
                given_to[place, :] = jnp.where(mine, 0.0, value)
    if packed:
        unpad(given_rows, given_ref, count)


def soundings_partial(starts, owners, lengths, table, answer, source, observed):
    count, tiles = starts.shape[0], starts.size
    packed = answer.shape[0] == count * EARTH
    planes = pltpu.VMEM((3, LZ, PACKED, SUB, LANES), jnp.float32)
    single = pltpu.VMEM((LZ, PACKED, SUB, LANES), jnp.float32)
    cells = tiles * TILE * LANES
    kept, given = call(
        functools.partial(fields_body, packed),
        (floats(tiles * TILE, LANES), floats(*answer.shape)),
        [SMEM] * 3 + [VMEM] * 4, 500 * cells, 40 * cells,
        scratch_shapes=[planes] * 4 + [single] * 3
        + [padded_rows(count * EARTH + TILE), padded_rows(count * PADDED)],
    )(starts, owners, lengths, table, answer, source, observed)
    return kept.reshape(tiles, TILE, LANES), given


def arranged(order):
    if not order:
        return [0]
    rest = arranged(order[1:])
    return [slot | (1 << order[0]) for slot in rest] + rest


def add_terms(index_ref, terms_ref, total, share, slots, padded):
    me = lax.axis_index("grp")
    packed = len(terms_ref.shape) == 2
    span, wide = share + 2 * TILE, index_ref.shape[1]
    tiles = terms_ref.shape[0] // EARTH * LZ if packed else terms_ref.shape[0]
    row = lax.broadcasted_iota(jnp.int32, (TILE, LANES), 0)
    if packed:
        pad_end(terms_ref, padded)
    for tile in range(tiles):
        start = index_ref[tile // wide, tile % wide]
        first = lax.div(start, share)
        target = first + ((first ^ me) & 1)
        where = start - target * share
        base = ((target >> 1) ^ (me >> 1)) * span + TILE + where
        base = jnp.where(where > -TILE, base, slots * span)
        if packed:
            place = tile // LZ * EARTH if tile % LZ == 0 else place + length
            length = index_ref[tiles // LZ + tile // LZ, tile % LZ]
            terms = jnp.where(row < length, padded[pl.ds(place, TILE), :], 0.0)
        else:
            terms = terms_ref[tile]
        total[pl.ds(base, TILE), :] += terms


def first_body(groups, count, *refs):
    model_ref, total = refs[2 * count], refs[-1]
    me = lax.axis_index("grp")
    share = model_ref.shape[0] // groups
    total[...] = jnp.zeros_like(total)
    local = model_ref[pl.ds(pl.multiple_of(me * share, share), share), :]
    lane = lax.broadcasted_iota(jnp.int32, local.shape, 1)
    left = jnp.where(lane == 0, local, pltpu.roll(local, 1, 1))
    right = jnp.where(lane == LANES - 1, local, pltpu.roll(local, LANES - 1, 1))
    total[TILE : TILE + share, :] = BETA * (2.0 * local - left - right)
    for i in range(count):
        add_terms(*refs[2 * i : 2 * i + 2], total, share, groups // 2, None)


def first_sums(groups_of, block):
    groups = lax.axis_size("grp")
    share = block.shape[0] // groups
    out = floats(groups // 2 * (share + 2 * TILE) + TILE, LANES)
    flat = [a for pair in groups_of for a in pair]
    return call(
        functools.partial(first_body, groups, len(groups_of)), out,
        [SMEM, VMEM] * len(groups_of) + [VMEM], out.size, 8 * out.size,
    )(*flat, block)


def low_rows(share):
    return max(1, share * 7 // 128) * SUB


def last_body(orders, groups, share, count, *refs):
    total, outs, padded = refs[2 * count + 1], refs[2 * count + 2 : -1], refs[-1]
    span, slots, half = share + 2 * TILE, groups // 2, low_rows(share)
    for i in range(count):
        add_terms(*refs[2 * i : 2 * i + 2], total, share, slots, padded)
    for which, order in enumerate(orders):
        for place, slot in enumerate(arranged(order)):
            out = outs[2 * which + (place * 2 >= slots)]
            begin = slot * span + TILE + which * half
            out[place % (slots // 2)] = total[begin : begin + out.shape[1], :]


def last_sums(groups_of, total, rows, orders):
    groups = lax.axis_size("grp")
    share, slots = rows // groups, groups // 2
    low, high = (floats(slots // 2, r, LANES) for r in (low_rows(share), share - low_rows(share)))
    terms_rows = max(a.shape[0] for _, a in groups_of)
    flat = [a for pair in groups_of for a in pair]
    count = len(groups_of)
    return call(
        functools.partial(last_body, orders, groups, share, count),
        (floats(*total.shape), low, low, high, high), [SMEM, VMEM] * count + [VMEM],
        total.size, 8 * total.size, input_output_aliases={2 * count: 0},
        scratch_shapes=[padded_rows(terms_rows + TILE)],
    )(*flat, total)[1:]


def join_body(got_low, low, got_high, high, give_ref, keep_ref):
    cut, split = low.shape[0] // 2, low.shape[1]
    for got, held, rows in ((got_low, low, slice(0, split)), (got_high, high, slice(split, None))):
        give_ref[:, rows] = got[:cut] + held[:cut]
        keep_ref[:, rows] = got[cut:] + held[cut:]


def finish_body(got, held, out_ref):
    out_ref[...] = got[0] + held[0]


def halve(low_give, low, high_give, high, orders):
    bit_pairs = list(zip(*orders))
    for step, (low_bit, high_bit) in enumerate(bit_pairs[:2]):
        got_low = swap_over("grp", 2 << low_bit)(low_give)
        got_high = swap_over("grp", 2 << high_bit)(high_give)
        cut = low.shape[0] // 2
        if step == 0:
            low_give, low = got_low[:cut] + low[:cut], got_low[cut:] + low[cut:]
            high_give, high = got_high[:cut] + high[:cut], got_high[cut:] + high[cut:]
    out = floats(cut, low.shape[1] + high.shape[1], LANES)
    give, keep = call(
        join_body, (out, out), [VMEM] * 4, low.size, 24 * low.size
    )(got_low, low, got_high, high)
    for bit, _ in bit_pairs[2:]:
        got = swap_over("grp", 2 << bit)(give)
        cut = keep.shape[0] // 2
        if cut:
            give, keep = got[:cut] + keep[:cut], got[cut:] + keep[cut:]
    return call(
        finish_body, floats(*keep.shape[1:]), [VMEM] * 2, keep.size, 12 * keep.size
    )(got, keep)


def hold_body(block_ref, out_ref, sem):
    copy = pltpu.make_async_copy(block_ref, out_ref, sem)
    copy.start()
    copy.wait()


def hold(block):
    return call(
        hold_body, floats(*block.shape), [pl.BlockSpec(memory_space=pltpu.HBM)], 0,
        8 * block.size, scratch_shapes=[pltpu.SemaphoreType.DMA],
    )(block)


def per_device(model, source, observed, owner_ids, offsets, lengths):
    rows, owners_count, groups = model.shape[0], lax.axis_size("mdl"), lax.axis_size("grp")
    tiles = source.shape[0] * LZ
    across, beside = swap_over("mdl", 1), swap_over("grp", 1)
    block = hold(model.reshape(rows, LANES))
    source, observed = prepare(source, observed)
    if owners_count == 2:
        asked = across(jnp.concatenate([offsets, lengths]))
        asked, block = lax.optimization_barrier((asked, block))
        given = gather_earth(asked, block)
        answer = across(given)
        told = beside(jnp.concatenate([offsets, asked]))
        answer, told = lax.optimization_barrier((answer, told))
        held = offsets.shape[0]
        kept, given = soundings_partial(
            offsets, owner_ids.reshape(offsets.shape), lengths, block, answer, source, observed
        )
        others = across(given)
        kept_beside = beside(kept)
        total = first_sums([(offsets, kept), (told[:held], kept_beside)], block)
        final = [(asked, others), (told[held:], beside(others))]
    else:
        capacity = max(4, 2 * tiles // owners_count)
        places = place_slots(owner_ids.reshape(tiles), owners_count, capacity)
        swap = functools.partial(
            lax.all_to_all, axis_name="mdl", split_axis=0, concat_axis=0, tiled=True
        )
        request = jnp.zeros((owners_count * capacity,), jnp.int32).at[places].set(
            offsets.reshape(tiles)
        )
        asked = swap(request.reshape(owners_count, capacity))
        given = gather_rows(asked, block).reshape(owners_count, capacity, TILE, LANES)
        fetched = swap(given).reshape(owners_count * capacity * TILE, LANES)
        terms, _ = soundings_partial(
            (places * TILE).reshape(offsets.shape), jnp.full_like(offsets, lax.axis_index("mdl")),
            lengths, fetched, jnp.zeros((tiles * TILE, LANES), jnp.float32), source, observed,
        )
        outgoing = jnp.zeros((owners_count * capacity, TILE, LANES), jnp.float32)
        outgoing = outgoing.at[places].set(terms).reshape(owners_count, capacity, TILE, LANES)
        arrived = swap(outgoing).reshape(owners_count * capacity, TILE, LANES)
        total = first_sums([(asked, arrived)], block)
        final = [(beside(asked), beside(arrived))]

    bits = tuple(range(groups.bit_length() - 2))
    orders = (bits, bits[1:2] + bits[0:1] + bits[2:])
    sums = halve(*last_sums(final, total, rows, orders), orders)
    return sums[:, None, :]


def solution(mesh):
    placed = (
        P(None, "mdl", None),
        P(("grp", "mdl"), None, None, None),
        P(("grp", "mdl"), None, None, None),
        P(("grp", "mdl"), None, None),
        P(("grp", "mdl"), None),
        P(("grp", "mdl"), None),
    )

    return jax.shard_map(
        per_device, mesh=mesh, in_specs=placed, out_specs=P("grp", "mdl", None), check_vma=False
    )
```

```python
import functools

import jax
import jax.numpy as jnp
from jax import lax
from jax.experimental import pallas as pl
from jax.experimental.pallas import tpu as pltpu
from jax.sharding import PartitionSpec as P


LY = 64
LZ = 8
STEPS_FWD = 4
STEPS_ADJ = 4
TILE = 32
LANES = 128
SUB = 8
PARTS = TILE // SUB

AIR = 0.05
OMEGA = 0.5
BETA = 0.5

HALVES = LANES // LY
PACKED = TILE // SUB * HALVES

VMEM = pl.BlockSpec(memory_space=pltpu.VMEM)
SMEM = pl.BlockSpec(memory_space=pltpu.SMEM)
LIMIT = 16 << 20

EARTH = LZ * TILE * 3 // 4
PADDED = EARTH + TILE


def call(body, out, in_specs, work, moved, **kwargs):
    return pl.pallas_call(
        body,
        out_shape=out,
        in_specs=in_specs,
        out_specs=jax.tree.map(lambda _: VMEM, out),
        compiler_params=pltpu.CompilerParams(vmem_limit_bytes=LIMIT),
        cost_estimate=pl.CostEstimate(flops=work, bytes_accessed=moved, transcendentals=0),
        **kwargs,
    )


def floats(*shape):
    return jax.ShapeDtypeStruct(shape, jnp.float32)


def place_slots(owner_flat, owners_count, capacity):
    chosen = (owner_flat[:, None] == jnp.arange(owners_count, dtype=jnp.int32)[None, :]).astype(
        jnp.int32
    )
    before = jnp.cumsum(chosen, axis=0) - chosen
    return owner_flat * capacity + jnp.sum(before * chosen, axis=1)


def swap_over(axis, mask):
    ring = [(i, i ^ mask) for i in range(lax.axis_size(axis))]
    return lambda value: lax.ppermute(value, axis, ring)


def gather_body(starts_ref, block_ref, out_ref):
    wide = starts_ref.shape[1]
    for tile in range(out_ref.shape[0]):
        start = starts_ref[tile // wide, tile % wide]
        out_ref[tile] = block_ref[pl.ds(start, TILE), :]


def gather_rows(starts, block):
    out = floats(starts.size, TILE, LANES)
    return call(gather_body, out, [SMEM, VMEM], 0, 8 * out.size)(starts, block)


def earth_gather_body(index_ref, block_ref, out_ref, padded):
    count = index_ref.shape[0] // 2
    for sounding in range(count):
        place = sounding * PADDED
        for z in range(LZ):
            rows = block_ref[pl.ds(index_ref[sounding, z], TILE), :]
            padded[pl.ds(place, TILE), :] = rows
            place += index_ref[count + sounding, z]
    unpad(padded, out_ref, count)


def unpad(padded, out_ref, count):
    for sounding in range(count):
        begin, first = sounding * EARTH, sounding * PADDED
        out_ref[begin : begin + EARTH, :] = padded[first : first + EARTH, :]


def pad_end(rows_ref, padded):
    count = rows_ref.shape[0]
    padded[:count, :] = rows_ref[...]
    padded[count:, :] = jnp.zeros((TILE, LANES), jnp.float32)


def padded_rows(count):
    return pltpu.VMEM((count, LANES), jnp.float32)


def gather_earth(index, block):
    count = index.shape[0] // 2
    out = floats(count * EARTH, LANES)
    return call(
        earth_gather_body, out, [SMEM, VMEM], 0, 8 * out.size,
        scratch_shapes=[padded_rows(count * PADDED)],
    )(index, block)


def low_half():
    return lax.broadcasted_iota(jnp.int32, (SUB, LANES), 1) < LY


def pack(first, second, low):
    even = jnp.where(low, first, pltpu.roll(second, LY, 1))
    odd = jnp.where(low, pltpu.roll(first, LY, 1), second)
    return even, odd


def rows_of(ref, base, step):
    return ref[pl.ds(base, SUB, stride=step * PARTS), :]


def prepare_body(source_ref, observed_ref, source_out, observed_out):
    low = low_half()
    for ref, out in ((source_ref, source_out), (observed_ref, observed_out)):
        for part in range(3):
            for z in range(LZ):
                for j in range(PARTS):
                    base = part * LZ * TILE + z + LZ * j
                    first = rows_of(ref, base, LZ)
                    second = rows_of(ref, base + 3 * LZ * TILE, LZ)
                    out[part, z, 2 * j], out[part, z, 2 * j + 1] = pack(first, second, low)


def by_rows(values):
    count = values.shape[0]
    parts = values.reshape(count, 3, LZ, TILE, LANES)
    return parts.transpose(0, 1, 3, 2, 4).reshape(count * 3 * TILE * LZ, LANES)


def prepare(source, observed):
    out = floats(3, LZ, PACKED, SUB, LANES)
    return call(
        prepare_body, (out, out), [VMEM, VMEM], 8 * source.size, 16 * source.size
    )(by_rows(source), by_rows(observed))


def fields_body(
    packed, starts_ref, owners_ref, lengths_ref, table_ref, answer_ref, source_ref, observed_ref, kept_ref,
    given_ref, field, adjoint, right, curl, scale, decay, weight, sent_rows, given_rows,
):
    me = lax.axis_index("mdl")
    lane = lax.broadcasted_iota(jnp.int32, (SUB, LANES), 1)
    sub = lax.broadcasted_iota(jnp.int32, (SUB, LANES), 0)
    low = low_half()
    not_last = lane % LY != LY - 1
    not_first = lane % LY != 0
    top, bottom = sub != 0, sub != SUB - 1
    zero = jnp.zeros((SUB, LANES), jnp.float32)

    def y_next(value):
        return jnp.where(not_last, pltpu.roll(value, LANES - 1, 1), 0.0)

    def y_prev(value):
        return jnp.where(not_first, pltpu.roll(value, 1, 1), 0.0)

    def x_next(ref, part, z, k):
        if k + 1 < PACKED:
            return ref[part, z, k + 1]
        return jnp.where(bottom, pltpu.roll(ref[part, z, 0], SUB - 1, 0), 0.0)

    def x_prev(ref, part, z, k):
        if k > 0:
            return ref[part, z, k - 1]
        return jnp.where(top, pltpu.roll(ref[part, z, PACKED - 1], 1, 0), 0.0)

    def sweep(state):
        for z in range(LZ):
            for k in range(PACKED):
                east, north, vert = state[0, z, k], state[1, z, k], state[2, z, k]
                east_d = state[0, z + 1, k] if z + 1 < LZ else zero
                north_d = state[1, z + 1, k] if z + 1 < LZ else zero
                curl[0, z, k] = (y_next(vert) - vert) - (north_d - north)
                curl[1, z, k] = (east_d - east) - (x_next(state, 2, z, k) - vert)
                curl[2, z, k] = (x_next(state, 1, z, k) - north) - (y_next(east) - east)
            for k in range(PACKED):
                curl_x, curl_y, curl_z = curl[0, z, k], curl[1, z, k], curl[2, z, k]
                up_x = curl[0, z - 1, k] if z else zero
                up_y = curl[1, z - 1, k] if z else zero
                back_x = (up_y - curl_y) - (y_prev(curl_z) - curl_z)
                back_y = (x_prev(curl, 2, z, k) - curl_z) - (up_x - curl_x)
                back_z = (y_prev(curl_x) - curl_x) - (x_prev(curl, 1, z, k) - curl_y)
                s, d = scale[z, k], decay[z, k]
                state[0, z, k] = d * state[0, z, k] + (right[0, z, k] - s * back_x)
                state[1, z, k] = d * state[1, z, k] + (right[1, z, k] - s * back_y)
                state[2, z, k] = d * state[2, z, k] + (right[2, z, k] - s * back_z)

    count = starts_ref.shape[0]
    sent_at, given_at = [], []
    for sounding in range(count):
        place = 0
        for z in range(LZ):
            tile = sounding * LZ + z
            sent_at.append(sounding * EARTH + place if packed else tile * TILE)
            given_at.append(sounding * PADDED + place if packed else tile * TILE)
            place += lengths_ref[sounding, z]
    if packed:
        pad_end(answer_ref, sent_rows)
    sent_from = sent_rows if packed else answer_ref
    given_to = given_rows if packed else given_ref

    for z in range(LZ):

        def layer(sounding, j):
            raw = rows_of(table_ref, starts_ref[sounding, z] + j, 1)
            sent = rows_of(sent_from, sent_at[sounding * LZ + z] + j, 1)
            mine = jnp.full((SUB, LANES), owners_ref[sounding, z] == me)
            return jnp.where(mine, raw, sent)

        length = jnp.where(low, lengths_ref[0, z], lengths_ref[1, z])
        for j in range(PARTS):
            earth = PARTS * sub + j < length
            for odd, logs in enumerate(pack(layer(0, j), layer(1, j), low)):
                k = 2 * j + odd
                conduct = jnp.where(earth, jnp.exp(logs), AIR)
                s = OMEGA / (4.0 + conduct)
                scale[z, k] = s
                decay[z, k] = 1.0 - s * conduct
                weight[z, k] = jnp.where(earth, -conduct, 0.0)
                for part in range(3):
                    value = s * source_ref[part, z, k]
                    right[part, z, k] = value
                    field[part, z, k] = value

    @pl.loop(0, STEPS_FWD - 1)
    def _(step):
        sweep(field)

    for z in range(LZ):
        for k in range(PACKED):
            for part in range(3):
                value = scale[z, k] * (field[part, z, k] - observed_ref[part, z, k])
                right[part, z, k] = value
                adjoint[part, z, k] = value

    @pl.loop(0, STEPS_ADJ - 1)
    def _(step):
        sweep(adjoint)

    for z in range(LZ):

        def partial(k):
            total = field[0, z, k] * adjoint[0, z, k]
            total += field[1, z, k] * adjoint[1, z, k]
            total += field[2, z, k] * adjoint[2, z, k]
            return weight[z, k] * total

        for j in range(PARTS):
            first, second = pack(partial(2 * j), partial(2 * j + 1), low)
            for sounding, value in enumerate((first, second)):
                mine = jnp.full((SUB, LANES), owners_ref[sounding, z] == me)
                tile = sounding * LZ + z
                kept_ref[pl.ds(tile * TILE + j, SUB, stride=PARTS), :] = jnp.where(mine, value, 0.0)
                place = pl.ds(given_at[tile] + j, SUB, stride=PARTS)
                given_to[place, :] = jnp.where(mine, 0.0, value)
    if packed:
        unpad(given_rows, given_ref, count)


def soundings_partial(starts, owners, lengths, table, answer, source, observed):
    count, tiles = starts.shape[0], starts.size
    packed = answer.shape[0] == count * EARTH
    planes = pltpu.VMEM((3, LZ, PACKED, SUB, LANES), jnp.float32)
    single = pltpu.VMEM((LZ, PACKED, SUB, LANES), jnp.float32)
    cells = tiles * TILE * LANES
    kept, given = call(
        functools.partial(fields_body, packed),
        (floats(tiles * TILE, LANES), floats(*answer.shape)),
        [SMEM] * 3 + [VMEM] * 4, 500 * cells, 40 * cells,
        scratch_shapes=[planes] * 4 + [single] * 3
        + [padded_rows(count * EARTH + TILE), padded_rows(count * PADDED)],
    )(starts, owners, lengths, table, answer, source, observed)
    return kept.reshape(tiles, TILE, LANES), given


def arranged(order):
    if not order:
        return [0]
    rest = arranged(order[1:])
    return [slot | (1 << order[0]) for slot in rest] + rest


def add_terms(index_ref, terms_ref, total, share, slots, padded):
    me = lax.axis_index("grp")
    packed = len(terms_ref.shape) == 2
    span, wide = share + 2 * TILE, index_ref.shape[1]
    tiles = terms_ref.shape[0] // EARTH * LZ if packed else terms_ref.shape[0]
    row = lax.broadcasted_iota(jnp.int32, (TILE, LANES), 0)
    if packed:
        pad_end(terms_ref, padded)
    for tile in range(tiles):
        start = index_ref[tile // wide, tile % wide]
        first = lax.div(start, share)
        target = first + ((first ^ me) & 1)
        where = start - target * share
        base = ((target >> 1) ^ (me >> 1)) * span + TILE + where
        base = jnp.where(where > -TILE, base, slots * span)
        if packed:
            place = tile // LZ * EARTH if tile % LZ == 0 else place + length
            length = index_ref[tiles // LZ + tile // LZ, tile % LZ]
            terms = jnp.where(row < length, padded[pl.ds(place, TILE), :], 0.0)
        else:
            terms = terms_ref[tile]
        total[pl.ds(base, TILE), :] += terms


def first_body(groups, count, *refs):
    model_ref, total = refs[2 * count], refs[-1]
    me = lax.axis_index("grp")
    share = model_ref.shape[0] // groups
    total[...] = jnp.zeros_like(total)
    local = model_ref[pl.ds(pl.multiple_of(me * share, share), share), :]
    lane = lax.broadcasted_iota(jnp.int32, local.shape, 1)
    left = jnp.where(lane == 0, local, pltpu.roll(local, 1, 1))
    right = jnp.where(lane == LANES - 1, local, pltpu.roll(local, LANES - 1, 1))
    total[TILE : TILE + share, :] = BETA * (2.0 * local - left - right)
    for i in range(count):
        add_terms(*refs[2 * i : 2 * i + 2], total, share, groups // 2, None)


def first_sums(groups_of, block):
    groups = lax.axis_size("grp")
    share = block.shape[0] // groups
    out = floats(groups // 2 * (share + 2 * TILE) + TILE, LANES)
    flat = [a for pair in groups_of for a in pair]
    return call(
        functools.partial(first_body, groups, len(groups_of)), out,
        [SMEM, VMEM] * len(groups_of) + [VMEM], out.size, 8 * out.size,
    )(*flat, block)


PIECES = 4


def last_body(orders, groups, share, count, *refs):
    total, outs, padded = refs[2 * count + 1], refs[2 * count + 2 : -1], refs[-1]
    span, slots, piece = share + 2 * TILE, groups // 2, share // PIECES
    for i in range(count):
        add_terms(*refs[2 * i : 2 * i + 2], total, share, slots, padded)
    for which in range(PIECES):
        for place, slot in enumerate(arranged(orders[which % 2])):
            out = outs[2 * which + (place * 2 >= slots)]
            begin = slot * span + TILE + which * piece
            out[place % (slots // 2)] = total[begin : begin + piece, :]


def last_sums(groups_of, total, rows, orders):
    groups = lax.axis_size("grp")
    share, slots = rows // groups, groups // 2
    out = floats(slots // 2, share // PIECES, LANES)
    flat = [a for pair in groups_of for a in pair]
    count = len(groups_of)
    terms_rows = max(a.shape[0] for _, a in groups_of)
    outs = call(
        functools.partial(last_body, orders, groups, share, count),
        (floats(*total.shape),) + (out,) * (2 * PIECES), [SMEM, VMEM] * count + [VMEM],
        total.size, 8 * total.size, input_output_aliases={2 * count: 0},
        scratch_shapes=[padded_rows(terms_rows + TILE)],
    )(*flat, total)[1:]
    return [outs[4 * i : 4 * i + 4] for i in range(PIECES // 2)]


def join_body(got_low, low, got_high, high, give_ref, keep_ref):
    cut, split = low.shape[0] // 2, low.shape[1]
    for got, held, rows in ((got_low, low, slice(0, split)), (got_high, high, slice(split, None))):
        give_ref[:, rows] = got[:cut] + held[:cut]
        keep_ref[:, rows] = got[cut:] + held[cut:]


def finish_body(*refs):
    out_ref = refs[-1]
    for i in range(0, len(refs) - 1, 2):
        got, held = refs[i : i + 2]
        rows = got.shape[1]
        out_ref[i // 2 * rows : (i // 2 + 1) * rows] = got[0] + held[0]


def halve(stages, orders):
    bit_pairs = list(zip(*orders))
    state = list(stages)
    for step, (low_bit, high_bit) in enumerate(bit_pairs[:2]):
        for i, (low_give, low, high_give, high) in enumerate(state):
            got_low = swap_over("grp", 2 << low_bit)(low_give)
            got_high = swap_over("grp", 2 << high_bit)(high_give)
            cut = low.shape[0] // 2
            if step == 0:
                low_give, low = got_low[:cut] + low[:cut], got_low[cut:] + low[cut:]
                high_give, high = got_high[:cut] + high[:cut], got_high[cut:] + high[cut:]
                state[i] = low_give, low, high_give, high
            else:
                out = floats(cut, low.shape[1] + high.shape[1], LANES)
                state[i] = call(
                    join_body, (out, out), [VMEM] * 4, low.size, 24 * low.size
                )(got_low, low, got_high, high)
    last = []
    for give, keep in state:
        for bit, _ in bit_pairs[2:]:
            got = swap_over("grp", 2 << bit)(give)
            cut = keep.shape[0] // 2
            if cut:
                give, keep = got[:cut] + keep[:cut], got[cut:] + keep[cut:]
        last += [got, keep]
    out = floats(sum(a.shape[1] for a in last) // 2, LANES)
    return call(finish_body, out, [VMEM] * len(last), out.size, 12 * out.size)(*last)


def hold_body(block_ref, out_ref, sem):
    copy = pltpu.make_async_copy(block_ref, out_ref, sem)
    copy.start()
    copy.wait()


def hold(block):
    return call(
        hold_body, floats(*block.shape), [pl.BlockSpec(memory_space=pltpu.HBM)], 0,
        8 * block.size, scratch_shapes=[pltpu.SemaphoreType.DMA],
    )(block)


def per_device(model, source, observed, owner_ids, offsets, lengths):
    rows, owners_count, groups = model.shape[0], lax.axis_size("mdl"), lax.axis_size("grp")
    tiles = source.shape[0] * LZ
    across, beside = swap_over("mdl", 1), swap_over("grp", 1)
    block = hold(model.reshape(rows, LANES))
    source, observed = prepare(source, observed)
    if owners_count == 2:
        asked = across(jnp.concatenate([offsets, lengths]))
        asked, block = lax.optimization_barrier((asked, block))
        given = gather_earth(asked, block)
        answer = across(given)
        told = beside(jnp.concatenate([offsets, asked]))
        answer, told = lax.optimization_barrier((answer, told))
        held = offsets.shape[0]
        kept, given = soundings_partial(
            offsets, owner_ids.reshape(offsets.shape), lengths, block, answer, source, observed
        )
        others = across(given)
        kept_beside = beside(kept)
        total = first_sums([(offsets, kept), (told[:held], kept_beside)], block)
        final = [(asked, others), (told[held:], beside(others))]
    else:
        capacity = max(4, 2 * tiles // owners_count)
        places = place_slots(owner_ids.reshape(tiles), owners_count, capacity)
        swap = functools.partial(
            lax.all_to_all, axis_name="mdl", split_axis=0, concat_axis=0, tiled=True
        )
        request = jnp.zeros((owners_count * capacity,), jnp.int32).at[places].set(
            offsets.reshape(tiles)
        )
        asked = swap(request.reshape(owners_count, capacity))
        given = gather_rows(asked, block).reshape(owners_count, capacity, TILE, LANES)
        fetched = swap(given).reshape(owners_count * capacity * TILE, LANES)
        terms, _ = soundings_partial(
            (places * TILE).reshape(offsets.shape), jnp.full_like(offsets, lax.axis_index("mdl")),
            lengths, fetched, jnp.zeros((tiles * TILE, LANES), jnp.float32), source, observed,
        )
        outgoing = jnp.zeros((owners_count * capacity, TILE, LANES), jnp.float32)
        outgoing = outgoing.at[places].set(terms).reshape(owners_count, capacity, TILE, LANES)
        arrived = swap(outgoing).reshape(owners_count * capacity, TILE, LANES)
        total = first_sums([(asked, arrived)], block)
        final = [(beside(asked), beside(arrived))]

    bits = tuple(range(groups.bit_length() - 2))
    orders = (bits, bits[1:2] + bits[0:1] + bits[2:])
    sums = halve(last_sums(final, total, rows, orders), orders)
    return sums[:, None, :]


def solution(mesh):
    placed = (
        P(None, "mdl", None),
        P(("grp", "mdl"), None, None, None),
        P(("grp", "mdl"), None, None, None),
        P(("grp", "mdl"), None, None),
        P(("grp", "mdl"), None),
        P(("grp", "mdl"), None),
    )

    return jax.shard_map(
        per_device, mesh=mesh, in_specs=placed, out_specs=P("grp", "mdl", None), check_vma=False
    )
```

```python
import functools

import jax
import jax.numpy as jnp
from jax import lax
from jax.experimental import pallas as pl
from jax.experimental.pallas import tpu as pltpu
from jax.sharding import PartitionSpec as P


LY = 64
LZ = 8
STEPS_FWD = 4
STEPS_ADJ = 4
TILE = 32
LANES = 128
SUB = 8
PARTS = TILE // SUB

AIR = 0.05
OMEGA = 0.5
BETA = 0.5

HALVES = LANES // LY
PACKED = TILE // SUB * HALVES

VMEM = pl.BlockSpec(memory_space=pltpu.VMEM)
SMEM = pl.BlockSpec(memory_space=pltpu.SMEM)
LIMIT = 16 << 20

EARTH = LZ * TILE * 3 // 4
PADDED = EARTH + TILE


def call(body, out, in_specs, work, moved, **kwargs):
    return pl.pallas_call(
        body,
        out_shape=out,
        in_specs=in_specs,
        out_specs=jax.tree.map(lambda _: VMEM, out),
        compiler_params=pltpu.CompilerParams(vmem_limit_bytes=LIMIT),
        cost_estimate=pl.CostEstimate(flops=work, bytes_accessed=moved, transcendentals=0),
        **kwargs,
    )


def floats(*shape):
    return jax.ShapeDtypeStruct(shape, jnp.float32)


def place_slots(owner_flat, owners_count, capacity):
    chosen = (owner_flat[:, None] == jnp.arange(owners_count, dtype=jnp.int32)[None, :]).astype(
        jnp.int32
    )
    before = jnp.cumsum(chosen, axis=0) - chosen
    return owner_flat * capacity + jnp.sum(before * chosen, axis=1)


def swap_over(axis, mask):
    ring = [(i, i ^ mask) for i in range(lax.axis_size(axis))]
    return lambda value: lax.ppermute(value, axis, ring)


def gather_body(starts_ref, block_ref, out_ref):
    wide = starts_ref.shape[1]
    for tile in range(out_ref.shape[0]):
        start = starts_ref[tile // wide, tile % wide]
        out_ref[tile] = block_ref[pl.ds(start, TILE), :]


def gather_rows(starts, block):
    out = floats(starts.size, TILE, LANES)
    return call(gather_body, out, [SMEM, VMEM], 0, 8 * out.size)(starts, block)


def earth_gather_body(index_ref, block_ref, out_ref, padded):
    count = index_ref.shape[0] // 2
    for sounding in range(count):
        place = sounding * PADDED
        for z in range(LZ):
            rows = block_ref[pl.ds(index_ref[sounding, z], TILE), :]
            padded[pl.ds(place, TILE), :] = rows
            place += index_ref[count + sounding, z]
    unpad(padded, out_ref, count)


def unpad(padded, out_ref, count):
    for sounding in range(count):
        begin, first = sounding * EARTH, sounding * PADDED
        out_ref[begin : begin + EARTH, :] = padded[first : first + EARTH, :]


def pad_end(rows_ref, padded):
    count = rows_ref.shape[0]
    padded[:count, :] = rows_ref[...]
    padded[count:, :] = jnp.zeros((TILE, LANES), jnp.float32)


def padded_rows(count):
    return pltpu.VMEM((count, LANES), jnp.float32)


def gather_earth(index, block):
    count = index.shape[0] // 2
    out = floats(count * EARTH, LANES)
    return call(
        earth_gather_body, out, [SMEM, VMEM], 0, 8 * out.size,
        scratch_shapes=[padded_rows(count * PADDED)],
    )(index, block)


def low_half():
    return lax.broadcasted_iota(jnp.int32, (SUB, LANES), 1) < LY


def pack(first, second, low):
    even = jnp.where(low, first, pltpu.roll(second, LY, 1))
    odd = jnp.where(low, pltpu.roll(first, LY, 1), second)
    return even, odd


def rows_of(ref, base, step):
    return ref[pl.ds(base, SUB, stride=step * PARTS), :]


def prepare_body(source_ref, observed_ref, source_out, observed_out):
    low = low_half()
    for ref, out in ((source_ref, source_out), (observed_ref, observed_out)):
        for part in range(3):
            for z in range(LZ):
                for j in range(PARTS):
                    base = part * LZ * TILE + z + LZ * j
                    first = rows_of(ref, base, LZ)
                    second = rows_of(ref, base + 3 * LZ * TILE, LZ)
                    out[part, z, 2 * j], out[part, z, 2 * j + 1] = pack(first, second, low)


def by_rows(values):
    count = values.shape[0]
    parts = values.reshape(count, 3, LZ, TILE, LANES)
    return parts.transpose(0, 1, 3, 2, 4).reshape(count * 3 * TILE * LZ, LANES)


def prepare(source, observed):
    out = floats(3, LZ, PACKED, SUB, LANES)
    return call(
        prepare_body, (out, out), [VMEM, VMEM], 8 * source.size, 16 * source.size
    )(by_rows(source), by_rows(observed))


def fields_body(
    packed, starts_ref, owners_ref, lengths_ref, table_ref, answer_ref, source_ref, observed_ref, kept_ref,
    given_ref, field, adjoint, right, curl, scale, decay, weight, sent_rows, given_rows,
):
    me = lax.axis_index("mdl")
    lane = lax.broadcasted_iota(jnp.int32, (SUB, LANES), 1)
    sub = lax.broadcasted_iota(jnp.int32, (SUB, LANES), 0)
    low = low_half()
    not_last = lane % LY != LY - 1
    not_first = lane % LY != 0
    top, bottom = sub != 0, sub != SUB - 1
    zero = jnp.zeros((SUB, LANES), jnp.float32)

    def y_next(value):
        return jnp.where(not_last, pltpu.roll(value, LANES - 1, 1), 0.0)

    def y_prev(value):
        return jnp.where(not_first, pltpu.roll(value, 1, 1), 0.0)

    def x_next(ref, part, z, k):
        if k + 1 < PACKED:
            return ref[part, z, k + 1]
        return jnp.where(bottom, pltpu.roll(ref[part, z, 0], SUB - 1, 0), 0.0)

    def sweep(state, start):
        above = None
        for z in range(LZ):
            curls = []
            for k in range(PACKED):
                east, north, vert = start[0, z, k], start[1, z, k], start[2, z, k]
                east_d = start[0, z + 1, k] if z + 1 < LZ else zero
                north_d = start[1, z + 1, k] if z + 1 < LZ else zero
                curls.append((
                    (y_next(vert) - vert) - (north_d - north),
                    (east_d - east) - (x_next(start, 2, z, k) - vert),
                    (x_next(start, 1, z, k) - north) - (y_next(east) - east),
                ))
            for k in range(PACKED):
                curl_x, curl_y, curl_z = curls[k]
                up_x, up_y = above[k][:2] if z else (zero, zero)
                if k:
                    before_y, before_z = curls[k - 1][1:]
                else:
                    before_y, before_z = (jnp.where(top, pltpu.roll(c, 1, 0), 0.0) for c in curls[-1][1:])
                back_x = (up_y - curl_y) - (y_prev(curl_z) - curl_z)
                back_y = (before_z - curl_z) - (up_x - curl_x)
                back_z = (y_prev(curl_x) - curl_x) - (before_y - curl_y)
                s, d = scale[z, k], decay[z, k]
                state[0, z, k] = d * start[0, z, k] + (right[0, z, k] - s * back_x)
                state[1, z, k] = d * start[1, z, k] + (right[1, z, k] - s * back_y)
                state[2, z, k] = d * start[2, z, k] + (right[2, z, k] - s * back_z)
            above = curls

    def relax(state, steps):
        sweep(state, right)

        @pl.loop(0, steps - 2)
        def _(step):
            sweep(state, state)

    count = starts_ref.shape[0]
    sent_at, given_at = [], []
    for sounding in range(count):
        place = 0
        for z in range(LZ):
            tile = sounding * LZ + z
            sent_at.append(sounding * EARTH + place if packed else tile * TILE)
            given_at.append(sounding * PADDED + place if packed else tile * TILE)
            place += lengths_ref[sounding, z]
    if packed:
        pad_end(answer_ref, sent_rows)
    sent_from = sent_rows if packed else answer_ref
    given_to = given_rows if packed else given_ref

    for z in range(LZ):

        def layer(sounding, j):
            raw = rows_of(table_ref, starts_ref[sounding, z] + j, 1)
            sent = rows_of(sent_from, sent_at[sounding * LZ + z] + j, 1)
            mine = jnp.full((SUB, LANES), owners_ref[sounding, z] == me)
            return jnp.where(mine, raw, sent)

        length = jnp.where(low, lengths_ref[0, z], lengths_ref[1, z])
        for j in range(PARTS):
            earth = PARTS * sub + j < length
            for odd, logs in enumerate(pack(layer(0, j), layer(1, j), low)):
                k = 2 * j + odd
                conduct = jnp.where(earth, jnp.exp(logs), AIR)
                s = OMEGA / (4.0 + conduct)
                scale[z, k] = s
                decay[z, k] = 1.0 - s * conduct
                weight[z, k] = jnp.where(earth, -conduct, 0.0)
                for part in range(3):
                    value = s * source_ref[part, z, k]
                    right[part, z, k] = value

    relax(field, STEPS_FWD)

    for z in range(LZ):
        for k in range(PACKED):
            for part in range(3):
                value = scale[z, k] * (field[part, z, k] - observed_ref[part, z, k])
                right[part, z, k] = value

    relax(adjoint, STEPS_ADJ)

    for z in range(LZ):

        def partial(k):
            total = field[0, z, k] * adjoint[0, z, k]
            total += field[1, z, k] * adjoint[1, z, k]
            total += field[2, z, k] * adjoint[2, z, k]
            return weight[z, k] * total

        for j in range(PARTS):
            first, second = pack(partial(2 * j), partial(2 * j + 1), low)
            for sounding, value in enumerate((first, second)):
                mine = jnp.full((SUB, LANES), owners_ref[sounding, z] == me)
                tile = sounding * LZ + z
                kept_ref[pl.ds(tile * TILE + j, SUB, stride=PARTS), :] = jnp.where(mine, value, 0.0)
                place = pl.ds(given_at[tile] + j, SUB, stride=PARTS)
                given_to[place, :] = jnp.where(mine, 0.0, value)
    if packed:
        unpad(given_rows, given_ref, count)


def soundings_partial(starts, owners, lengths, table, answer, source, observed):
    count, tiles = starts.shape[0], starts.size
    packed = answer.shape[0] == count * EARTH
    planes = pltpu.VMEM((3, LZ, PACKED, SUB, LANES), jnp.float32)
    single = pltpu.VMEM((LZ, PACKED, SUB, LANES), jnp.float32)
    cells = tiles * TILE * LANES
    kept, given = call(
        functools.partial(fields_body, packed),
        (floats(tiles * TILE, LANES), floats(*answer.shape)),
        [SMEM] * 3 + [VMEM] * 4, 500 * cells, 40 * cells,
        scratch_shapes=[planes] * 4 + [single] * 3
        + [padded_rows(count * EARTH + TILE), padded_rows(count * PADDED)],
    )(starts, owners, lengths, table, answer, source, observed)
    return kept.reshape(tiles, TILE, LANES), given


def arranged(order):
    if not order:
        return [0]
    rest = arranged(order[1:])
    return [slot | (1 << order[0]) for slot in rest] + rest


def add_terms(index_ref, terms_ref, total, share, slots, padded):
    me = lax.axis_index("grp")
    packed = len(terms_ref.shape) == 2
    span, wide = share + 2 * TILE, index_ref.shape[1]
    tiles = terms_ref.shape[0] // EARTH * LZ if packed else terms_ref.shape[0]
    row = lax.broadcasted_iota(jnp.int32, (TILE, LANES), 0)
    if packed:
        pad_end(terms_ref, padded)
    for tile in range(tiles):
        start = index_ref[tile // wide, tile % wide]
        first = lax.div(start, share)
        target = first + ((first ^ me) & 1)
        where = start - target * share
        base = ((target >> 1) ^ (me >> 1)) * span + TILE + where
        base = jnp.where(where > -TILE, base, slots * span)
        if packed:
            place = tile // LZ * EARTH if tile % LZ == 0 else place + length
            length = index_ref[tiles // LZ + tile // LZ, tile % LZ]
            terms = jnp.where(row < length, padded[pl.ds(place, TILE), :], 0.0)
        else:
            terms = terms_ref[tile]
        total[pl.ds(base, TILE), :] += terms


def first_body(groups, count, *refs):
    model_ref, total = refs[2 * count], refs[-1]
    me = lax.axis_index("grp")
    share = model_ref.shape[0] // groups
    total[...] = jnp.zeros_like(total)
    local = model_ref[pl.ds(pl.multiple_of(me * share, share), share), :]
    lane = lax.broadcasted_iota(jnp.int32, local.shape, 1)
    left = jnp.where(lane == 0, local, pltpu.roll(local, 1, 1))
    right = jnp.where(lane == LANES - 1, local, pltpu.roll(local, LANES - 1, 1))
    total[TILE : TILE + share, :] = BETA * (2.0 * local - left - right)
    for i in range(count):
        add_terms(*refs[2 * i : 2 * i + 2], total, share, groups // 2, None)


def first_sums(groups_of, block):
    groups = lax.axis_size("grp")
    share = block.shape[0] // groups
    out = floats(groups // 2 * (share + 2 * TILE) + TILE, LANES)
    flat = [a for pair in groups_of for a in pair]
    return call(
        functools.partial(first_body, groups, len(groups_of)), out,
        [SMEM, VMEM] * len(groups_of) + [VMEM], out.size, 8 * out.size,
    )(*flat, block)


def more_body(groups, share, index_ref, terms_ref, given_total, total, padded):
    add_terms(index_ref, terms_ref, total, share, groups // 2, padded)


def more_sums(index, terms, total, rows):
    groups = lax.axis_size("grp")
    return call(
        functools.partial(more_body, groups, rows // groups), floats(*total.shape),
        [SMEM, VMEM, VMEM], total.size, 8 * total.size, input_output_aliases={2: 0},
        scratch_shapes=[padded_rows(terms.shape[0] + TILE)],
    )(index, terms, total)


PIECES = 4


def last_body(orders, groups, share, count, *refs):
    total, outs, padded = refs[2 * count + 1], refs[2 * count + 2 : -1], refs[-1]
    span, slots, piece = share + 2 * TILE, groups // 2, share // PIECES
    for i in range(count):
        add_terms(*refs[2 * i : 2 * i + 2], total, share, slots, padded)
    for which in range(PIECES):
        for place, slot in enumerate(arranged(orders[which % 2])):
            out = outs[2 * which + (place * 2 >= slots)]
            begin = slot * span + TILE + which * piece
            out[place % (slots // 2)] = total[begin : begin + piece, :]


def last_sums(groups_of, total, rows, orders):
    groups = lax.axis_size("grp")
    share, slots = rows // groups, groups // 2
    out = floats(slots // 2, share // PIECES, LANES)
    flat = [a for pair in groups_of for a in pair]
    count = len(groups_of)
    terms_rows = max(a.shape[0] for _, a in groups_of)
    outs = call(
        functools.partial(last_body, orders, groups, share, count),
        (floats(*total.shape),) + (out,) * (2 * PIECES), [SMEM, VMEM] * count + [VMEM],
        total.size, 8 * total.size, input_output_aliases={2 * count: 0},
        scratch_shapes=[padded_rows(terms_rows + TILE)],
    )(*flat, total)[1:]
    return [outs[4 * i : 4 * i + 4] for i in range(PIECES // 2)]


def join_body(got_low, low, got_high, high, give_ref, keep_ref):
    cut, split = low.shape[0] // 2, low.shape[1]
    for got, held, rows in ((got_low, low, slice(0, split)), (got_high, high, slice(split, None))):
        give_ref[:, rows] = got[:cut] + held[:cut]
        keep_ref[:, rows] = got[cut:] + held[cut:]


def finish_body(*refs):
    out_ref = refs[-1]
    for i in range(0, len(refs) - 1, 2):
        got, held = refs[i : i + 2]
        rows = got.shape[1]
        out_ref[i // 2 * rows : (i // 2 + 1) * rows] = got[0] + held[0]


def halve(stages, orders):
    bit_pairs = list(zip(*orders))
    state = list(stages)
    for step, (low_bit, high_bit) in enumerate(bit_pairs[:2]):
        for i, (low_give, low, high_give, high) in enumerate(state):
            got_low = swap_over("grp", 2 << low_bit)(low_give)
            got_high = swap_over("grp", 2 << high_bit)(high_give)
            cut = low.shape[0] // 2
            if step == 0:
                low_give, low = got_low[:cut] + low[:cut], got_low[cut:] + low[cut:]
                high_give, high = got_high[:cut] + high[:cut], got_high[cut:] + high[cut:]
                state[i] = low_give, low, high_give, high
            else:
                out = floats(cut, low.shape[1] + high.shape[1], LANES)
                state[i] = call(
                    join_body, (out, out), [VMEM] * 4, low.size, 24 * low.size
                )(got_low, low, got_high, high)
    last = []
    for give, keep in state:
        for bit, _ in bit_pairs[2:]:
            got = swap_over("grp", 2 << bit)(give)
            cut = keep.shape[0] // 2
            if cut:
                give, keep = got[:cut] + keep[:cut], got[cut:] + keep[cut:]
        last += [got, keep]
    out = floats(sum(a.shape[1] for a in last) // 2, LANES)
    return call(finish_body, out, [VMEM] * len(last), out.size, 12 * out.size)(*last)


def hold_body(block_ref, out_ref, sem):
    copy = pltpu.make_async_copy(block_ref, out_ref, sem)
    copy.start()
    copy.wait()


def hold(block):
    return call(
        hold_body, floats(*block.shape), [pl.BlockSpec(memory_space=pltpu.HBM)], 0,
        8 * block.size, scratch_shapes=[pltpu.SemaphoreType.DMA],
    )(block)


def per_device(model, source, observed, owner_ids, offsets, lengths):
    rows, owners_count, groups = model.shape[0], lax.axis_size("mdl"), lax.axis_size("grp")
    tiles = source.shape[0] * LZ
    across, beside = swap_over("mdl", 1), swap_over("grp", 1)
    block = hold(model.reshape(rows, LANES))
    source, observed = prepare(source, observed)
    if owners_count == 2:
        asked = across(jnp.concatenate([offsets, lengths]))
        asked, block = lax.optimization_barrier((asked, block))
        given = gather_earth(asked, block)
        answer = across(given)
        told = beside(jnp.concatenate([offsets, asked]))
        answer, told = lax.optimization_barrier((answer, told))
        held = offsets.shape[0]
        kept, given = soundings_partial(
            offsets, owner_ids.reshape(offsets.shape), lengths, block, answer, source, observed
        )
        others = across(given)
        kept_beside = beside(kept)
        total = first_sums([(offsets, kept), (told[:held], kept_beside)], block)
        others_beside = beside(others)
        total = more_sums(asked, others, total, rows)
        final = [(told[held:], others_beside)]
    else:
        capacity = max(4, 2 * tiles // owners_count)
        places = place_slots(owner_ids.reshape(tiles), owners_count, capacity)
        swap = functools.partial(
            lax.all_to_all, axis_name="mdl", split_axis=0, concat_axis=0, tiled=True
        )
        request = jnp.zeros((owners_count * capacity,), jnp.int32).at[places].set(
            offsets.reshape(tiles)
        )
        asked = swap(request.reshape(owners_count, capacity))
        given = gather_rows(asked, block).reshape(owners_count, capacity, TILE, LANES)
        fetched = swap(given).reshape(owners_count * capacity * TILE, LANES)
        terms, _ = soundings_partial(
            (places * TILE).reshape(offsets.shape), jnp.full_like(offsets, lax.axis_index("mdl")),
            lengths, fetched, jnp.zeros((tiles * TILE, LANES), jnp.float32), source, observed,
        )
        outgoing = jnp.zeros((owners_count * capacity, TILE, LANES), jnp.float32)
        outgoing = outgoing.at[places].set(terms).reshape(owners_count, capacity, TILE, LANES)
        arrived = swap(outgoing).reshape(owners_count * capacity, TILE, LANES)
        total = first_sums([(asked, arrived)], block)
        final = [(beside(asked), beside(arrived))]

    bits = tuple(range(groups.bit_length() - 2))
    orders = (bits, bits[1:2] + bits[0:1] + bits[2:])
    sums = halve(last_sums(final, total, rows, orders), orders)
    return sums[:, None, :]


def solution(mesh):
    placed = (
        P(None, "mdl", None),
        P(("grp", "mdl"), None, None, None),
        P(("grp", "mdl"), None, None, None),
        P(("grp", "mdl"), None, None),
        P(("grp", "mdl"), None),
        P(("grp", "mdl"), None),
    )

    return jax.shard_map(
        per_device, mesh=mesh, in_specs=placed, out_specs=P("grp", "mdl", None), check_vma=False
    )
```

```python
import functools

import jax
import jax.numpy as jnp
from jax import lax
from jax.experimental import pallas as pl
from jax.experimental.pallas import tpu as pltpu
from jax.sharding import PartitionSpec as P


LY = 64
LZ = 8
STEPS_FWD = 4
STEPS_ADJ = 4
TILE = 32
LANES = 128
SUB = 8
PARTS = TILE // SUB

AIR = 0.05
OMEGA = 0.5
BETA = 0.5

HALVES = LANES // LY
PACKED = TILE // SUB * HALVES

VMEM = pl.BlockSpec(memory_space=pltpu.VMEM)
SMEM = pl.BlockSpec(memory_space=pltpu.SMEM)
LIMIT = 16 << 20

EARTH = LZ * TILE * 3 // 4
PADDED = EARTH + TILE


def call(body, out, in_specs, work, moved, **kwargs):
    return pl.pallas_call(
        body,
        out_shape=out,
        in_specs=in_specs,
        out_specs=jax.tree.map(lambda _: VMEM, out),
        compiler_params=pltpu.CompilerParams(vmem_limit_bytes=LIMIT),
        cost_estimate=pl.CostEstimate(flops=work, bytes_accessed=moved, transcendentals=0),
        **kwargs,
    )


def floats(*shape):
    return jax.ShapeDtypeStruct(shape, jnp.float32)


def place_slots(owner_flat, owners_count, capacity):
    chosen = (owner_flat[:, None] == jnp.arange(owners_count, dtype=jnp.int32)[None, :]).astype(
        jnp.int32
    )
    before = jnp.cumsum(chosen, axis=0) - chosen
    return owner_flat * capacity + jnp.sum(before * chosen, axis=1)


def swap_over(axis, mask):
    ring = [(i, i ^ mask) for i in range(lax.axis_size(axis))]
    return lambda value: lax.ppermute(value, axis, ring)


def gather_body(starts_ref, block_ref, out_ref):
    wide = starts_ref.shape[1]
    for tile in range(out_ref.shape[0]):
        start = starts_ref[tile // wide, tile % wide]
        out_ref[tile] = block_ref[pl.ds(start, TILE), :]


def gather_rows(starts, block):
    out = floats(starts.size, TILE, LANES)
    return call(gather_body, out, [SMEM, VMEM], 0, 8 * out.size)(starts, block)


def earth_gather_body(index_ref, block_ref, out_ref, padded):
    count = index_ref.shape[0] // 2
    for sounding in range(count):
        place = sounding * PADDED
        for z in range(LZ):
            rows = block_ref[pl.ds(index_ref[sounding, z], TILE), :]
            padded[pl.ds(place, TILE), :] = rows
            place += index_ref[count + sounding, z]
    unpad(padded, out_ref, count)


def unpad(padded, out_ref, count):
    for sounding in range(count):
        begin, first = sounding * EARTH, sounding * PADDED
        out_ref[begin : begin + EARTH, :] = padded[first : first + EARTH, :]


def pad_end(rows_ref, padded):
    count = rows_ref.shape[0]
    padded[:count, :] = rows_ref[...]
    padded[count:, :] = jnp.zeros((TILE, LANES), jnp.float32)


def padded_rows(count):
    return pltpu.VMEM((count, LANES), jnp.float32)


def gather_earth(index, block):
    count = index.shape[0] // 2
    out = floats(count * EARTH, LANES)
    return call(
        earth_gather_body, out, [SMEM, VMEM], 0, 8 * out.size,
        scratch_shapes=[padded_rows(count * PADDED)],
    )(index, block)


def low_half():
    return lax.broadcasted_iota(jnp.int32, (SUB, LANES), 1) < LY


def pack(first, second, low):
    even = jnp.where(low, first, pltpu.roll(second, LY, 1))
    odd = jnp.where(low, pltpu.roll(first, LY, 1), second)
    return even, odd


def rows_of(ref, base, step):
    return ref[pl.ds(base, SUB, stride=step * PARTS), :]


def prepare_body(source_ref, observed_ref, source_out, observed_out):
    low = low_half()
    for ref, out in ((source_ref, source_out), (observed_ref, observed_out)):
        for part in range(3):
            for z in range(LZ):
                for j in range(PARTS):
                    base = part * LZ * TILE + z + LZ * j
                    first = rows_of(ref, base, LZ)
                    second = rows_of(ref, base + 3 * LZ * TILE, LZ)
                    out[part, z, 2 * j], out[part, z, 2 * j + 1] = pack(first, second, low)


def by_rows(values):
    count = values.shape[0]
    parts = values.reshape(count, 3, LZ, TILE, LANES)
    return parts.transpose(0, 1, 3, 2, 4).reshape(count * 3 * TILE * LZ, LANES)


def prepare(source, observed):
    out = floats(3, LZ, PACKED, SUB, LANES)
    return call(
        prepare_body, (out, out), [VMEM, VMEM], 8 * source.size, 16 * source.size
    )(by_rows(source), by_rows(observed))


def fields_body(
    packed, starts_ref, owners_ref, lengths_ref, table_ref, answer_ref, source_ref, observed_ref, kept_ref,
    given_ref, field, adjoint, right, curl, scale, decay, weight, sent_rows, given_rows,
):
    me = lax.axis_index("mdl")
    lane = lax.broadcasted_iota(jnp.int32, (SUB, LANES), 1)
    sub = lax.broadcasted_iota(jnp.int32, (SUB, LANES), 0)
    low = low_half()
    not_last = lane % LY != LY - 1
    not_first = lane % LY != 0
    top, bottom = sub != 0, sub != SUB - 1
    zero = jnp.zeros((SUB, LANES), jnp.float32)

    def y_next(value):
        return jnp.where(not_last, pltpu.roll(value, LANES - 1, 1), 0.0)

    def y_prev(value):
        return jnp.where(not_first, pltpu.roll(value, 1, 1), 0.0)

    def x_next(ref, part, z, k):
        if k + 1 < PACKED:
            return ref[part, z, k + 1]
        return jnp.where(bottom, pltpu.roll(ref[part, z, 0], SUB - 1, 0), 0.0)

    def sweep(state, start):
        above = None
        for z in range(LZ):
            curls = []
            for k in range(PACKED):
                east, north, vert = start[0, z, k], start[1, z, k], start[2, z, k]
                east_d = start[0, z + 1, k] if z + 1 < LZ else zero
                north_d = start[1, z + 1, k] if z + 1 < LZ else zero
                curls.append((
                    (y_next(vert) - vert) - (north_d - north),
                    (east_d - east) - (x_next(start, 2, z, k) - vert),
                    (x_next(start, 1, z, k) - north) - (y_next(east) - east),
                ))
            for k in range(PACKED):
                curl_x, curl_y, curl_z = curls[k]
                up_x, up_y = above[k][:2] if z else (zero, zero)
                if k:
                    before_y, before_z = curls[k - 1][1:]
                else:
                    before_y, before_z = (jnp.where(top, pltpu.roll(c, 1, 0), 0.0) for c in curls[-1][1:])
                back_x = (up_y - curl_y) - (y_prev(curl_z) - curl_z)
                back_y = (before_z - curl_z) - (up_x - curl_x)
                back_z = (y_prev(curl_x) - curl_x) - (before_y - curl_y)
                s, d = scale[z, k], decay[z, k]
                state[0, z, k] = d * start[0, z, k] + (right[0, z, k] - s * back_x)
                state[1, z, k] = d * start[1, z, k] + (right[1, z, k] - s * back_y)
                state[2, z, k] = d * start[2, z, k] + (right[2, z, k] - s * back_z)
            above = curls

    def relax(state, steps):
        sweep(state, right)

        @pl.loop(0, steps - 2)
        def _(step):
            sweep(state, state)

    count = starts_ref.shape[0]
    sent_at, given_at = [], []
    for sounding in range(count):
        place = 0
        for z in range(LZ):
            tile = sounding * LZ + z
            sent_at.append(sounding * EARTH + place if packed else tile * TILE)
            given_at.append(sounding * PADDED + place if packed else tile * TILE)
            place += lengths_ref[sounding, z]
    if packed:
        pad_end(answer_ref, sent_rows)
    sent_from = sent_rows if packed else answer_ref
    given_to = given_rows if packed else given_ref

    for z in range(LZ):

        def layer(sounding, j):
            raw = rows_of(table_ref, starts_ref[sounding, z] + j, 1)
            sent = rows_of(sent_from, sent_at[sounding * LZ + z] + j, 1)
            mine = jnp.full((SUB, LANES), owners_ref[sounding, z] == me)
            return jnp.where(mine, raw, sent)

        length = jnp.where(low, lengths_ref[0, z], lengths_ref[1, z])
        for j in range(PARTS):
            earth = PARTS * sub + j < length
            for odd, logs in enumerate(pack(layer(0, j), layer(1, j), low)):
                k = 2 * j + odd
                conduct = jnp.where(earth, jnp.exp(logs), AIR)
                s = OMEGA / (4.0 + conduct)
                scale[z, k] = s
                decay[z, k] = 1.0 - s * conduct
                weight[z, k] = jnp.where(earth, -conduct, 0.0)
                for part in range(3):
                    value = s * source_ref[part, z, k]
                    right[part, z, k] = value

    relax(field, STEPS_FWD)

    for z in range(LZ):
        for k in range(PACKED):
            for part in range(3):
                value = scale[z, k] * (field[part, z, k] - observed_ref[part, z, k])
                right[part, z, k] = value

    relax(adjoint, STEPS_ADJ)

    for z in range(LZ):

        def partial(k):
            total = field[0, z, k] * adjoint[0, z, k]
            total += field[1, z, k] * adjoint[1, z, k]
            total += field[2, z, k] * adjoint[2, z, k]
            return weight[z, k] * total

        for j in range(PARTS):
            first, second = pack(partial(2 * j), partial(2 * j + 1), low)
            for sounding, value in enumerate((first, second)):
                mine = jnp.full((SUB, LANES), owners_ref[sounding, z] == me)
                tile = sounding * LZ + z
                kept_ref[pl.ds(tile * TILE + j, SUB, stride=PARTS), :] = jnp.where(mine, value, 0.0)
                place = pl.ds(given_at[tile] + j, SUB, stride=PARTS)
                given_to[place, :] = jnp.where(mine, 0.0, value)
    if packed:
        unpad(given_rows, given_ref, count)


def soundings_partial(starts, owners, lengths, table, answer, source, observed):
    count, tiles = starts.shape[0], starts.size
    packed = answer.shape[0] == count * EARTH
    planes = pltpu.VMEM((3, LZ, PACKED, SUB, LANES), jnp.float32)
    single = pltpu.VMEM((LZ, PACKED, SUB, LANES), jnp.float32)
    cells = tiles * TILE * LANES
    kept, given = call(
        functools.partial(fields_body, packed),
        (floats(tiles * TILE, LANES), floats(*answer.shape)),
        [SMEM] * 3 + [VMEM] * 4, 500 * cells, 40 * cells,
        scratch_shapes=[planes] * 4 + [single] * 3
        + [padded_rows(count * EARTH + TILE), padded_rows(count * PADDED)],
    )(starts, owners, lengths, table, answer, source, observed)
    return kept.reshape(tiles, TILE, LANES), given


def arranged(order):
    if not order:
        return [0]
    rest = arranged(order[1:])
    return [slot | (1 << order[0]) for slot in rest] + rest


def slot_of(target, me):
    far = (target >> 1) ^ (me >> 1)
    flip = (far ^ (far >> 1)) & (me & 1)
    return far ^ (flip | (flip << 1))


def add_terms(index_ref, terms_ref, total, share, slots, padded):
    me = lax.axis_index("grp")
    packed = len(terms_ref.shape) == 2
    span, wide = share + 2 * TILE, index_ref.shape[1]
    tiles = terms_ref.shape[0] // EARTH * LZ if packed else terms_ref.shape[0]
    row = lax.broadcasted_iota(jnp.int32, (TILE, LANES), 0)
    if packed:
        pad_end(terms_ref, padded)
    for tile in range(tiles):
        start = index_ref[tile // wide, tile % wide]
        first = lax.div(start, share)
        target = first + ((first ^ me) & 1)
        where = start - target * share
        base = slot_of(target, me) * span + TILE + where
        base = jnp.where(where > -TILE, base, slots * span)
        if packed:
            place = tile // LZ * EARTH if tile % LZ == 0 else place + length
            length = index_ref[tiles // LZ + tile // LZ, tile % LZ]
            terms = jnp.where(row < length, padded[pl.ds(place, TILE), :], 0.0)
        else:
            terms = terms_ref[tile]
        total[pl.ds(base, TILE), :] += terms


def first_body(groups, count, *refs):
    model_ref, total = refs[2 * count], refs[-1]
    me = lax.axis_index("grp")
    share = model_ref.shape[0] // groups
    total[...] = jnp.zeros_like(total)
    local = model_ref[pl.ds(pl.multiple_of(me * share, share), share), :]
    lane = lax.broadcasted_iota(jnp.int32, local.shape, 1)
    left = jnp.where(lane == 0, local, pltpu.roll(local, 1, 1))
    right = jnp.where(lane == LANES - 1, local, pltpu.roll(local, LANES - 1, 1))
    total[TILE : TILE + share, :] = BETA * (2.0 * local - left - right)
    for i in range(count):
        add_terms(*refs[2 * i : 2 * i + 2], total, share, groups // 2, None)


def first_sums(groups_of, block):
    groups = lax.axis_size("grp")
    share = block.shape[0] // groups
    out = floats(groups // 2 * (share + 2 * TILE) + TILE, LANES)
    flat = [a for pair in groups_of for a in pair]
    return call(
        functools.partial(first_body, groups, len(groups_of)), out,
        [SMEM, VMEM] * len(groups_of) + [VMEM], out.size, 8 * out.size,
    )(*flat, block)


def more_body(groups, share, index_ref, terms_ref, given_total, total, padded):
    add_terms(index_ref, terms_ref, total, share, groups // 2, padded)


def more_sums(index, terms, total, rows):
    groups = lax.axis_size("grp")
    return call(
        functools.partial(more_body, groups, rows // groups), floats(*total.shape),
        [SMEM, VMEM, VMEM], total.size, 8 * total.size, input_output_aliases={2: 0},
        scratch_shapes=[padded_rows(terms.shape[0] + TILE)],
    )(index, terms, total)


PIECES = 2


def last_body(groups, share, count, *refs):
    total, outs, padded = refs[2 * count + 1], refs[2 * count + 2 : -1], refs[-1]
    span, slots, piece = share + 2 * TILE, groups // 2, share // PIECES
    for i in range(count):
        add_terms(*refs[2 * i : 2 * i + 2], total, share, slots, padded)
    for which in range(PIECES):
        for place, slot in enumerate(arranged(tuple(range(slots.bit_length() - 1)))):
            out = outs[2 * which + (place * 2 >= slots)]
            begin = slot * span + TILE + which * piece
            out[place % (slots // 2)] = total[begin : begin + piece, :]


def last_sums(groups_of, total, rows):
    groups = lax.axis_size("grp")
    share, slots = rows // groups, groups // 2
    out = floats(slots // 2, share // PIECES, LANES)
    flat = [a for pair in groups_of for a in pair]
    count = len(groups_of)
    terms_rows = max(a.shape[0] for _, a in groups_of)
    outs = call(
        functools.partial(last_body, groups, share, count),
        (floats(*total.shape),) + (out,) * (2 * PIECES), [SMEM, VMEM] * count + [VMEM],
        total.size, 8 * total.size, input_output_aliases={2 * count: 0},
        scratch_shapes=[padded_rows(terms_rows + TILE)],
    )(*flat, total)[1:]
    return [outs[2 * i : 2 * i + 2] for i in range(PIECES)]


def finish_body(*refs):
    out_ref = refs[-1]
    for i in range(0, len(refs) - 1, 2):
        got, held = refs[i : i + 2]
        rows = got.shape[1]
        out_ref[i // 2 * rows : (i // 2 + 1) * rows] = got[0] + held[0]


def halve(stages):
    groups = lax.axis_size("grp")
    state, bits = list(stages), groups.bit_length() - 2
    for step in range(bits):
        other = 1 - step if step < 2 else step
        ring = [(i, i ^ (2 << (other if i & 1 else step))) for i in range(groups)]
        for i, (give, keep) in enumerate(state):
            got = lax.ppermute(give, "grp", ring)
            cut = keep.shape[0] // 2
            if step + 1 < bits:
                state[i] = got[:cut] + keep[:cut], got[cut:] + keep[cut:]
            else:
                state[i] = got, keep
    last = [a for pair in state for a in pair]
    out = floats(sum(a.shape[1] for a in last) // 2, LANES)
    return call(finish_body, out, [VMEM] * len(last), out.size, 12 * out.size)(*last)


def hold_body(block_ref, out_ref, sem):
    copy = pltpu.make_async_copy(block_ref, out_ref, sem)
    copy.start()
    copy.wait()


def hold(block):
    return call(
        hold_body, floats(*block.shape), [pl.BlockSpec(memory_space=pltpu.HBM)], 0,
        8 * block.size, scratch_shapes=[pltpu.SemaphoreType.DMA],
    )(block)


def per_device(model, source, observed, owner_ids, offsets, lengths):
    rows, owners_count = model.shape[0], lax.axis_size("mdl")
    tiles = source.shape[0] * LZ
    across, beside = swap_over("mdl", 1), swap_over("grp", 1)
    block = hold(model.reshape(rows, LANES))
    source, observed = prepare(source, observed)
    if owners_count == 2:
        asked = across(jnp.concatenate([offsets, lengths]))
        asked, block = lax.optimization_barrier((asked, block))
        given = gather_earth(asked, block)
        answer = across(given)
        told = beside(jnp.concatenate([offsets, asked]))
        answer, told = lax.optimization_barrier((answer, told))
        held = offsets.shape[0]
        kept, given = soundings_partial(
            offsets, owner_ids.reshape(offsets.shape), lengths, block, answer, source, observed
        )
        others = across(given)
        kept_beside = beside(kept)
        total = first_sums([(offsets, kept), (told[:held], kept_beside)], block)
        others_beside = beside(others)
        total = more_sums(asked, others, total, rows)
        final = [(told[held:], others_beside)]
    else:
        capacity = max(4, 2 * tiles // owners_count)
        places = place_slots(owner_ids.reshape(tiles), owners_count, capacity)
        swap = functools.partial(
            lax.all_to_all, axis_name="mdl", split_axis=0, concat_axis=0, tiled=True
        )
        request = jnp.zeros((owners_count * capacity,), jnp.int32).at[places].set(
            offsets.reshape(tiles)
        )
        asked = swap(request.reshape(owners_count, capacity))
        given = gather_rows(asked, block).reshape(owners_count, capacity, TILE, LANES)
        fetched = swap(given).reshape(owners_count * capacity * TILE, LANES)
        terms, _ = soundings_partial(
            (places * TILE).reshape(offsets.shape), jnp.full_like(offsets, lax.axis_index("mdl")),
            lengths, fetched, jnp.zeros((tiles * TILE, LANES), jnp.float32), source, observed,
        )
        outgoing = jnp.zeros((owners_count * capacity, TILE, LANES), jnp.float32)
        outgoing = outgoing.at[places].set(terms).reshape(owners_count, capacity, TILE, LANES)
        arrived = swap(outgoing).reshape(owners_count * capacity, TILE, LANES)
        total = first_sums([(asked, arrived)], block)
        final = [(beside(asked), beside(arrived))]

    return halve(last_sums(final, total, rows))[:, None, :]


def solution(mesh):
    placed = (
        P(None, "mdl", None),
        P(("grp", "mdl"), None, None, None),
        P(("grp", "mdl"), None, None, None),
        P(("grp", "mdl"), None, None),
        P(("grp", "mdl"), None),
        P(("grp", "mdl"), None),
    )

    return jax.shard_map(
        per_device, mesh=mesh, in_specs=placed, out_specs=P("grp", "mdl", None), check_vma=False
    )
```

```python
import functools

import jax
import jax.numpy as jnp
from jax import lax
from jax.experimental import pallas as pl
from jax.experimental.pallas import tpu as pltpu
from jax.sharding import PartitionSpec as P


LY = 64
LZ = 8
STEPS_FWD = 4
STEPS_ADJ = 4
TILE = 32
LANES = 128
SUB = 8
PARTS = TILE // SUB

AIR = 0.05
OMEGA = 0.5
BETA = 0.5

HALVES = LANES // LY
PACKED = TILE // SUB * HALVES

VMEM = pl.BlockSpec(memory_space=pltpu.VMEM)
SMEM = pl.BlockSpec(memory_space=pltpu.SMEM)
LIMIT = 16 << 20

EARTH = LZ * TILE * 3 // 4
PADDED = EARTH + TILE


def call(body, out, in_specs, work, moved, **kwargs):
    return pl.pallas_call(
        body,
        out_shape=out,
        in_specs=in_specs,
        out_specs=jax.tree.map(lambda _: VMEM, out),
        compiler_params=pltpu.CompilerParams(vmem_limit_bytes=LIMIT),
        cost_estimate=pl.CostEstimate(flops=work, bytes_accessed=moved, transcendentals=0),
        **kwargs,
    )


def floats(*shape):
    return jax.ShapeDtypeStruct(shape, jnp.float32)


def place_slots(owner_flat, owners_count, capacity):
    chosen = (owner_flat[:, None] == jnp.arange(owners_count, dtype=jnp.int32)[None, :]).astype(
        jnp.int32
    )
    before = jnp.cumsum(chosen, axis=0) - chosen
    return owner_flat * capacity + jnp.sum(before * chosen, axis=1)


def swap_over(axis, mask):
    ring = [(i, i ^ mask) for i in range(lax.axis_size(axis))]
    return lambda value: lax.ppermute(value, axis, ring)


def gather_body(starts_ref, block_ref, out_ref):
    wide = starts_ref.shape[1]
    for tile in range(out_ref.shape[0]):
        start = starts_ref[tile // wide, tile % wide]
        out_ref[tile] = block_ref[pl.ds(start, TILE), :]


def gather_rows(starts, block):
    out = floats(starts.size, TILE, LANES)
    return call(gather_body, out, [SMEM, VMEM], 0, 8 * out.size)(starts, block)


def earth_gather_body(index_ref, block_ref, out_ref, padded):
    count = index_ref.shape[0] // 2
    for sounding in range(count):
        place = sounding * PADDED
        for z in range(LZ):
            rows = block_ref[pl.ds(index_ref[sounding, z], TILE), :]
            padded[pl.ds(place, TILE), :] = rows
            place += index_ref[count + sounding, z]
    unpad(padded, out_ref, count)


def unpad(padded, out_ref, count):
    for sounding in range(count):
        begin, first = sounding * EARTH, sounding * PADDED
        out_ref[begin : begin + EARTH, :] = padded[first : first + EARTH, :]


def pad_end(rows_ref, padded):
    count = rows_ref.shape[0]
    padded[:count, :] = rows_ref[...]
    padded[count:, :] = jnp.zeros((TILE, LANES), jnp.float32)


def padded_rows(count):
    return pltpu.VMEM((count, LANES), jnp.float32)


def gather_earth(index, block):
    count = index.shape[0] // 2
    out = floats(count * EARTH, LANES)
    return call(
        earth_gather_body, out, [SMEM, VMEM], 0, 8 * out.size,
        scratch_shapes=[padded_rows(count * PADDED)],
    )(index, block)


def low_half():
    return lax.broadcasted_iota(jnp.int32, (SUB, LANES), 1) < LY


def pack(first, second, low):
    even = jnp.where(low, first, pltpu.roll(second, LY, 1))
    odd = jnp.where(low, pltpu.roll(first, LY, 1), second)
    return even, odd


def rows_of(ref, base, step):
    return ref[pl.ds(base, SUB, stride=step * PARTS), :]


def prepare_body(source_ref, observed_ref, source_out, observed_out):
    low = low_half()
    for ref, out in ((source_ref, source_out), (observed_ref, observed_out)):
        for part in range(3):
            for z in range(LZ):
                for j in range(PARTS):
                    base = part * LZ * TILE + z + LZ * j
                    first = rows_of(ref, base, LZ)
                    second = rows_of(ref, base + 3 * LZ * TILE, LZ)
                    out[part, z, 2 * j], out[part, z, 2 * j + 1] = pack(first, second, low)


def by_rows(values):
    count = values.shape[0]
    parts = values.reshape(count, 3, LZ, TILE, LANES)
    return parts.transpose(0, 1, 3, 2, 4).reshape(count * 3 * TILE * LZ, LANES)


def prepare(source, observed):
    out = floats(3, LZ, PACKED, SUB, LANES)
    return call(
        prepare_body, (out, out), [VMEM, VMEM], 8 * source.size, 16 * source.size
    )(by_rows(source), by_rows(observed))


def fields_body(
    packed, starts_ref, owners_ref, lengths_ref, table_ref, answer_ref, source_ref, observed_ref, kept_ref,
    given_ref, field, adjoint, right, curl, scale, decay, weight, sent_rows, given_rows,
):
    me = lax.axis_index("mdl")
    lane = lax.broadcasted_iota(jnp.int32, (SUB, LANES), 1)
    sub = lax.broadcasted_iota(jnp.int32, (SUB, LANES), 0)
    low = low_half()
    not_last = lane % LY != LY - 1
    not_first = lane % LY != 0
    top, bottom = sub != 0, sub != SUB - 1
    zero = jnp.zeros((SUB, LANES), jnp.float32)

    def y_next(value):
        return jnp.where(not_last, pltpu.roll(value, LANES - 1, 1), 0.0)

    def y_prev(value):
        return jnp.where(not_first, pltpu.roll(value, 1, 1), 0.0)

    def x_next(ref, part, z, k):
        if k + 1 < PACKED:
            return ref[part, z, k + 1]
        return jnp.where(bottom, pltpu.roll(ref[part, z, 0], SUB - 1, 0), 0.0)

    def sweep(state, start):
        above = None
        for z in range(LZ):
            curls = []
            for k in range(PACKED):
                east, north, vert = start[0, z, k], start[1, z, k], start[2, z, k]
                east_d = start[0, z + 1, k] if z + 1 < LZ else zero
                north_d = start[1, z + 1, k] if z + 1 < LZ else zero
                curls.append((
                    (y_next(vert) - vert) - (north_d - north),
                    (east_d - east) - (x_next(start, 2, z, k) - vert),
                    (x_next(start, 1, z, k) - north) - (y_next(east) - east),
                ))
            for k in range(PACKED):
                curl_x, curl_y, curl_z = curls[k]
                up_x, up_y = above[k][:2] if z else (zero, zero)
                if k:
                    before_y, before_z = curls[k - 1][1:]
                else:
                    before_y, before_z = (jnp.where(top, pltpu.roll(c, 1, 0), 0.0) for c in curls[-1][1:])
                back_x = (up_y - curl_y) - (y_prev(curl_z) - curl_z)
                back_y = (before_z - curl_z) - (up_x - curl_x)
                back_z = (y_prev(curl_x) - curl_x) - (before_y - curl_y)
                s, d = scale[z, k], decay[z, k]
                state[0, z, k] = d * start[0, z, k] + (right[0, z, k] - s * back_x)
                state[1, z, k] = d * start[1, z, k] + (right[1, z, k] - s * back_y)
                state[2, z, k] = d * start[2, z, k] + (right[2, z, k] - s * back_z)
            above = curls

    def relax(state, steps):
        sweep(state, right)

        @pl.loop(0, steps - 2)
        def _(step):
            sweep(state, state)

    count = starts_ref.shape[0]
    sent_at, given_at = [], []
    for sounding in range(count):
        place = 0
        for z in range(LZ):
            tile = sounding * LZ + z
            sent_at.append(sounding * EARTH + place if packed else tile * TILE)
            given_at.append(sounding * PADDED + place if packed else tile * TILE)
            place += lengths_ref[sounding, z]
    if packed:
        pad_end(answer_ref, sent_rows)
    sent_from = sent_rows if packed else answer_ref
    given_to = given_rows if packed else given_ref

    for z in range(LZ):

        def layer(sounding, j):
            raw = rows_of(table_ref, starts_ref[sounding, z] + j, 1)
            sent = rows_of(sent_from, sent_at[sounding * LZ + z] + j, 1)
            mine = jnp.full((SUB, LANES), owners_ref[sounding, z] == me)
            return jnp.where(mine, raw, sent)

        length = jnp.where(low, lengths_ref[0, z], lengths_ref[1, z])
        for j in range(PARTS):
            earth = PARTS * sub + j < length
            for odd, logs in enumerate(pack(layer(0, j), layer(1, j), low)):
                k = 2 * j + odd
                conduct = jnp.where(earth, jnp.exp(logs), AIR)
                s = OMEGA / (4.0 + conduct)
                scale[z, k] = s
                decay[z, k] = 1.0 - s * conduct
                weight[z, k] = jnp.where(earth, -conduct, 0.0)
                for part in range(3):
                    value = s * source_ref[part, z, k]
                    right[part, z, k] = value

    relax(field, STEPS_FWD)

    for z in range(LZ):
        for k in range(PACKED):
            for part in range(3):
                value = scale[z, k] * (field[part, z, k] - observed_ref[part, z, k])
                right[part, z, k] = value

    relax(adjoint, STEPS_ADJ)

    for z in range(LZ):

        def partial(k):
            total = field[0, z, k] * adjoint[0, z, k]
            total += field[1, z, k] * adjoint[1, z, k]
            total += field[2, z, k] * adjoint[2, z, k]
            return weight[z, k] * total

        for j in range(PARTS):
            first, second = pack(partial(2 * j), partial(2 * j + 1), low)
            for sounding, value in enumerate((first, second)):
                mine = jnp.full((SUB, LANES), owners_ref[sounding, z] == me)
                tile = sounding * LZ + z
                kept_ref[pl.ds(tile * TILE + j, SUB, stride=PARTS), :] = jnp.where(mine, value, 0.0)
                place = pl.ds(given_at[tile] + j, SUB, stride=PARTS)
                given_to[place, :] = jnp.where(mine, 0.0, value)
    if packed:
        unpad(given_rows, given_ref, count)


def soundings_partial(starts, owners, lengths, table, answer, source, observed):
    count, tiles = starts.shape[0], starts.size
    packed = answer.shape[0] == count * EARTH
    planes = pltpu.VMEM((3, LZ, PACKED, SUB, LANES), jnp.float32)
    single = pltpu.VMEM((LZ, PACKED, SUB, LANES), jnp.float32)
    cells = tiles * TILE * LANES
    kept, given = call(
        functools.partial(fields_body, packed),
        (floats(tiles * TILE, LANES), floats(*answer.shape)),
        [SMEM] * 3 + [VMEM] * 4, 500 * cells, 40 * cells,
        scratch_shapes=[planes] * 4 + [single] * 3
        + [padded_rows(count * EARTH + TILE), padded_rows(count * PADDED)],
    )(starts, owners, lengths, table, answer, source, observed)
    return kept.reshape(tiles, TILE, LANES), given


def arranged(order):
    if not order:
        return [0]
    rest = arranged(order[1:])
    return [slot | (1 << order[0]) for slot in rest] + rest


def add_terms(index_ref, terms_ref, total, share, slots, padded):
    me = lax.axis_index("grp")
    packed = len(terms_ref.shape) == 2
    span, wide = share + 2 * TILE, index_ref.shape[1]
    tiles = terms_ref.shape[0] // EARTH * LZ if packed else terms_ref.shape[0]
    row = lax.broadcasted_iota(jnp.int32, (TILE, LANES), 0)
    if packed:
        pad_end(terms_ref, padded)
    for tile in range(tiles):
        start = index_ref[tile // wide, tile % wide]
        first = lax.div(start, share)
        target = first + ((first ^ me) & 1)
        where = start - target * share
        base = ((target >> 1) ^ (me >> 1)) * span + TILE + where
        base = jnp.where(where > -TILE, base, slots * span)
        if packed:
            place = tile // LZ * EARTH if tile % LZ == 0 else place + length
            length = index_ref[tiles // LZ + tile // LZ, tile % LZ]
            terms = jnp.where(row < length, padded[pl.ds(place, TILE), :], 0.0)
        else:
            terms = terms_ref[tile]
        total[pl.ds(base, TILE), :] += terms


def first_body(groups, count, *refs):
    model_ref, total = refs[2 * count], refs[-1]
    me = lax.axis_index("grp")
    share = model_ref.shape[0] // groups
    total[...] = jnp.zeros_like(total)
    local = model_ref[pl.ds(pl.multiple_of(me * share, share), share), :]
    lane = lax.broadcasted_iota(jnp.int32, local.shape, 1)
    left = jnp.where(lane == 0, local, pltpu.roll(local, 1, 1))
    right = jnp.where(lane == LANES - 1, local, pltpu.roll(local, LANES - 1, 1))
    total[TILE : TILE + share, :] = BETA * (2.0 * local - left - right)
    for i in range(count):
        add_terms(*refs[2 * i : 2 * i + 2], total, share, groups // 2, None)


def first_sums(groups_of, block):
    groups = lax.axis_size("grp")
    share = block.shape[0] // groups
    out = floats(groups // 2 * (share + 2 * TILE) + TILE, LANES)
    flat = [a for pair in groups_of for a in pair]
    return call(
        functools.partial(first_body, groups, len(groups_of)), out,
        [SMEM, VMEM] * len(groups_of) + [VMEM], out.size, 8 * out.size,
    )(*flat, block)


def more_body(groups, share, index_ref, terms_ref, given_total, total, padded):
    add_terms(index_ref, terms_ref, total, share, groups // 2, padded)


def more_sums(index, terms, total, rows):
    groups = lax.axis_size("grp")
    return call(
        functools.partial(more_body, groups, rows // groups), floats(*total.shape),
        [SMEM, VMEM, VMEM], total.size, 8 * total.size, input_output_aliases={2: 0},
        scratch_shapes=[padded_rows(terms.shape[0] + TILE)],
    )(index, terms, total)


PIECES = 4


def piece_rows(share):
    few = max(1, share * 7 // 256) * SUB
    many = share // 2 - few
    return (many, many, few, few)


def last_body(orders, groups, share, count, *refs):
    total, outs, padded = refs[2 * count + 1], refs[2 * count + 2 : -1], refs[-1]
    span, slots = share + 2 * TILE, groups // 2
    for i in range(count):
        add_terms(*refs[2 * i : 2 * i + 2], total, share, slots, padded)
    for which in range(PIECES):
        for place, slot in enumerate(arranged(orders[which % 2])):
            out = outs[2 * which + (place * 2 >= slots)]
            begin = slot * span + TILE + sum(piece_rows(share)[:which])
            out[place % (slots // 2)] = total[begin : begin + out.shape[1], :]


def last_sums(groups_of, total, rows, orders):
    groups = lax.axis_size("grp")
    share, slots = rows // groups, groups // 2
    out = tuple(floats(slots // 2, r, LANES) for r in piece_rows(share) for _ in range(2))
    flat = [a for pair in groups_of for a in pair]
    count = len(groups_of)
    terms_rows = max(a.shape[0] for _, a in groups_of)
    outs = call(
        functools.partial(last_body, orders, groups, share, count),
        (floats(*total.shape),) + out, [SMEM, VMEM] * count + [VMEM],
        total.size, 8 * total.size, input_output_aliases={2 * count: 0},
        scratch_shapes=[padded_rows(terms_rows + TILE)],
    )(*flat, total)[1:]
    return [outs[4 * i : 4 * i + 4] for i in range(PIECES // 2)]


def join_body(got_low, low, got_high, high, give_ref, keep_ref):
    cut, split = low.shape[0] // 2, low.shape[1]
    for got, held, rows in ((got_low, low, slice(0, split)), (got_high, high, slice(split, None))):
        give_ref[:, rows] = got[:cut] + held[:cut]
        keep_ref[:, rows] = got[cut:] + held[cut:]


def finish_body(*refs):
    out_ref, begin = refs[-1], 0
    for i in range(0, len(refs) - 1, 2):
        got, held = refs[i : i + 2]
        rows = got.shape[1]
        out_ref[begin : begin + rows] = got[0] + held[0]
        begin += rows


def halve(stages, orders):
    bit_pairs = list(zip(*orders))
    state = list(stages)
    for step, (low_bit, high_bit) in enumerate(bit_pairs[:2]):
        for i, (low_give, low, high_give, high) in enumerate(state):
            got_low = swap_over("grp", 2 << low_bit)(low_give)
            got_high = swap_over("grp", 2 << high_bit)(high_give)
            cut = low.shape[0] // 2
            if step == 0:
                low_give, low = got_low[:cut] + low[:cut], got_low[cut:] + low[cut:]
                high_give, high = got_high[:cut] + high[:cut], got_high[cut:] + high[cut:]
                state[i] = low_give, low, high_give, high
            else:
                out = floats(cut, low.shape[1] + high.shape[1], LANES)
                state[i] = call(
                    join_body, (out, out), [VMEM] * 4, low.size, 24 * low.size
                )(got_low, low, got_high, high)
    last = []
    for give, keep in state:
        for bit, _ in bit_pairs[2:]:
            got = swap_over("grp", 2 << bit)(give)
            cut = keep.shape[0] // 2
            if cut:
                give, keep = got[:cut] + keep[:cut], got[cut:] + keep[cut:]
        last += [got, keep]
    out = floats(sum(a.shape[1] for a in last) // 2, LANES)
    return call(finish_body, out, [VMEM] * len(last), out.size, 12 * out.size)(*last)


def hold_body(block_ref, out_ref, sem):
    copy = pltpu.make_async_copy(block_ref, out_ref, sem)
    copy.start()
    copy.wait()


def hold(block):
    return call(
        hold_body, floats(*block.shape), [pl.BlockSpec(memory_space=pltpu.HBM)], 0,
        8 * block.size, scratch_shapes=[pltpu.SemaphoreType.DMA],
    )(block)


def per_device(model, source, observed, owner_ids, offsets, lengths):
    rows, owners_count, groups = model.shape[0], lax.axis_size("mdl"), lax.axis_size("grp")
    tiles = source.shape[0] * LZ
    across, beside = swap_over("mdl", 1), swap_over("grp", 1)
    block = hold(model.reshape(rows, LANES))
    source, observed = prepare(source, observed)
    if owners_count == 2:
        asked = across(jnp.concatenate([offsets, lengths]))
        asked, block = lax.optimization_barrier((asked, block))
        given = gather_earth(asked, block)
        answer = across(given)
        told = beside(jnp.concatenate([offsets, asked]))
        answer, told = lax.optimization_barrier((answer, told))
        held = offsets.shape[0]
        kept, given = soundings_partial(
            offsets, owner_ids.reshape(offsets.shape), lengths, block, answer, source, observed
        )
        others = across(given)
        kept_beside = beside(kept)
        total = first_sums([(offsets, kept), (told[:held], kept_beside)], block)
        others_beside = beside(others)
        total = more_sums(asked, others, total, rows)
        final = [(told[held:], others_beside)]
    else:
        capacity = max(4, 2 * tiles // owners_count)
        places = place_slots(owner_ids.reshape(tiles), owners_count, capacity)
        swap = functools.partial(
            lax.all_to_all, axis_name="mdl", split_axis=0, concat_axis=0, tiled=True
        )
        request = jnp.zeros((owners_count * capacity,), jnp.int32).at[places].set(
            offsets.reshape(tiles)
        )
        asked = swap(request.reshape(owners_count, capacity))
        given = gather_rows(asked, block).reshape(owners_count, capacity, TILE, LANES)
        fetched = swap(given).reshape(owners_count * capacity * TILE, LANES)
        terms, _ = soundings_partial(
            (places * TILE).reshape(offsets.shape), jnp.full_like(offsets, lax.axis_index("mdl")),
            lengths, fetched, jnp.zeros((tiles * TILE, LANES), jnp.float32), source, observed,
        )
        outgoing = jnp.zeros((owners_count * capacity, TILE, LANES), jnp.float32)
        outgoing = outgoing.at[places].set(terms).reshape(owners_count, capacity, TILE, LANES)
        arrived = swap(outgoing).reshape(owners_count * capacity, TILE, LANES)
        total = first_sums([(asked, arrived)], block)
        final = [(beside(asked), beside(arrived))]

    bits = tuple(range(groups.bit_length() - 2))
    orders = (bits, bits[1:2] + bits[0:1] + bits[2:])
    sums = halve(last_sums(final, total, rows, orders), orders)
    return sums[:, None, :]


def solution(mesh):
    placed = (
        P(None, "mdl", None),
        P(("grp", "mdl"), None, None, None),
        P(("grp", "mdl"), None, None, None),
        P(("grp", "mdl"), None, None),
        P(("grp", "mdl"), None),
        P(("grp", "mdl"), None),
    )

    return jax.shard_map(
        per_device, mesh=mesh, in_specs=placed, out_specs=P("grp", "mdl", None), check_vma=False
    )
```

```python
import functools

import jax
import jax.numpy as jnp
from jax import lax
from jax.experimental import pallas as pl
from jax.experimental.pallas import tpu as pltpu
from jax.sharding import PartitionSpec as P


LY = 64
LZ = 8
STEPS_FWD = 4
STEPS_ADJ = 4
TILE = 32
LANES = 128
SUB = 8
PARTS = TILE // SUB

AIR = 0.05
OMEGA = 0.5
BETA = 0.5

HALVES = LANES // LY
PACKED = TILE // SUB * HALVES

VMEM = pl.BlockSpec(memory_space=pltpu.VMEM)
SMEM = pl.BlockSpec(memory_space=pltpu.SMEM)
LIMIT = 16 << 20

EARTH = LZ * TILE * 3 // 4
PADDED = EARTH + TILE


def call(body, out, in_specs, work, moved, **kwargs):
    return pl.pallas_call(
        body,
        out_shape=out,
        in_specs=in_specs,
        out_specs=jax.tree.map(lambda _: VMEM, out),
        compiler_params=pltpu.CompilerParams(vmem_limit_bytes=LIMIT),
        cost_estimate=pl.CostEstimate(flops=work, bytes_accessed=moved, transcendentals=0),
        **kwargs,
    )


def floats(*shape):
    return jax.ShapeDtypeStruct(shape, jnp.float32)


def place_slots(owner_flat, owners_count, capacity):
    chosen = (owner_flat[:, None] == jnp.arange(owners_count, dtype=jnp.int32)[None, :]).astype(
        jnp.int32
    )
    before = jnp.cumsum(chosen, axis=0) - chosen
    return owner_flat * capacity + jnp.sum(before * chosen, axis=1)


def swap_over(axis, mask):
    ring = [(i, i ^ mask) for i in range(lax.axis_size(axis))]
    return lambda value: lax.ppermute(value, axis, ring)


def gather_body(starts_ref, block_ref, out_ref):
    wide = starts_ref.shape[1]
    for tile in range(out_ref.shape[0]):
        start = starts_ref[tile // wide, tile % wide]
        out_ref[tile] = block_ref[pl.ds(start, TILE), :]


def gather_rows(starts, block):
    out = floats(starts.size, TILE, LANES)
    return call(gather_body, out, [SMEM, VMEM], 0, 8 * out.size)(starts, block)


def earth_gather_body(index_ref, block_ref, out_ref, padded):
    count = index_ref.shape[0] // 2
    for sounding in range(count):
        place = sounding * PADDED
        for z in range(LZ):
            rows = block_ref[pl.ds(index_ref[sounding, z], TILE), :]
            padded[pl.ds(place, TILE), :] = rows
            place += index_ref[count + sounding, z]
    unpad(padded, out_ref, count)


def unpad(padded, out_ref, count):
    for sounding in range(count):
        begin, first = sounding * EARTH, sounding * PADDED
        out_ref[begin : begin + EARTH, :] = padded[first : first + EARTH, :]


def pad_end(rows_ref, padded):
    count = rows_ref.shape[0]
    padded[:count, :] = rows_ref[...]
    padded[count:, :] = jnp.zeros((TILE, LANES), jnp.float32)


def padded_rows(count):
    return pltpu.VMEM((count, LANES), jnp.float32)


def gather_earth(index, block):
    count = index.shape[0] // 2
    out = floats(count * EARTH, LANES)
    return call(
        earth_gather_body, out, [SMEM, VMEM], 0, 8 * out.size,
        scratch_shapes=[padded_rows(count * PADDED)],
    )(index, block)


def low_half():
    return lax.broadcasted_iota(jnp.int32, (SUB, LANES), 1) < LY


def pack(first, second, low):
    even = jnp.where(low, first, pltpu.roll(second, LY, 1))
    odd = jnp.where(low, pltpu.roll(first, LY, 1), second)
    return even, odd


def rows_of(ref, base, step):
    return ref[pl.ds(base, SUB, stride=step * PARTS), :]


def prepare_body(source_ref, observed_ref, source_out, observed_out):
    low = low_half()
    for ref, out in ((source_ref, source_out), (observed_ref, observed_out)):
        for part in range(3):
            for z in range(LZ):
                for j in range(PARTS):
                    base = part * LZ * TILE + z + LZ * j
                    first = rows_of(ref, base, LZ)
                    second = rows_of(ref, base + 3 * LZ * TILE, LZ)
                    out[part, z, 2 * j], out[part, z, 2 * j + 1] = pack(first, second, low)


def by_rows(values):
    count = values.shape[0]
    parts = values.reshape(count, 3, LZ, TILE, LANES)
    return parts.transpose(0, 1, 3, 2, 4).reshape(count * 3 * TILE * LZ, LANES)


def prepare(source, observed):
    out = floats(3, LZ, PACKED, SUB, LANES)
    return call(
        prepare_body, (out, out), [VMEM, VMEM], 8 * source.size, 16 * source.size
    )(by_rows(source), by_rows(observed))


def fields_body(
    packed, starts_ref, owners_ref, lengths_ref, table_ref, answer_ref, source_ref, observed_ref, kept_ref,
    given_ref, field, adjoint, right, curl, scale, decay, weight, sent_rows, given_rows,
):
    me = lax.axis_index("mdl")
    lane = lax.broadcasted_iota(jnp.int32, (SUB, LANES), 1)
    sub = lax.broadcasted_iota(jnp.int32, (SUB, LANES), 0)
    low = low_half()
    not_last = lane % LY != LY - 1
    not_first = lane % LY != 0
    top, bottom = sub != 0, sub != SUB - 1
    zero = jnp.zeros((SUB, LANES), jnp.float32)

    def y_next(value):
        return jnp.where(not_last, pltpu.roll(value, LANES - 1, 1), 0.0)

    def y_prev(value):
        return jnp.where(not_first, pltpu.roll(value, 1, 1), 0.0)

    def x_next(ref, part, z, k):
        if k + 1 < PACKED:
            return ref[part, z, k + 1]
        return jnp.where(bottom, pltpu.roll(ref[part, z, 0], SUB - 1, 0), 0.0)

    def sweep(state, start):
        above = None
        for z in range(LZ):
            curls = []
            for k in range(PACKED):
                east, north, vert = start[0, z, k], start[1, z, k], start[2, z, k]
                east_d = start[0, z + 1, k] if z + 1 < LZ else zero
                north_d = start[1, z + 1, k] if z + 1 < LZ else zero
                curls.append((
                    (y_next(vert) - vert) - (north_d - north),
                    (east_d - east) - (x_next(start, 2, z, k) - vert),
                    (x_next(start, 1, z, k) - north) - (y_next(east) - east),
                ))
            for k in range(PACKED):
                curl_x, curl_y, curl_z = curls[k]
                up_x, up_y = above[k][:2] if z else (zero, zero)
                if k:
                    before_y, before_z = curls[k - 1][1:]
                else:
                    before_y, before_z = (jnp.where(top, pltpu.roll(c, 1, 0), 0.0) for c in curls[-1][1:])
                back_x = (up_y - curl_y) - (y_prev(curl_z) - curl_z)
                back_y = (before_z - curl_z) - (up_x - curl_x)
                back_z = (y_prev(curl_x) - curl_x) - (before_y - curl_y)
                s, d = scale[z, k], decay[z, k]
                state[0, z, k] = d * start[0, z, k] + (right[0, z, k] - s * back_x)
                state[1, z, k] = d * start[1, z, k] + (right[1, z, k] - s * back_y)
                state[2, z, k] = d * start[2, z, k] + (right[2, z, k] - s * back_z)
            above = curls

    def relax(state, steps):
        sweep(state, right)

        @pl.loop(0, steps - 2)
        def _(step):
            sweep(state, state)

    count = starts_ref.shape[0]
    sent_at, given_at = [], []
    for sounding in range(count):
        place = 0
        for z in range(LZ):
            tile = sounding * LZ + z
            sent_at.append(sounding * EARTH + place if packed else tile * TILE)
            given_at.append(sounding * PADDED + place if packed else tile * TILE)
            place += lengths_ref[sounding, z]
    if packed:
        pad_end(answer_ref, sent_rows)
    sent_from = sent_rows if packed else answer_ref
    given_to = given_rows if packed else given_ref

    for z in range(LZ):

        def layer(sounding, j):
            raw = rows_of(table_ref, starts_ref[sounding, z] + j, 1)
            sent = rows_of(sent_from, sent_at[sounding * LZ + z] + j, 1)
            mine = jnp.full((SUB, LANES), owners_ref[sounding, z] == me)
            return jnp.where(mine, raw, sent)

        length = jnp.where(low, lengths_ref[0, z], lengths_ref[1, z])
        for j in range(PARTS):
            earth = PARTS * sub + j < length
            for odd, logs in enumerate(pack(layer(0, j), layer(1, j), low)):
                k = 2 * j + odd
                conduct = jnp.where(earth, jnp.exp(logs), AIR)
                s = OMEGA / (4.0 + conduct)
                scale[z, k] = s
                decay[z, k] = 1.0 - s * conduct
                weight[z, k] = jnp.where(earth, -conduct, 0.0)
                for part in range(3):
                    value = s * source_ref[part, z, k]
                    right[part, z, k] = value

    relax(field, STEPS_FWD)

    for z in range(LZ):
        for k in range(PACKED):
            for part in range(3):
                value = scale[z, k] * (field[part, z, k] - observed_ref[part, z, k])
                right[part, z, k] = value

    relax(adjoint, STEPS_ADJ)

    for z in range(LZ):

        def partial(k):
            total = field[0, z, k] * adjoint[0, z, k]
            total += field[1, z, k] * adjoint[1, z, k]
            total += field[2, z, k] * adjoint[2, z, k]
            return weight[z, k] * total

        for j in range(PARTS):
            first, second = pack(partial(2 * j), partial(2 * j + 1), low)
            for sounding, value in enumerate((first, second)):
                mine = jnp.full((SUB, LANES), owners_ref[sounding, z] == me)
                tile = sounding * LZ + z
                kept_ref[pl.ds(tile * TILE + j, SUB, stride=PARTS), :] = jnp.where(mine, value, 0.0)
                place = pl.ds(given_at[tile] + j, SUB, stride=PARTS)
                given_to[place, :] = jnp.where(mine, 0.0, value)
    if packed:
        unpad(given_rows, given_ref, count)


def soundings_partial(starts, owners, lengths, table, answer, source, observed):
    count, tiles = starts.shape[0], starts.size
    packed = answer.shape[0] == count * EARTH
    planes = pltpu.VMEM((3, LZ, PACKED, SUB, LANES), jnp.float32)
    single = pltpu.VMEM((LZ, PACKED, SUB, LANES), jnp.float32)
    cells = tiles * TILE * LANES
    kept, given = call(
        functools.partial(fields_body, packed),
        (floats(tiles * TILE, LANES), floats(*answer.shape)),
        [SMEM] * 3 + [VMEM] * 4, 500 * cells, 40 * cells,
        scratch_shapes=[planes] * 4 + [single] * 3
        + [padded_rows(count * EARTH + TILE), padded_rows(count * PADDED)],
    )(starts, owners, lengths, table, answer, source, observed)
    return kept.reshape(tiles, TILE, LANES), given


def arranged(order):
    if not order:
        return [0]
    rest = arranged(order[1:])
    return [slot | (1 << order[0]) for slot in rest] + rest


def add_terms(index_ref, terms_ref, total, share, slots, padded):
    me = lax.axis_index("grp")
    packed = len(terms_ref.shape) == 2
    span, wide = share + 2 * TILE, index_ref.shape[1]
    tiles = terms_ref.shape[0] // EARTH * LZ if packed else terms_ref.shape[0]
    row = lax.broadcasted_iota(jnp.int32, (TILE, LANES), 0)
    if packed:
        pad_end(terms_ref, padded)
    for tile in range(tiles):
        start = index_ref[tile // wide, tile % wide]
        first = lax.div(start, share)
        target = first + ((first ^ me) & 1)
        where = start - target * share
        base = ((target >> 1) ^ (me >> 1)) * span + TILE + where
        base = jnp.where(where > -TILE, base, slots * span)
        if packed:
            place = tile // LZ * EARTH if tile % LZ == 0 else place + length
            length = index_ref[tiles // LZ + tile // LZ, tile % LZ]
            terms = jnp.where(row < length, padded[pl.ds(place, TILE), :], 0.0)
        else:
            terms = terms_ref[tile]
        total[pl.ds(base, TILE), :] += terms


def first_body(groups, count, *refs):
    model_ref, total = refs[2 * count], refs[-1]
    me = lax.axis_index("grp")
    share = model_ref.shape[0] // groups
    total[...] = jnp.zeros_like(total)
    local = model_ref[pl.ds(pl.multiple_of(me * share, share), share), :]
    lane = lax.broadcasted_iota(jnp.int32, local.shape, 1)
    left = jnp.where(lane == 0, local, pltpu.roll(local, 1, 1))
    right = jnp.where(lane == LANES - 1, local, pltpu.roll(local, LANES - 1, 1))
    total[TILE : TILE + share, :] = BETA * (2.0 * local - left - right)
    for i in range(count):
        add_terms(*refs[2 * i : 2 * i + 2], total, share, groups // 2, None)


def first_sums(groups_of, block):
    groups = lax.axis_size("grp")
    share = block.shape[0] // groups
    out = floats(groups // 2 * (share + 2 * TILE) + TILE, LANES)
    flat = [a for pair in groups_of for a in pair]
    return call(
        functools.partial(first_body, groups, len(groups_of)), out,
        [SMEM, VMEM] * len(groups_of) + [VMEM], out.size, 8 * out.size,
    )(*flat, block)


def more_body(groups, share, index_ref, terms_ref, given_total, total, padded):
    add_terms(index_ref, terms_ref, total, share, groups // 2, padded)


def more_sums(index, terms, total, rows):
    groups = lax.axis_size("grp")
    return call(
        functools.partial(more_body, groups, rows // groups), floats(*total.shape),
        [SMEM, VMEM, VMEM], total.size, 8 * total.size, input_output_aliases={2: 0},
        scratch_shapes=[padded_rows(terms.shape[0] + TILE)],
    )(index, terms, total)


def piece_rows(share):
    return (share // 2, share // 4, share // 4)


def last_body(orders, groups, share, count, *refs):
    total, outs, padded = refs[2 * count + 1], refs[2 * count + 2 : -1], refs[-1]
    span, slots = share + 2 * TILE, groups // 2
    second = lax.axis_index("grp") & 1
    for i in range(count):
        add_terms(*refs[2 * i : 2 * i + 2], total, share, slots, padded)
    for which, order in enumerate((orders[0],) + orders):
        for place, slot in enumerate(arranged(order)):
            out = outs[2 * which + (place * 2 >= slots)]
            if which == 0:
                flip = (slot ^ (slot >> 1)) & 1
                slot = slot ^ (second * (3 * flip))
            begin = pl.multiple_of(slot * span + TILE + sum(piece_rows(share)[:which]), SUB)
            out[place % (slots // 2)] = total[pl.ds(begin, out.shape[1]), :]


def last_sums(groups_of, total, rows, orders):
    groups = lax.axis_size("grp")
    share, slots = rows // groups, groups // 2
    out = tuple(floats(slots // 2, r, LANES) for r in piece_rows(share) for _ in range(2))
    flat = [a for pair in groups_of for a in pair]
    count = len(groups_of)
    terms_rows = max(a.shape[0] for _, a in groups_of)
    outs = call(
        functools.partial(last_body, orders, groups, share, count),
        (floats(*total.shape),) + out, [SMEM, VMEM] * count + [VMEM],
        total.size, 8 * total.size, input_output_aliases={2 * count: 0},
        scratch_shapes=[padded_rows(terms_rows + TILE)],
    )(*flat, total)[1:]
    return outs[:2], outs[2:]


def join_body(got_low, low, got_high, high, give_ref, keep_ref):
    cut, split = low.shape[0] // 2, low.shape[1]
    for got, held, rows in ((got_low, low, slice(0, split)), (got_high, high, slice(split, None))):
        give_ref[:, rows] = got[:cut] + held[:cut]
        keep_ref[:, rows] = got[cut:] + held[cut:]


def finish_body(*refs):
    out_ref, begin = refs[-1], 0
    for i in range(0, len(refs) - 1, 2):
        got, held = refs[i : i + 2]
        rows = got.shape[1]
        out_ref[begin : begin + rows] = got[0] + held[0]
        begin += rows


def halve(whole, split, orders):
    groups = lax.axis_size("grp")
    give, keep = whole
    low_give, low, high_give, high = split
    for step, (low_bit, high_bit) in enumerate(zip(*orders)):
        if step < 2:
            got_low = swap_over("grp", 2 << low_bit)(low_give)
            got_high = swap_over("grp", 2 << high_bit)(high_give)
        else:
            got_both = swap_over("grp", 2 << low_bit)(both_give)
        ring = [(i, i ^ (2 << (high_bit if i & 1 else low_bit))) for i in range(groups)]
        got = lax.ppermute(give, "grp", ring)
        cut = keep.shape[0] // 2
        if step == 0:
            low_give, low = got_low[:cut] + low[:cut], got_low[cut:] + low[cut:]
            high_give, high = got_high[:cut] + high[:cut], got_high[cut:] + high[cut:]
        elif step == 1:
            out = floats(cut, low.shape[1] + high.shape[1], LANES)
            both_give, both = call(
                join_body, (out, out), [VMEM] * 4, low.size, 24 * low.size
            )(got_low, low, got_high, high)
        elif cut:
            both_give, both = got_both[:cut] + both[:cut], got_both[cut:] + both[cut:]
        if cut:
            give, keep = got[:cut] + keep[:cut], got[cut:] + keep[cut:]
    last = (got, keep, got_both, both)
    out = floats(keep.shape[1] + both.shape[1], LANES)
    return call(finish_body, out, [VMEM] * 4, out.size, 12 * out.size)(*last)


def hold_body(block_ref, out_ref, sem):
    copy = pltpu.make_async_copy(block_ref, out_ref, sem)
    copy.start()
    copy.wait()


def hold(block):
    return call(
        hold_body, floats(*block.shape), [pl.BlockSpec(memory_space=pltpu.HBM)], 0,
        8 * block.size, scratch_shapes=[pltpu.SemaphoreType.DMA],
    )(block)


def per_device(model, source, observed, owner_ids, offsets, lengths):
    rows, owners_count, groups = model.shape[0], lax.axis_size("mdl"), lax.axis_size("grp")
    tiles = source.shape[0] * LZ
    across, beside = swap_over("mdl", 1), swap_over("grp", 1)
    block = hold(model.reshape(rows, LANES))
    source, observed = prepare(source, observed)
    if owners_count == 2:
        asked = across(jnp.concatenate([offsets, lengths]))
        asked, block = lax.optimization_barrier((asked, block))
        given = gather_earth(asked, block)
        answer = across(given)
        told = beside(jnp.concatenate([offsets, asked]))
        answer, told = lax.optimization_barrier((answer, told))
        held = offsets.shape[0]
        kept, given = soundings_partial(
            offsets, owner_ids.reshape(offsets.shape), lengths, block, answer, source, observed
        )
        others = across(given)
        kept_beside = beside(kept)
        total = first_sums([(offsets, kept), (told[:held], kept_beside)], block)
        others_beside = beside(others)
        total = more_sums(asked, others, total, rows)
        final = [(told[held:], others_beside)]
    else:
        capacity = max(4, 2 * tiles // owners_count)
        places = place_slots(owner_ids.reshape(tiles), owners_count, capacity)
        swap = functools.partial(
            lax.all_to_all, axis_name="mdl", split_axis=0, concat_axis=0, tiled=True
        )
        request = jnp.zeros((owners_count * capacity,), jnp.int32).at[places].set(
            offsets.reshape(tiles)
        )
        asked = swap(request.reshape(owners_count, capacity))
        given = gather_rows(asked, block).reshape(owners_count, capacity, TILE, LANES)
        fetched = swap(given).reshape(owners_count * capacity * TILE, LANES)
        terms, _ = soundings_partial(
            (places * TILE).reshape(offsets.shape), jnp.full_like(offsets, lax.axis_index("mdl")),
            lengths, fetched, jnp.zeros((tiles * TILE, LANES), jnp.float32), source, observed,
        )
        outgoing = jnp.zeros((owners_count * capacity, TILE, LANES), jnp.float32)
        outgoing = outgoing.at[places].set(terms).reshape(owners_count, capacity, TILE, LANES)
        arrived = swap(outgoing).reshape(owners_count * capacity, TILE, LANES)
        total = first_sums([(asked, arrived)], block)
        final = [(beside(asked), beside(arrived))]

    bits = tuple(range(groups.bit_length() - 2))
    orders = (bits, bits[1:2] + bits[0:1] + bits[2:])
    sums = halve(*last_sums(final, total, rows, orders), orders)
    return sums[:, None, :]


def solution(mesh):
    placed = (
        P(None, "mdl", None),
        P(("grp", "mdl"), None, None, None),
        P(("grp", "mdl"), None, None, None),
        P(("grp", "mdl"), None, None),
        P(("grp", "mdl"), None),
        P(("grp", "mdl"), None),
    )

    return jax.shard_map(
        per_device, mesh=mesh, in_specs=placed, out_specs=P("grp", "mdl", None), check_vma=False
    )
```
